128 devices in a mesh: seq: 32 (over x, y, core), tp: 4 (over z).
Axes of the slice: x: 4, y: 4, z: 4, core: 2. Of those that a mesh axis runs over, the one named last changes fastest.
Arguments:
- inputs: float32 [8192, 1024], P('seq', 'tp'), may hold values from -6 to 6
- cotangent: float32 [8192, 1024], P('seq', 'tp'), may hold values from -6 to 6
- entry_weight: float32 [2, 3, 1024, 1024], P(None, None, 'seq', 'tp'), may hold values from -0.1875 to 0.1875
- exit_weight: float32 [2, 1024, 1024], P(None, 'tp', 'seq'), may hold values from -0.1875 to 0.1875
- gate_up: float32 [2, 2, 1024, 4608], P(None, None, 'seq', 'tp'), may hold values from -0.1875 to 0.1875
- down_weight: float32 [2, 4608, 1024], P(None, 'tp', 'seq'), may hold values from -0.1875 to 0.1875
- conv_kernel: float32 [2, 3, 1024], P(None, None, 'tp'), may hold values from -3 to 3
- norm_gain: float32 [2, 2, 1024], P(None, None, 'tp'), may hold values from 0.5 to 1.5
- entry_first: float32 [2, 3, 1024, 1024], P(None, None, 'seq', 'tp'), may hold values from -27.1529 to 27.1529
- entry_second: float32 [2, 3, 1024, 1024], P(None, None, 'seq', 'tp'), may hold values from 0.8192 to 16.384
- exit_first: float32 [2, 1024, 1024], P(None, 'tp', 'seq'), may hold values from -27.1529 to 27.1529
- exit_second: float32 [2, 1024, 1024], P(None, 'tp', 'seq'), may hold values from 0.8192 to 16.384
- gate_first: float32 [2, 2, 1024, 4608], P(None, None, 'seq', 'tp'), may hold values from -27.1529 to 27.1529
- gate_second: float32 [2, 2, 1024, 4608], P(None, None, 'seq', 'tp'), may hold values from 0.8192 to 16.384
- down_first: float32 [2, 4608, 1024], P(None, 'tp', 'seq'), may hold values from -27.1529 to 27.1529
- down_second: float32 [2, 4608, 1024], P(None, 'tp', 'seq'), may hold values from 0.8192 to 16.384
- kernel_first: float32 [2, 3, 1024], P(None, None, 'tp'), may hold values from -27.1529 to 27.1529
- kernel_second: float32 [2, 3, 1024], P(None, None, 'tp'), may hold values from 0.8192 to 16.384
- gain_first: float32 [2, 2, 1024], P(None, None, 'tp'), may hold values from -27.1529 to 27.1529
- gain_second: float32 [2, 2, 1024], P(None, None, 'tp'), may hold values from 0.8192 to 16.384
Outputs:
- output: float32 [8192, 1024], P('seq', 'tp')
- input_grad: float32 [8192, 1024], P('seq', 'tp')
- entry_grad: float32 [2, 3, 1024, 1024], P(None, None, 'seq', 'tp')
- exit_grad: float32 [2, 1024, 1024], P(None, 'tp', 'seq')
- gate_grad: float32 [2, 2, 1024, 4608], P(None, None, 'seq', 'tp')
- down_grad: float32 [2, 4608, 1024], P(None, 'tp', 'seq')
- kernel_grad: float32 [2, 3, 1024], P(None, None, 'tp')
- gain_grad: float32 [2, 2, 1024], P(None, None, 'tp')
- entry_updated: float32 [2, 3, 1024, 1024], P(None, None, 'seq', 'tp')
- exit_updated: float32 [2, 1024, 1024], P(None, 'tp', 'seq')
- gate_updated: float32 [2, 2, 1024, 4608], P(None, None, 'seq', 'tp')
- down_updated: float32 [2, 4608, 1024], P(None, 'tp', 'seq')
- kernel_updated: float32 [2, 3, 1024], P(None, None, 'tp')
- gain_updated: float32 [2, 2, 1024], P(None, None, 'tp')
- entry_first_new: float32 [2, 3, 1024, 1024], P(None, None, 'seq', 'tp')
- entry_second_new: float32 [2, 3, 1024, 1024], P(None, None, 'seq', 'tp')
- exit_first_new: float32 [2, 1024, 1024], P(None, 'tp', 'seq')
- exit_second_new: float32 [2, 1024, 1024], P(None, 'tp', 'seq')
- gate_first_new: float32 [2, 2, 1024, 4608], P(None, None, 'seq', 'tp')
- gate_second_new: float32 [2, 2, 1024, 4608], P(None, None, 'seq', 'tp')
- down_first_new: float32 [2, 4608, 1024], P(None, 'tp', 'seq')
- down_second_new: float32 [2, 4608, 1024], P(None, 'tp', 'seq')
- kernel_first_new: float32 [2, 3, 1024], P(None, None, 'tp')
- kernel_second_new: float32 [2, 3, 1024], P(None, None, 'tp')
- gain_first_new: float32 [2, 2, 1024], P(None, None, 'tp')
- gain_second_new: float32 [2, 2, 1024], P(None, None, 'tp')
The draws below stay inside these ranges and needn't reach their ends.
All inputs are finite; a program needn't handle non-finite values.
Results may differ from the reference program's by a relative error of at most 0.019.
The reference program's roundings to bfloat16 on the way count: a program that leaves them out, or rounds other values in their place, can miss the bound.
Values may be sent and summed in bfloat16 or wider, within the bound.
A program may use at most 192 MiB of HBM per device.

```python
import math
import jax
import jax.numpy as jnp
from jax import lax

D = 1024
FF = 4608
KW = 3
LAYERS = 2
STEP = 4
TOKENS = 8192


def shard_levels(key, shape, cuts, smallest, high):
    factor_of, own = 1.0, jax.random.fold_in(key, 6)
    for position, shards_of in cuts:
        steps = jnp.exp(jax.random.uniform(jax.random.fold_in(own, position), (shards_of,), jnp.float32, smallest / len(cuts), high / len(cuts)))
        factor_of = factor_of * jnp.repeat(steps, shape[position] // shards_of).reshape([-1 if axis == position else 1 for axis in range(len(shape))])
    return factor_of


def normal_values(stream_key, shape, scale, reach, shards=(), kind=jnp.bfloat16):
    values = scale * jax.random.normal(stream_key, shape, jnp.float32)
    if shards:
        values = values * shard_levels(stream_key, shape, shards, -0.22, 0.18)
    return jnp.clip(values, -reach, reach).astype(kind)


def setup_inputs(seed: int = 0) -> dict:
    splits = jax.random.split(jax.random.key(seed), 21)
    inputs = normal_values(splits[0], (TOKENS, D), 1.0, 6.0, ((0, 32), (1, 4)), jnp.float32)
    cotangent = normal_values(splits[1], (TOKENS, D), 1.0, 6.0, ((0, 32), (1, 4)), jnp.float32)
    entry_weight = normal_values(splits[2], (LAYERS, 3, D, D), D ** -0.5, 0.1875, ((2, 32), (3, 4)), jnp.float32)
    exit_weight = normal_values(splits[3], (LAYERS, D, D), D ** -0.5, 0.1875, ((1, 4), (2, 32)), jnp.float32)
    gate_up = normal_values(splits[4], (LAYERS, 2, D, FF), D ** -0.5, 0.1875, ((2, 32), (3, 4)), jnp.float32)
    down_weight = normal_values(splits[5], (LAYERS, FF, D), (FF // 4) ** -0.5, 0.1875, ((1, 4), (2, 32)), jnp.float32)
    conv_kernel = normal_values(splits[6], (LAYERS, KW, D), 0.5, 3.0, ((2, 4),), jnp.float32)
    norm_gain = jnp.clip(1.0 + 0.1 * jax.random.normal(splits[7], (LAYERS, 2, D), jnp.float32), 0.5, 1.5)
    entry_first = normal_values(splits[8], (LAYERS, 3, D, D), (0.1 * TOKENS ** 0.5), 27.1529, ((2, 32), (3, 4)), jnp.float32)
    entry_second = jnp.clip(jnp.exp(math.log(16.384) - 2.9957323 * jax.random.uniform(splits[9], (LAYERS, 3, D, D), jnp.float32) ** shard_levels(splits[9], (LAYERS, 3, D, D), ((2, 32), (3, 4)), -0.2, 0.2)), 0.8192, 16.384)
    exit_first = normal_values(splits[10], (LAYERS, D, D), (0.1 * TOKENS ** 0.5), 27.1529, ((1, 4), (2, 32)), jnp.float32)
    exit_second = jnp.clip(jnp.exp(math.log(16.384) - 2.9957323 * jax.random.uniform(splits[11], (LAYERS, D, D), jnp.float32) ** shard_levels(splits[11], (LAYERS, D, D), ((1, 4), (2, 32)), -0.2, 0.2)), 0.8192, 16.384)
    gate_first = normal_values(splits[12], (LAYERS, 2, D, FF), (0.1 * TOKENS ** 0.5), 27.1529, ((2, 32), (3, 4)), jnp.float32)
    gate_second = jnp.clip(jnp.exp(math.log(16.384) - 2.9957323 * jax.random.uniform(splits[13], (LAYERS, 2, D, FF), jnp.float32) ** shard_levels(splits[13], (LAYERS, 2, D, FF), ((2, 32), (3, 4)), -0.2, 0.2)), 0.8192, 16.384)
    down_first = normal_values(splits[14], (LAYERS, FF, D), (0.1 * TOKENS ** 0.5), 27.1529, ((1, 4), (2, 32)), jnp.float32)
    down_second = jnp.clip(jnp.exp(math.log(16.384) - 2.9957323 * jax.random.uniform(splits[15], (LAYERS, FF, D), jnp.float32) ** shard_levels(splits[15], (LAYERS, FF, D), ((1, 4), (2, 32)), -0.2, 0.2)), 0.8192, 16.384)
    kernel_first = normal_values(splits[16], (LAYERS, KW, D), (0.1 * TOKENS ** 0.5), 27.1529, ((2, 4),), jnp.float32)
    kernel_second = jnp.clip(jnp.exp(math.log(16.384) - 2.9957323 * jax.random.uniform(splits[17], (LAYERS, KW, D), jnp.float32) ** shard_levels(splits[17], (LAYERS, KW, D), ((2, 4),), -0.2, 0.2)), 0.8192, 16.384)
    gain_first = normal_values(splits[18], (LAYERS, 2, D), (0.1 * TOKENS ** 0.5), 27.1529, ((2, 4),), jnp.float32)
    gain_second = jnp.clip(jnp.exp(math.log(16.384) - 2.9957323 * jax.random.uniform(splits[19], (LAYERS, 2, D), jnp.float32) ** shard_levels(splits[19], (LAYERS, 2, D), ((2, 4),), -0.2, 0.2)), 0.8192, 16.384)
    return dict(inputs=inputs, cotangent=cotangent, entry_weight=entry_weight, exit_weight=exit_weight, gate_up=gate_up, down_weight=down_weight, conv_kernel=conv_kernel, norm_gain=norm_gain, entry_first=entry_first, entry_second=entry_second, exit_first=exit_first, exit_second=exit_second, gate_first=gate_first, gate_second=gate_second, down_first=down_first, down_second=down_second, kernel_first=kernel_first, kernel_second=kernel_second, gain_first=gain_first, gain_second=gain_second)


EPS = 1e-06

def row_norm(value):
    scale = lax.rsqrt(lax.optimization_barrier(jnp.mean(value * value, axis=1, keepdims=True)) + EPS)
    return (value * scale, scale)

def norm_back(dnorm, normed, scale, gain):
    dnormed = dnorm * gain
    inner = lax.optimization_barrier(jnp.mean(dnormed * normed, axis=1, keepdims=True))
    return (scale * (dnormed - normed * inner), lax.optimization_barrier(jnp.sum(dnorm * normed, axis=0)))

def bdot(left, right):
    return jnp.dot(left, right, preferred_element_type=jnp.float32)

def adamw(weight, grad, first, second, rate, decay):
    first_new = 0.9 * first + 0.1 * grad
    second_new = 0.999 * second + 0.001 * grad * grad
    update = first_new / (1.0 - 0.9 ** STEP) / (jnp.sqrt(second_new / (1.0 - 0.999 ** STEP)) + 1e-08)
    return (weight - rate * (update + decay * weight), first_new, second_new)

def reference(inputs, cotangent, entry_weight, exit_weight, gate_up, down_weight, conv_kernel, norm_gain, entry_first, entry_second, exit_first, exit_second, gate_first, gate_second, down_first, down_second, kernel_first, kernel_second, gain_first, gain_second):
    entry_b = entry_weight.astype(jnp.bfloat16)
    exit_b = exit_weight.astype(jnp.bfloat16)
    gate_b = gate_up.astype(jnp.bfloat16)
    down_b = down_weight.astype(jnp.bfloat16)
    width = inputs.shape[1]
    hidden = inputs
    saved = []
    for layer in range(LAYERS):
        kern = conv_kernel[layer]
        gain = norm_gain[layer]
        normed1, scale1 = row_norm(hidden)
        first_in = (normed1 * gain[0]).astype(jnp.bfloat16)
        b_part = bdot(first_in, entry_b[layer, 0])
        c_part = bdot(first_in, entry_b[layer, 1])
        x_part = bdot(first_in, entry_b[layer, 2])
        product = b_part * x_part
        extended = jnp.concatenate([jnp.zeros((2, width), jnp.float32), product], axis=0)
        conv_out = kern[0] * extended[:-2] + kern[1] * extended[1:-1] + kern[2] * extended[2:]
        gated = (c_part * conv_out).astype(jnp.bfloat16)
        mid = hidden + bdot(gated, exit_b[layer])
        normed2, scale2 = row_norm(mid)
        second_in = (normed2 * gain[1]).astype(jnp.bfloat16)
        gate_val = bdot(second_in, gate_b[layer, 0])
        up_val = bdot(second_in, gate_b[layer, 1])
        sig = jax.nn.sigmoid(gate_val)
        swish = gate_val * sig
        acted = (swish * up_val).astype(jnp.bfloat16)
        saved.append((hidden, normed1, scale1, first_in, b_part, c_part, x_part, extended, conv_out, gated, normed2, scale2, second_in, gate_val, up_val, sig, swish, acted))
        hidden = mid + bdot(acted, down_b[layer])
    output = hidden
    grad = cotangent
    entry_g = [None] * LAYERS
    exit_g = [None] * LAYERS
    gate_g = [None] * LAYERS
    down_g = [None] * LAYERS
    kernel_g = [None] * LAYERS
    gain_g = [None] * LAYERS
    for layer in reversed(range(LAYERS)):
        hidden, normed1, scale1, first_in, b_part, c_part, x_part, extended, conv_out, gated, normed2, scale2, second_in, gate_val, up_val, sig, swish, acted = saved[layer]
        kern = conv_kernel[layer]
        gain = norm_gain[layer]
        grad_b = grad.astype(jnp.bfloat16)
        dacted = bdot(grad_b, down_b[layer].T)
        down_g[layer] = bdot(acted.T, grad_b)
        dgate = (dacted * up_val * sig * (1.0 + gate_val * (1.0 - sig))).astype(jnp.bfloat16)
        dup = (dacted * swish).astype(jnp.bfloat16)
        gate_g[layer] = jnp.stack([bdot(second_in.T, dgate), bdot(second_in.T, dup)])
        dnorm2 = bdot(dgate, gate_b[layer, 0].T) + bdot(dup, gate_b[layer, 1].T)
        back2, dgain2 = norm_back(dnorm2, normed2, scale2, gain[1])
        dmid = grad + back2
        dmid_b = dmid.astype(jnp.bfloat16)
        dgated = bdot(dmid_b, exit_b[layer].T)
        exit_g[layer] = bdot(gated.T, dmid_b)
        dc_part = dgated * conv_out
        dconv = dgated * c_part
        kernel_g[layer] = jnp.stack([lax.optimization_barrier(jnp.sum(dconv * extended[:-2], axis=0)), lax.optimization_barrier(jnp.sum(dconv * extended[1:-1], axis=0)), lax.optimization_barrier(jnp.sum(dconv * extended[2:], axis=0))])
        zero_one = jnp.zeros((1, width), jnp.float32)
        zero_two = jnp.zeros((2, width), jnp.float32)
        dextended = jnp.concatenate([kern[0] * dconv, zero_two], axis=0) + jnp.concatenate([zero_one, kern[1] * dconv, zero_one], axis=0) + jnp.concatenate([zero_two, kern[2] * dconv], axis=0)
        dproduct = dextended[2:]
        dproj = jnp.stack([dproduct * x_part, dc_part, dproduct * b_part]).astype(jnp.bfloat16)
        entry_g[layer] = jnp.stack([bdot(first_in.T, dproj[c]) for c in range(3)])
        dnorm1 = bdot(dproj[0], entry_b[layer, 0].T) + bdot(dproj[1], entry_b[layer, 1].T) + bdot(dproj[2], entry_b[layer, 2].T)
        back1, dgain1 = norm_back(dnorm1, normed1, scale1, gain[0])
        gain_g[layer] = jnp.stack([dgain1, dgain2])
        grad = dmid + back1
    entry_grad = jnp.stack(entry_g)
    exit_grad = jnp.stack(exit_g)
    gate_grad = jnp.stack(gate_g)
    down_grad = jnp.stack(down_g)
    kernel_grad = jnp.stack(kernel_g)
    gain_grad = jnp.stack(gain_g)
    entry_u, entry_f, entry_s = adamw(entry_weight, entry_grad, entry_first, entry_second, 0.01, 0.1)
    exit_u, exit_f, exit_s = adamw(exit_weight, exit_grad, exit_first, exit_second, 0.01, 0.1)
    gate_u, gate_f, gate_s = adamw(gate_up, gate_grad, gate_first, gate_second, 0.01, 0.1)
    down_u, down_f, down_s = adamw(down_weight, down_grad, down_first, down_second, 0.01, 0.1)
    kernel_u, kernel_f, kernel_s = adamw(conv_kernel, kernel_grad, kernel_first, kernel_second, 0.2, 0.0)
    gain_u, gain_f, gain_s = adamw(norm_gain, gain_grad, gain_first, gain_second, 0.2, 0.0)
    return (output, grad, entry_grad, exit_grad, gate_grad, down_grad, kernel_grad, gain_grad, entry_u, exit_u, gate_u, down_u, kernel_u, gain_u, entry_f, entry_s, exit_f, exit_s, gate_f, gate_s, down_f, down_s, kernel_f, kernel_s, gain_f, gain_s)
```

```python
import functools

import jax
import jax.numpy as jnp
from jax import lax
from jax.experimental import pallas as pl
from jax.experimental.pallas import tpu as pltpu
from jax.sharding import PartitionSpec as P

STEP = 4
EPS = 1e-06
MESH = pl.DeviceIdType.MESH
BF = jnp.bfloat16
F32 = jnp.float32
SPAN = 384


def nn(a, b):
    return lax.dot_general(a, b, (((1,), (0,)), ((), ())), preferred_element_type=F32)


def nt(a, b):
    return lax.dot_general(a, b, (((1,), (1,)), ((), ())), preferred_element_type=F32)


def as_column(row):
    return jnp.broadcast_to(row, (128, row.shape[1])).T[:, 0:1]


def step_kernel(
    cfg,
    x_ref,
    cot_ref,
    w_ref,
    kern_ref,
    gain_ref,
    out_ref,
    din_ref,
    gw_ref,
    small_ref,
    rows,
    part,
    stage,
    landed,
    stats,
    normed,
    scales,
    ext,
    dext,
    bcx,
    conv,
    gated,
    gates,
    ups,
    acted,
    dgs,
    dus,
    dproj,
    turned,
    ag_send,
    ag_recv,
    rs_send,
    rs_recv,
    st_send,
    st_recv,
    halo_send,
    halo_recv,
):
    layers, seqs, tokens, ch, ff = cfg
    half = tokens // 2
    width = 4 * ch
    per = 4 * ch + 3 * ff
    z = lax.axis_index("tp")
    s = lax.axis_index("seq")
    zr, zl, zo = lax.rem(z + 1, 4), lax.rem(z + 3, 4), lax.rem(z + 2, 4)
    after, before = lax.rem(s + 1, seqs), lax.rem(s + seqs - 1, seqs)

    barrier = pltpu.get_barrier_semaphore()
    for where in ((s, zr), (s, zl), (s, zo), (after, z), (before, z)):
        pl.semaphore_signal(barrier, inc=1, device_id=where, device_id_type=MESH)
    pl.semaphore_wait(barrier, 5)

    pending = []

    def send(src, dst, ssem, rsem, where):
        copy = pltpu.make_async_remote_copy(
            src_ref=src, dst_ref=dst, send_sem=ssem, recv_sem=rsem, device_id=where, device_id_type=MESH
        )
        copy.start()
        pending.append(copy)
        return copy

    def cols(who):
        return pl.ds(pl.multiple_of(who * ch, ch), ch)

    def own_rows(who):
        return pl.ds(pl.multiple_of(who * ch, ch), ch)

    top, low = pl.ds(0, half), pl.ds(half, half)

    class Gather:
        def __init__(self, i, block):
            self.i = i
            rows[i, :, cols(z)] = block
            mine = lambda r: rows.at[i, r, cols(z)]
            self.r1 = send(mine(top), mine(top), ag_send.at[i, 0], ag_recv.at[i, 0], (s, zr))
            self.l1 = send(mine(low), mine(low), ag_send.at[i, 1], ag_recv.at[i, 1], (s, zl))
            self.r2 = send(mine(low), mine(low), ag_send.at[i, 2], ag_recv.at[i, 2], (s, zr))
            self.l2 = send(mine(top), mine(top), ag_send.at[i, 3], ag_recv.at[i, 3], (s, zl))

        def pass_on(self):
            i = self.i
            self.r1.wait_recv()
            b = rows.at[i, top, cols(zl)]
            self.rf = send(b, b, ag_send.at[i, 4], ag_recv.at[i, 4], (s, zr))
            self.l1.wait_recv()
            b = rows.at[i, low, cols(zr)]
            self.lf = send(b, b, ag_send.at[i, 5], ag_recv.at[i, 5], (s, zl))

        def finish(self):
            for c in (self.r2, self.l2, self.rf, self.lf):
                c.wait_recv()

    class Scatter:
        def __init__(self, i, piece):
            self.i = i
            at = lambda k, r: stage.at[i, k, r]
            to = lambda k: landed.at[i, k]
            stage[i, 0] = piece(zo).astype(BF)
            self.r1 = send(at(0, top), to(0), rs_send.at[i, 0], rs_recv.at[i, 0], (s, zr))
            self.l1 = send(at(0, low), to(1), rs_send.at[i, 1], rs_recv.at[i, 1], (s, zl))
            right = piece(zr)
            stage[i, 1, half:] = right[half:].astype(BF)
            self.r2 = send(at(1, low), to(2), rs_send.at[i, 2], rs_recv.at[i, 2], (s, zr))
            part[0] = right[:half]
            left = piece(zl)
            stage[i, 2, :half] = left[:half].astype(BF)
            self.l2 = send(at(2, top), to(3), rs_send.at[i, 3], rs_recv.at[i, 3], (s, zl))
            part[1] = left[half:]
            own = piece(z)
            part[2] = own[:half]
            part[3] = own[half:]

        def pass_on(self):
            i = self.i
            self.r1.wait_recv()
            stage[i, 1, :half] = (part[0] + landed[i, 0].astype(F32)).astype(BF)
            self.rf = send(stage.at[i, 1, top], landed.at[i, 4], rs_send.at[i, 4], rs_recv.at[i, 4], (s, zr))
            self.l1.wait_recv()
            stage[i, 2, half:] = (part[1] + landed[i, 1].astype(F32)).astype(BF)
            self.lf = send(stage.at[i, 2, low], landed.at[i, 5], rs_send.at[i, 5], rs_recv.at[i, 5], (s, zl))

        def finish(self):
            i = self.i
            for c in (self.r2, self.l2, self.rf, self.lf):
                c.wait_recv()
            upper = part[2] + landed[i, 4].astype(F32) + landed[i, 3].astype(F32)
            lower = part[3] + landed[i, 2].astype(F32) + landed[i, 5].astype(F32)
            return jnp.concatenate([upper, lower], axis=0)

    def row_total(i, value):
        sums = jnp.sum(value, axis=1, keepdims=True)
        stats[i, z] = jnp.broadcast_to(sums, (tokens, 128)).T[0:8]
        there = stats.at[i, z]
        got = [
            send(there, there, st_send.at[i, k], st_recv.at[i, k], (s, who))
            for k, who in enumerate((zr, zl, zo))
        ]
        for c in got:
            c.wait_recv()
        total = stats[i, 0] + stats[i, 1] + stats[i, 2] + stats[i, 3]
        return as_column(total[0:1])

    def columns(at, j, size=SPAN):
        return pl.ds(pl.multiple_of(at + j * size, 128), size)

    def weight_grad(left_index, spans):
        turned[...] = rows[left_index].T
        for right_ref, lead, width_r, at in spans:
            size = SPAN if width_r % SPAN == 0 else width_r

            @pl.loop(0, width_r // size)
            def _(j, right_ref=right_ref, lead=lead, at=at, size=size):
                right = right_ref[lead, :, columns(0, j, size)]
                gw_ref[:, columns(at, j, size)] = nn(turned[...], right).astype(BF)

    def norm_forward(k, h, gain):
        total = row_total(k, h * h)
        scale = lax.rsqrt(total / width + EPS)
        scales[k] = jnp.broadcast_to(scale, (tokens, 128))
        a = h * scale
        normed[k] = a
        return (a * gain).astype(BF)

    def norm_backward(k, dn, gain, small_row):
        a = normed[k]
        t = dn * gain
        small_ref[pl.ds(small_row, 1), :] = jnp.sum(dn * a, axis=0, keepdims=True)
        inner = row_total(2 * layers + k, t * a)
        return scales[k][:, 0:1] * (t - a * (inner / width))

    small_ref[...] = jnp.zeros_like(small_ref)
    hidden = x_ref[...]
    cot_gather = None
    for l in range(layers):
        base = l * per
        at_exit, at_gate, at_up, at_down = base + 3 * ch, base + 4 * ch, base + 4 * ch + ff, base + 4 * ch + 2 * ff
        n1 = norm_forward(2 * l, hidden, gain_ref[l, 0:1])
        gather = Gather(2 * l, n1)
        if l == 0:
            cot_gather = Gather(2 * layers + 2 * (layers - 1), cot_ref[...].astype(BF))
        gather.pass_on()
        gather.finish()
        if l == 0:
            cot_gather.pass_on()
        full = rows[2 * l]
        bm = nn(full, w_ref[:, columns(base, 0, ch)])
        xm = nn(full, w_ref[:, columns(base, 2, ch)])
        bx = bm * xm
        ext[l, 8:] = bx
        tail = send(
            ext.at[l, pl.ds(tokens, 8)], ext.at[l, pl.ds(0, 8)], halo_send.at[l], halo_recv.at[l], (after, z)
        )
        bcx[l, 0] = bm
        bcx[l, 2] = xm
        cm = nn(full, w_ref[:, columns(base, 1, ch)])
        bcx[l, 1] = cm
        tail.wait_recv()
        head = ext[l, 0:8]
        ext[l, 0:8] = jnp.where(s > 0, head, jnp.zeros_like(head))
        k = kern_ref[l]
        zc = k[0:1] * ext[l, 6 : 6 + tokens] + k[1:2] * ext[l, 7 : 7 + tokens] + k[2:3] * ext[l, 8 : 8 + tokens]
        conv[l] = zc
        gated[l] = (cm * zc).astype(BF)

        def exit_piece(who, l=l, at=at_exit):
            return nt(gated[l], w_ref[own_rows(who), columns(at, 0, ch)])

        scatter = Scatter(2 * l, exit_piece)
        scatter.pass_on()
        mid = hidden + scatter.finish()
        n2 = norm_forward(2 * l + 1, mid, gain_ref[l, 1:2])
        gather = Gather(2 * l + 1, n2)
        gather.pass_on()
        gather.finish()

        @pl.loop(0, ff // SPAN)
        def _(j, l=l, at_gate=at_gate, at_up=at_up):
            full = rows[2 * l + 1]
            g = nn(full, w_ref[:, columns(at_gate, j)])
            u = nn(full, w_ref[:, columns(at_up, j)])
            gates[l, :, columns(0, j)] = g
            ups[l, :, columns(0, j)] = u
            acted[l, :, columns(0, j)] = (g * jax.nn.sigmoid(g) * u).astype(BF)

        def down_piece(who, l=l, at=at_down):
            return nt(acted[l], w_ref[own_rows(who), columns(at, 0, ff)])

        scatter = Scatter(2 * l + 1, down_piece)
        scatter.pass_on()
        hidden = mid + scatter.finish()
    out_ref[...] = hidden

    grad = cot_ref[...]
    for l in reversed(range(layers)):
        base = l * per
        at_exit, at_gate, at_up, at_down = base + 3 * ch, base + 4 * ch, base + 4 * ch + ff, base + 4 * ch + 2 * ff
        ie = 2 * layers + 2 * l
        if l == layers - 1:
            gather = cot_gather
        else:
            gather = Gather(ie, grad.astype(BF))
            gather.pass_on()
        gather.finish()

        @pl.loop(0, ff // SPAN)
        def _(j, l=l, ie=ie, at_down=at_down):
            ds = nn(rows[ie], w_ref[:, columns(at_down, j)])
            g = gates[l, :, columns(0, j)]
            u = ups[l, :, columns(0, j)]
            sig = jax.nn.sigmoid(g)
            dgs[0, :, columns(0, j)] = (ds * u * sig * (1.0 + g * (1.0 - sig))).astype(BF)
            dus[0, :, columns(0, j)] = (ds * (g * sig)).astype(BF)

        def norm2_piece(who, at_gate=at_gate, at_up=at_up):
            return nt(dgs[0], w_ref[own_rows(who), columns(at_gate, 0, ff)]) + nt(
                dus[0], w_ref[own_rows(who), columns(at_up, 0, ff)]
            )

        scatter = Scatter(2 * layers + 2 * l, norm2_piece)
        weight_grad(ie, [(acted, l, ff, at_down)])
        scatter.pass_on()
        weight_grad(2 * l + 1, [(dgs, 0, ff, at_gate), (dus, 0, ff, at_up)])
        dn2 = scatter.finish()
        dmid = grad + norm_backward(2 * l + 1, dn2, gain_ref[l, 1:2], 3 * layers + 2 * l + 1)
        gather = Gather(ie + 1, dmid.astype(BF))
        gather.pass_on()
        gather.finish()
        dy = nn(rows[ie + 1], w_ref[:, columns(at_exit, 0, ch)])
        dz = dy * bcx[l, 1]
        dext[l, :tokens] = dz
        tail = send(
            dext.at[l, pl.ds(0, 8)],
            dext.at[l, pl.ds(tokens, 8)],
            halo_send.at[layers + l],
            halo_recv.at[layers + l],
            (before, z),
        )
        dproj[0, :, ch : 2 * ch] = (dy * conv[l]).astype(BF)
        for j in range(3):
            small_ref[pl.ds(3 * l + j, 1), :] = jnp.sum(dz * ext[l, 6 + j : 6 + j + tokens], axis=0, keepdims=True)
        weight_grad(ie + 1, [(gated, l, ch, at_exit)])
        tail.wait_recv()
        last = dext[l, tokens:]
        dext[l, tokens:] = jnp.where(s < seqs - 1, last, jnp.zeros_like(last))
        k = kern_ref[l]
        dbx = k[2:3] * dext[l, 0:tokens] + k[1:2] * dext[l, 1 : 1 + tokens] + k[0:1] * dext[l, 2 : 2 + tokens]
        dproj[0, :, :ch] = (dbx * bcx[l, 2]).astype(BF)
        dproj[0, :, 2 * ch :] = (dbx * bcx[l, 0]).astype(BF)

        def norm1_piece(who, base=base):
            return nt(dproj[0], w_ref[own_rows(who), columns(base, 0, 3 * ch)])

        scatter = Scatter(2 * layers + 2 * l + 1, norm1_piece)
        scatter.pass_on()
        weight_grad(2 * l, [(dproj, 0, 3 * ch, base)])
        dn1 = scatter.finish()
        grad = dmid + norm_backward(2 * l, dn1, gain_ref[l, 0:1], 3 * layers + 2 * l)
    din_ref[...] = grad
    for copy in pending:
        copy.wait_send()


def run_step(x, cot, w, kern, gain, seqs):
    layers, taps, ch = kern.shape
    tokens = x.shape[0]
    width = w.shape[0]
    per = w.shape[1] // layers
    ff = (per - 4 * ch) // 3
    n = 4 * layers
    vmem = pl.BlockSpec(memory_space=pltpu.VMEM)
    dma = pltpu.SemaphoreType.DMA
    return pl.pallas_call(
        functools.partial(step_kernel, (layers, seqs, tokens, ch, ff)),
        out_shape=(
            jax.ShapeDtypeStruct((tokens, ch), F32),
            jax.ShapeDtypeStruct((tokens, ch), F32),
            jax.ShapeDtypeStruct(w.shape, BF),
            jax.ShapeDtypeStruct((16, ch), F32),
        ),
        in_specs=[vmem] * 5,
        out_specs=(vmem,) * 4,
        scratch_shapes=[
            pltpu.VMEM((n, tokens, width), BF),
            pltpu.VMEM((4, tokens // 2, ch), F32),
            pltpu.VMEM((n, 3, tokens, ch), BF),
            pltpu.VMEM((n, 6, tokens // 2, ch), BF),
            pltpu.VMEM((n, 4, 8, tokens), F32),
            pltpu.VMEM((2 * layers, tokens, ch), F32),
            pltpu.VMEM((2 * layers, tokens, 128), F32),
            pltpu.VMEM((layers, tokens + 8, ch), F32),
            pltpu.VMEM((layers, tokens + 8, ch), F32),
            pltpu.VMEM((layers, 3, tokens, ch), F32),
            pltpu.VMEM((layers, tokens, ch), F32),
            pltpu.VMEM((layers, tokens, ch), BF),
            pltpu.VMEM((layers, tokens, ff), F32),
            pltpu.VMEM((layers, tokens, ff), F32),
            pltpu.VMEM((layers, tokens, ff), BF),
            pltpu.VMEM((1, tokens, ff), BF),
            pltpu.VMEM((1, tokens, ff), BF),
            pltpu.VMEM((1, tokens, 3 * ch), BF),
            pltpu.VMEM((width, tokens), BF),
            dma((n, 6)),
            dma((n, 6)),
            dma((n, 6)),
            dma((n, 6)),
            dma((n, 3)),
            dma((n, 3)),
            dma((2 * layers,)),
            dma((2 * layers,)),
        ],
        compiler_params=pltpu.CompilerParams(
            collective_id=0, has_side_effects=True, vmem_limit_bytes=62 * 1024 * 1024
        ),
        name="layers",
    )(x, cot, w, kern, gain)


def adamw(weight, grad, first, second, rate, decay):
    first_new = 0.9 * first + 0.1 * grad
    second_new = 0.999 * second + 0.001 * grad * grad
    update = first_new / (1.0 - 0.9**STEP) / (jnp.sqrt(second_new / (1.0 - 0.999**STEP)) + 1e-08)
    return (weight - rate * (update + decay * weight), first_new, second_new)


def laid_out(entry, leave, gates, down):
    layers = entry.shape[0]
    parts = []
    for l in range(layers):
        parts += [entry[l, 0], entry[l, 1], entry[l, 2], leave[l].T, gates[l, 0], gates[l, 1], down[l].T]
    return jnp.concatenate(parts, axis=1)


def taken_apart(flat, layers, ch, ff):
    per = 4 * ch + 3 * ff
    entry, leave, gates, down = [], [], [], []
    for l in range(layers):
        b = l * per
        entry.append(jnp.stack([flat[:, b + c * ch : b + (c + 1) * ch] for c in range(3)]))
        leave.append(flat[:, b + 3 * ch : b + 4 * ch].T)
        g = b + 4 * ch
        gates.append(jnp.stack([flat[:, g : g + ff], flat[:, g + ff : g + 2 * ff]]))
        down.append(flat[:, g + 2 * ff : g + 3 * ff].T)
    return tuple(jnp.stack(v) for v in (entry, leave, gates, down))


def per_device(
    inputs,
    cotangent,
    entry_weight,
    exit_weight,
    gate_up,
    down_weight,
    conv_kernel,
    norm_gain,
    entry_first,
    entry_second,
    exit_first,
    exit_second,
    gate_first,
    gate_second,
    down_first,
    down_second,
    kernel_first,
    kernel_second,
    gain_first,
    gain_second,
):
    layers, _, _, ch = entry_weight.shape
    ff = gate_up.shape[3]
    seqs = lax.axis_size("seq")
    mine = laid_out(
        entry_weight.astype(BF), exit_weight.astype(BF), gate_up.astype(BF), down_weight.astype(BF)
    )
    whole = lax.all_gather(mine, "seq", axis=0, tiled=True)
    hidden, grad, terms, small = run_step(inputs, cotangent, whole, conv_kernel, norm_gain, seqs)
    summed = lax.psum_scatter(terms, "seq", scatter_dimension=0, tiled=True).astype(F32)
    small = lax.psum(small, "seq")
    entry_grad, exit_grad, gate_grad, down_grad = taken_apart(summed, layers, ch, ff)
    kernel_grad = small[: 3 * layers].reshape(layers, 3, ch)
    gain_grad = small[3 * layers : 5 * layers].reshape(layers, 2, ch)
    entry_u, entry_f, entry_s = adamw(entry_weight, entry_grad, entry_first, entry_second, 0.01, 0.1)
    exit_u, exit_f, exit_s = adamw(exit_weight, exit_grad, exit_first, exit_second, 0.01, 0.1)
    gate_u, gate_f, gate_s = adamw(gate_up, gate_grad, gate_first, gate_second, 0.01, 0.1)
    down_u, down_f, down_s = adamw(down_weight, down_grad, down_first, down_second, 0.01, 0.1)
    kernel_u, kernel_f, kernel_s = adamw(conv_kernel, kernel_grad, kernel_first, kernel_second, 0.2, 0.0)
    gain_u, gain_f, gain_s = adamw(norm_gain, gain_grad, gain_first, gain_second, 0.2, 0.0)
    return (
        hidden,
        grad,
        entry_grad,
        exit_grad,
        gate_grad,
        down_grad,
        kernel_grad,
        gain_grad,
        entry_u,
        exit_u,
        gate_u,
        down_u,
        kernel_u,
        gain_u,
        entry_f,
        entry_s,
        exit_f,
        exit_s,
        gate_f,
        gate_s,
        down_f,
        down_s,
        kernel_f,
        kernel_s,
        gain_f,
        gain_s,
    )


def solution(mesh):
    tokens, rows, columns, replicated = (
        P("seq", "tp"),
        P(None, None, "seq", "tp"),
        P(None, "tp", "seq"),
        P(None, None, "tp"),
    )
    matrices = (rows, columns, rows, columns)
    moments = (rows, rows, columns, columns, rows, rows, columns, columns)
    return jax.shard_map(
        per_device,
        mesh=mesh,
        in_specs=(tokens, tokens, *matrices, replicated, replicated, *moments, *([replicated] * 4)),
        out_specs=(
            tokens,
            tokens,
            *matrices,
            replicated,
            replicated,
            *matrices,
            replicated,
            replicated,
            *moments,
            *([replicated] * 4),
        ),
        check_vma=False,
    )
```

```python
import functools

import jax
import jax.numpy as jnp
from jax import lax
from jax.experimental import pallas as pl
from jax.experimental.pallas import tpu as pltpu
from jax.sharding import PartitionSpec as P

STEP = 4
EPS = 1e-06
MESH = pl.DeviceIdType.MESH
BF = jnp.bfloat16
F32 = jnp.float32
SPAN = 384


def nn(a, b):
    return lax.dot_general(a, b, (((1,), (0,)), ((), ())), preferred_element_type=F32)


def nt(a, b):
    return lax.dot_general(a, b, (((1,), (1,)), ((), ())), preferred_element_type=F32)


def as_column(row):
    return jnp.broadcast_to(row, (128, row.shape[1])).T[:, 0:1]


def step_kernel(
    cfg,
    x_ref,
    cot_ref,
    mine_ref,
    kern_ref,
    gain_ref,
    out_ref,
    din_ref,
    final_ref,
    small_ref,
    rows,
    part,
    stage,
    landed,
    stats,
    normed,
    scales,
    ext,
    dext,
    bcx,
    conv,
    gated,
    gates,
    acted,
    dgates,
    dproj,
    turned,
    w_ref,
    gw_ref,
    from_pair,
    from_far,
    from_near,
    tally,
    ag_send,
    ag_recv,
    rs_send,
    rs_recv,
    st_send,
    st_recv,
    halo_send,
    halo_recv,
    w_send,
    w_recv,
    g_send,
    g_recv,
    t_send,
    t_recv,
    credit,
):
    layers, seqs, tokens, ch, ff = cfg
    half = tokens // 2
    width = 4 * ch
    per = 4 * ch + 3 * ff
    z = lax.axis_index("tp")
    s = lax.axis_index("seq")
    zr, zl, zo = lax.rem(z + 1, 4), lax.rem(z + 3, 4), lax.rem(z + 2, 4)
    after, before = lax.rem(s + 1, seqs), lax.rem(s + seqs - 1, seqs)

    c = lax.rem(s, 2)
    x, y = lax.div(s, 8), lax.rem(lax.div(s, 2), 4)
    u, v = x * (1 - c) + y * c, y * (1 - c) + x * c

    def place(uu, vv):
        return uu * (1 - c) + vv * c, vv * (1 - c) + uu * c

    def device(uu, vv):
        px, py = place(uu, vv)
        return (px * 8 + py * 2 + c, z)

    up, un, uo = lax.rem(u + 3, 4), lax.rem(u + 1, 4), lax.rem(u + 2, 4)
    vp, vn, vo = lax.rem(v + 3, 4), lax.rem(v + 1, 4), lax.rem(v + 2, 4)
    u_next, u_prev, v_next, v_prev = device(un, v), device(up, v), device(u, vn), device(u, vp)
    pair = (s + 1 - 2 * c, z)

    barrier = pltpu.get_barrier_semaphore()
    partners = [(s, zr), (s, zl), (s, zo), (after, z), (before, z), u_next, u_prev, v_next, v_prev, pair]
    partners += [device(uo, v), device(u, vo)]
    for where in partners:
        pl.semaphore_signal(barrier, inc=1, device_id=where, device_id_type=MESH)
    pl.semaphore_wait(barrier, len(partners))

    pending = []

    def send(src, dst, ssem, rsem, where):
        copy = pltpu.make_async_remote_copy(
            src_ref=src, dst_ref=dst, send_sem=ssem, recv_sem=rsem, device_id=where, device_id_type=MESH
        )
        copy.start()
        pending.append(copy)
        return copy

    def cols(who):
        return pl.ds(pl.multiple_of(who * ch, ch), ch)

    def own_rows(who):
        return pl.ds(pl.multiple_of(who * ch, ch), ch)

    top, low = pl.ds(0, half), pl.ds(half, half)

    def chunk_of(ref, lead, vv, lo, hi, where):
        if lead == 0:
            return ref.at[pl.ds(lo, hi - lo), vv, 0, :, where]
        return ref.at[vv, pl.ds(lo, hi - lo), 1, :, where]

    def send_either(make, ssem, rsem, where, held=pending):
        for core in (0, 1):

            @pl.when(c == core)
            def _(core=core):
                src, dst = make(core)
                pltpu.make_async_remote_copy(
                    src_ref=src, dst_ref=dst, send_sem=ssem, recv_sem=rsem, device_id=where, device_id_type=MESH
                ).start()

        src, dst = make(0)
        copy = pltpu.make_async_remote_copy(
            src_ref=src, dst_ref=dst, send_sem=ssem, recv_sem=rsem, device_id=where, device_id_type=MESH
        )
        held.append(copy)
        return copy

    spans = []
    for l in range(layers):
        at = l * per
        for size in (3 * ch, ch + 2 * SPAN, 2 * SPAN, 2 * SPAN, ff):
            spans.append(pl.ds(at, size))
            at += size

    class Weights:
        def __init__(self, k):
            self.k, self.where, self.stage = k, spans[k], 0

        def block(self, uu, vv, r=slice(None)):
            px, py = place(uu, vv)
            return w_ref.at[px, py, c, r, self.where]

        def move(self, ref, n, where):
            return send(ref, ref, w_send.at[self.k, n], w_recv.at[self.k, n], where)

        def move_row(self, vv, lo, hi, n, where):
            def make(core):
                ref = chunk_of(w_ref, core, vv, lo, hi, self.where)
                return ref, ref

            return send_either(make, w_send.at[self.k, n], w_recv.at[self.k, n], where)

        def step(self):
            stage, self.stage = self.stage, self.stage + 1
            if stage == 0:
                self.a0 = self.move(self.block(u, v), 0, u_next)
                self.a1 = self.move(self.block(u, v), 1, u_prev)
            elif stage == 1:
                self.a0.wait_recv()
                self.a2 = self.move(self.block(up, v, pl.ds(0, 16)), 2, u_next)
                self.a1.wait_recv()
                self.a3 = self.move(self.block(un, v, pl.ds(16, 16)), 3, u_prev)
            elif stage == 2:
                self.a2.wait_recv()
                self.a3.wait_recv()
                self.b0 = self.move_row(v, 0, 4, 4, v_next)
                self.b1 = self.move_row(v, 0, 4, 5, v_prev)
                self.p0 = self.move_row(v, 0, 4, 8, pair)
            elif stage == 3:
                self.b0.wait_recv()
                self.b2 = self.move_row(vp, 0, 2, 6, v_next)
                self.b1.wait_recv()
                self.b3 = self.move_row(vn, 2, 4, 7, v_prev)
                self.p1 = self.move_row(vp, 0, 4, 9, pair)
                self.p2 = self.move_row(vn, 0, 4, 10, pair)
            elif stage == 4:
                self.b2.wait_recv()
                self.b3.wait_recv()
                self.p3 = self.move_row(vo, 0, 4, 11, pair)
            else:
                for copy in (self.p0, self.p1, self.p2, self.p3):
                    copy.wait_recv()

    class Sums:
        def __init__(self, l, k, where):
            self.l, self.k, self.where, self.stage = l, k, where, 0
            self.total = pl.ds(l * per + where.start, where.size)
            self.first = l == layers - 1
            self.sent = []

        def send(self, src, dst, n, where):
            copy = pltpu.make_async_remote_copy(
                src_ref=src,
                dst_ref=dst,
                send_sem=g_send.at[self.l, self.k, n],
                recv_sem=g_recv.at[self.l, self.k, n],
                device_id=where,
                device_id_type=MESH,
            )
            copy.start()
            self.sent.append(copy)
            return copy

        def far(self, vv, lo, n, where):
            def make(core):
                return chunk_of(gw_ref, core, vv, lo, lo + 2, self.where), from_far.at[n - 1, :, :, self.where]

            copy = send_either(make, g_send.at[self.l, self.k, n], g_recv.at[self.l, self.k, n], where, self.sent)
            return copy

        def near(self, uu, r, n, where):
            px, py = place(uu, v)
            return self.send(gw_ref.at[px, py, c, r, self.where], from_near.at[n - 7, :, self.where], n, where)

        def add_far(self, vv, lo, slots):
            for i in range(2):
                px, py = place(lo + i, vv)
                value = gw_ref[px, py, c, :, self.where].astype(F32)
                for slot in slots:
                    value += from_far[slot, i, :, self.where].astype(F32)
                gw_ref[px, py, c, :, self.where] = value.astype(BF)

        def add_near(self, uu, r, slots):
            px, py = place(uu, v)
            value = gw_ref[px, py, c, r, self.where].astype(F32)
            for slot in slots:
                value += from_near[slot, :, self.where].astype(F32)
            return value

        def allow(self, kind, devices):
            if self.first:
                for where in devices:
                    pl.semaphore_signal(credit.at[self.k, kind], inc=1, device_id=where, device_id_type=MESH)

        def ask(self, kind, count):
            if not self.first:
                pl.semaphore_wait(credit.at[self.k, kind], count)

        def step(self):
            stage, self.stage = self.stage, self.stage + 1
            upper, lower = pl.ds(0, 16), pl.ds(16, 16)
            if stage == 0:
                self.ask(0, 1)
                self.q = self.send(
                    gw_ref.at[:, :, 1 - c, :, self.where], from_pair.at[:, :, :, self.where], 0, pair
                )
            elif stage == 1:
                self.q.wait_recv()

                @pl.loop(0, 4)
                def _(i):
                    gw_ref[i, :, c, :, self.where] = (
                        gw_ref[i, :, c, :, self.where].astype(F32) + from_pair[i, :, :, self.where].astype(F32)
                    ).astype(BF)

                self.allow(0, [pair])
                self.ask(1, 2)
                self.f0 = self.far(vo, 0, 1, v_next)
                self.f1 = self.far(vo, 2, 2, v_prev)
                self.f2 = self.far(vn, 2, 3, v_next)
                self.f3 = self.far(vp, 0, 4, v_prev)
            elif stage == 2:
                self.f0.wait_recv()
                self.add_far(vn, 0, [0])
                self.f4 = self.far(vn, 0, 5, v_next)
                self.f1.wait_recv()
                self.add_far(vp, 2, [1])
                self.f5 = self.far(vp, 2, 6, v_prev)
            elif stage == 3:
                for copy in (self.f2, self.f3, self.f4, self.f5):
                    copy.wait_recv()
                self.add_far(v, 0, [3, 4])
                self.add_far(v, 2, [2, 5])
                self.allow(1, [v_next, v_prev])
                self.ask(2, 2)
                self.n0 = self.near(uo, upper, 7, u_next)
                self.n1 = self.near(uo, lower, 8, u_prev)
                self.n2 = self.near(un, lower, 9, u_next)
                self.n3 = self.near(up, upper, 10, u_prev)
            elif stage == 4:
                self.n0.wait_recv()
                px, py = place(un, v)
                gw_ref[px, py, c, upper, self.where] = self.add_near(un, upper, [0]).astype(BF)
                self.n4 = self.near(un, upper, 11, u_next)
                self.n1.wait_recv()
                px, py = place(up, v)
                gw_ref[px, py, c, lower, self.where] = self.add_near(up, lower, [1]).astype(BF)
                self.n5 = self.near(up, lower, 12, u_prev)
            else:
                for copy in (self.n2, self.n3, self.n4, self.n5):
                    copy.wait_recv()
                final_ref[0:16, self.total] = self.add_near(u, upper, [3, 4])
                final_ref[16:32, self.total] = self.add_near(u, lower, [2, 5])
                self.allow(2, [u_next, u_prev])
                for copy in self.sent:
                    copy.wait_send()

    fetches = [Weights(k) for k in range(len(spans))]
    fetched = [0]
    sums = []

    def tick():
        t = fetched[0]
        if t < len(fetches) + 5:
            fetched[0] += 1
            for k, fetch in enumerate(fetches):
                if 0 <= t - k < 6:
                    fetch.step()
        for total in sums:
            if total.stage < 6:
                total.step()

    def need(l, part_index):
        while fetches[5 * l + part_index].stage < 6:
            tick()

    def ready(l, k, at, size):
        total = Sums(l, k, pl.ds(at, size))
        total.step()
        sums.append(total)

    def clear(k):
        for total in sums:
            if total.k == k:
                while total.stage < 6:
                    tick()

    def weight(where):
        return w_ref[:, :, :, :, where].reshape(width, where.size)

    def weight_rows(who, where):
        return w_ref[who, :, :, :, where].reshape(ch, where.size)

    w_ref[x, y, c] = mine_ref[...]
    tick()

    class Gather:
        def __init__(self, i, block):
            self.i = i
            rows[i, :, cols(z)] = block
            mine = lambda r: rows.at[i, r, cols(z)]
            self.r1 = send(mine(top), mine(top), ag_send.at[i, 0], ag_recv.at[i, 0], (s, zr))
            self.l1 = send(mine(low), mine(low), ag_send.at[i, 1], ag_recv.at[i, 1], (s, zl))
            self.r2 = send(mine(low), mine(low), ag_send.at[i, 2], ag_recv.at[i, 2], (s, zr))
            self.l2 = send(mine(top), mine(top), ag_send.at[i, 3], ag_recv.at[i, 3], (s, zl))

        def pass_on(self):
            i = self.i
            self.r1.wait_recv()
            b = rows.at[i, top, cols(zl)]
            self.rf = send(b, b, ag_send.at[i, 4], ag_recv.at[i, 4], (s, zr))
            self.l1.wait_recv()
            b = rows.at[i, low, cols(zr)]
            self.lf = send(b, b, ag_send.at[i, 5], ag_recv.at[i, 5], (s, zl))

        def finish(self):
            for c in (self.r2, self.l2, self.rf, self.lf):
                c.wait_recv()

    class Scatter:
        def __init__(self, i, piece):
            self.i = i
            at = lambda k, r: stage.at[i, k, r]
            to = lambda k: landed.at[i, k]
            stage[i, 0] = piece(zo).astype(BF)
            self.r1 = send(at(0, top), to(0), rs_send.at[i, 0], rs_recv.at[i, 0], (s, zr))
            self.l1 = send(at(0, low), to(1), rs_send.at[i, 1], rs_recv.at[i, 1], (s, zl))
            right = piece(zr)
            stage[i, 1, half:] = right[half:].astype(BF)
            self.r2 = send(at(1, low), to(2), rs_send.at[i, 2], rs_recv.at[i, 2], (s, zr))
            part[0] = right[:half]
            left = piece(zl)
            stage[i, 2, :half] = left[:half].astype(BF)
            self.l2 = send(at(2, top), to(3), rs_send.at[i, 3], rs_recv.at[i, 3], (s, zl))
            part[1] = left[half:]
            own = piece(z)
            part[2] = own[:half]
            part[3] = own[half:]

        def pass_on(self):
            i = self.i
            self.r1.wait_recv()
            stage[i, 1, :half] = (part[0] + landed[i, 0].astype(F32)).astype(BF)
            self.rf = send(stage.at[i, 1, top], landed.at[i, 4], rs_send.at[i, 4], rs_recv.at[i, 4], (s, zr))
            self.l1.wait_recv()
            stage[i, 2, half:] = (part[1] + landed[i, 1].astype(F32)).astype(BF)
            self.lf = send(stage.at[i, 2, low], landed.at[i, 5], rs_send.at[i, 5], rs_recv.at[i, 5], (s, zl))

        def finish(self):
            i = self.i
            for c in (self.r2, self.l2, self.rf, self.lf):
                c.wait_recv()
            upper = part[2] + landed[i, 4].astype(F32) + landed[i, 3].astype(F32)
            lower = part[3] + landed[i, 2].astype(F32) + landed[i, 5].astype(F32)
            return jnp.concatenate([upper, lower], axis=0)

    def row_total(i, value):
        sums = jnp.sum(value, axis=1, keepdims=True)
        stats[i, z] = jnp.broadcast_to(sums, (tokens, 128)).T[0:8]
        there = stats.at[i, z]
        got = [
            send(there, there, st_send.at[i, k], st_recv.at[i, k], (s, who))
            for k, who in enumerate((zr, zl, zo))
        ]
        for c in got:
            c.wait_recv()
        total = stats[i, 0] + stats[i, 1] + stats[i, 2] + stats[i, 3]
        return as_column(total[0:1])

    def columns(at, j, size=SPAN):
        return pl.ds(at + j * size, size)

    def turn(left_index):
        turned[...] = rows[left_index].T

    def weight_grad(l, k, right_ref, lead, start, size, at):
        clear(k)
        piece = nn(turned[...], right_ref[lead, :, start : start + size]).astype(BF)
        gw_ref[:, :, :, :, at : at + size] = piece.reshape(4, 4, 2, 32, size)

    def norm_forward(k, h, gain):
        total = row_total(k, h * h)
        scale = lax.rsqrt(total / width + EPS)
        scales[k] = jnp.broadcast_to(scale, (tokens, 128))
        a = h * scale
        normed[k] = a
        return (a * gain).astype(BF)

    def norm_backward(k, dn, gain, small_row):
        a = normed[k]
        t = dn * gain
        small_ref[pl.ds(small_row, 1), :] = jnp.sum(dn * a, axis=0, keepdims=True)
        inner = row_total(2 * layers + k, t * a)
        return scales[k][:, 0:1] * (t - a * (inner / width))

    small_ref[...] = jnp.zeros_like(small_ref)
    hidden = x_ref[...]
    cot_gather = None
    for l in range(layers):
        base = l * per
        at_exit, at_gate, at_down = base + 3 * ch, base + 4 * ch, base + 4 * ch + 2 * ff
        n1 = norm_forward(2 * l, hidden, gain_ref[l, 0:1])
        gather = Gather(2 * l, n1)
        if l == 0:
            cot_gather = Gather(2 * layers + 2 * (layers - 1), cot_ref[...].astype(BF))
        tick()
        gather.pass_on()
        tick()
        gather.finish()
        if l == 0:
            cot_gather.pass_on()
        need(l, 0)
        full = rows[2 * l]
        bm = nn(full, weight(columns(base, 0, ch)))
        xm = nn(full, weight(columns(base, 2, ch)))
        bx = bm * xm
        ext[l, 8:] = bx
        tail = send(
            ext.at[l, pl.ds(tokens, 8)], ext.at[l, pl.ds(0, 8)], halo_send.at[l], halo_recv.at[l], (after, z)
        )
        bcx[l, 0] = bm
        bcx[l, 2] = xm
        cm = nn(full, weight(columns(base, 1, ch)))
        bcx[l, 1] = cm
        tick()
        tail.wait_recv()
        head = ext[l, 0:8]
        ext[l, 0:8] = jnp.where(s > 0, head, jnp.zeros_like(head))
        k = kern_ref[l]
        zc = k[0:1] * ext[l, 6 : 6 + tokens] + k[1:2] * ext[l, 7 : 7 + tokens] + k[2:3] * ext[l, 8 : 8 + tokens]
        conv[l] = zc
        gated[l] = (cm * zc).astype(BF)

        def exit_piece(who, l=l, at=at_exit):
            return nt(gated[l], weight_rows(who, columns(at, 0, ch)))

        need(l, 1)
        scatter = Scatter(2 * l, exit_piece)
        tick()
        scatter.pass_on()
        tick()
        mid = hidden + scatter.finish()
        n2 = norm_forward(2 * l + 1, mid, gain_ref[l, 1:2])
        gather = Gather(2 * l + 1, n2)
        tick()
        gather.pass_on()
        tick()
        gather.finish()
        need(l, 1)

        for j in range(ff // SPAN):
            need(l, 1 + j)
            both = nn(rows[2 * l + 1], weight(columns(at_gate, j, 2 * SPAN)))
            gates[l, :, j * 2 * SPAN : (j + 1) * 2 * SPAN] = both
            g, up_value = both[:, :SPAN], both[:, SPAN:]
            acted[l, :, j * SPAN : (j + 1) * SPAN] = (g * jax.nn.sigmoid(g) * up_value).astype(BF)

        def down_piece(who, l=l, at=at_down):
            return nt(acted[l], weight_rows(who, columns(at, 0, ff)))

        need(l, 4)
        scatter = Scatter(2 * l + 1, down_piece)
        tick()
        scatter.pass_on()
        tick()
        hidden = mid + scatter.finish()
    out_ref[...] = hidden

    grad = cot_ref[...]
    for l in reversed(range(layers)):
        base = l * per
        at_exit, at_gate, at_down = base + 3 * ch, base + 4 * ch, base + 4 * ch + 2 * ff
        ie = 2 * layers + 2 * l
        if l == layers - 1:
            gather = cot_gather
        else:
            gather = Gather(ie, grad.astype(BF))
            tick()
            gather.pass_on()
            tick()
        gather.finish()

        for j in range(ff // SPAN):
            ds = nn(rows[ie], weight(columns(at_down, j)))
            g = gates[l, :, j * 2 * SPAN : j * 2 * SPAN + SPAN]
            up_value = gates[l, :, j * 2 * SPAN + SPAN : (j + 1) * 2 * SPAN]
            sig = jax.nn.sigmoid(g)
            dgates[0, :, j * 2 * SPAN : j * 2 * SPAN + SPAN] = (
                ds * up_value * sig * (1.0 + g * (1.0 - sig))
            ).astype(BF)
            dgates[0, :, j * 2 * SPAN + SPAN : (j + 1) * 2 * SPAN] = (ds * (g * sig)).astype(BF)

        def norm2_piece(who, at_gate=at_gate):
            return nt(dgates[0], weight_rows(who, columns(at_gate, 0, 2 * ff)))

        scatter = Scatter(2 * layers + 2 * l, norm2_piece)
        turn(ie)
        weight_grad(l, 4, acted, l, 0, ff, 4 * ch + 2 * ff)
        scatter.pass_on()
        ready(l, 4, 4 * ch + 2 * ff, ff)
        turn(2 * l + 1)
        for j in range(ff // SPAN):
            weight_grad(l, 1 + j, dgates, 0, j * 2 * SPAN, 2 * SPAN, 4 * ch + j * 2 * SPAN)
            tick()
            ready(l, 1 + j, 4 * ch + j * 2 * SPAN, 2 * SPAN)
        dn2 = scatter.finish()
        dmid = grad + norm_backward(2 * l + 1, dn2, gain_ref[l, 1:2], 3 * layers + 2 * l + 1)
        gather = Gather(ie + 1, dmid.astype(BF))
        tick()
        gather.pass_on()
        tick()
        gather.finish()
        dy = nn(rows[ie + 1], weight(columns(at_exit, 0, ch)))
        dz = dy * bcx[l, 1]
        dext[l, :tokens] = dz
        tail = send(
            dext.at[l, pl.ds(0, 8)],
            dext.at[l, pl.ds(tokens, 8)],
            halo_send.at[layers + l],
            halo_recv.at[layers + l],
            (before, z),
        )
        dproj[0, :, ch : 2 * ch] = (dy * conv[l]).astype(BF)
        for j in range(3):
            small_ref[pl.ds(3 * l + j, 1), :] = jnp.sum(dz * ext[l, 6 + j : 6 + j + tokens], axis=0, keepdims=True)
        turn(ie + 1)
        weight_grad(l, 0, gated, l, 0, ch, 3 * ch)
        tail.wait_recv()
        last = dext[l, tokens:]
        dext[l, tokens:] = jnp.where(s < seqs - 1, last, jnp.zeros_like(last))
        k = kern_ref[l]
        dbx = k[2:3] * dext[l, 0:tokens] + k[1:2] * dext[l, 1 : 1 + tokens] + k[0:1] * dext[l, 2 : 2 + tokens]
        dproj[0, :, :ch] = (dbx * bcx[l, 2]).astype(BF)
        dproj[0, :, 2 * ch :] = (dbx * bcx[l, 0]).astype(BF)

        def norm1_piece(who, base=base):
            return nt(dproj[0], weight_rows(who, columns(base, 0, 3 * ch)))

        scatter = Scatter(2 * layers + 2 * l + 1, norm1_piece)
        turn(2 * l)
        weight_grad(l, 0, dproj, 0, 0, 3 * ch, 0)
        scatter.pass_on()
        ready(l, 0, 0, 4 * ch)
        dn1 = scatter.finish()
        grad = dmid + norm_backward(2 * l, dn1, gain_ref[l, 0:1], 3 * layers + 2 * l)
    din_ref[...] = grad
    own = tally.at[0, 0]
    tally[0, 0] = small_ref[...]
    copy = send(own, tally.at[0, 1], t_send.at[0], t_recv.at[0], pair)
    tick()
    copy.wait_recv()
    tally[1, x] = tally[0, 0] + tally[0, 1]
    stages = ((1, x, lambda k: (lax.rem(x + k, 4) * 8 + y * 2 + c, z)), (2, y, lambda k: (x * 8 + lax.rem(y + k, 4) * 2 + c, z)))
    for n, here, where in stages:
        slot = tally.at[n, here]
        copies = [send(slot, slot, t_send.at[3 * n - 3 + k], t_recv.at[3 * n - 3 + k], where(k)) for k in (1, 2, 3)]
        tick()
        for copy in copies:
            copy.wait_recv()
        total = tally[n, 0] + tally[n, 1] + tally[n, 2] + tally[n, 3]
        if n == 1:
            tally[2, y] = total
        else:
            small_ref[...] = total
    while any(total.stage < 6 for total in sums):
        tick()
    for copy in pending:
        copy.wait_send()


def run_step(x, cot, mine, kern, gain, seqs):
    layers, taps, ch = kern.shape
    tokens = x.shape[0]
    width = 4 * ch
    per = mine.shape[1] // layers
    ff = (per - 4 * ch) // 3
    n = 4 * layers
    vmem = pl.BlockSpec(memory_space=pltpu.VMEM)
    dma = pltpu.SemaphoreType.DMA
    return pl.pallas_call(
        functools.partial(step_kernel, (layers, seqs, tokens, ch, ff)),
        out_shape=(
            jax.ShapeDtypeStruct((tokens, ch), F32),
            jax.ShapeDtypeStruct((tokens, ch), F32),
            jax.ShapeDtypeStruct(mine.shape, F32),
            jax.ShapeDtypeStruct((16, ch), F32),
        ),
        in_specs=[vmem] * 5,
        out_specs=(vmem,) * 4,
        scratch_shapes=[
            pltpu.VMEM((n, tokens, width), BF),
            pltpu.VMEM((4, tokens // 2, ch), F32),
            pltpu.VMEM((n, 3, tokens, ch), BF),
            pltpu.VMEM((n, 6, tokens // 2, ch), BF),
            pltpu.VMEM((n, 4, 8, tokens), F32),
            pltpu.VMEM((2 * layers, tokens, ch), F32),
            pltpu.VMEM((2 * layers, tokens, 128), F32),
            pltpu.VMEM((layers, tokens + 8, ch), F32),
            pltpu.VMEM((layers, tokens + 8, ch), F32),
            pltpu.VMEM((layers, 3, tokens, ch), F32),
            pltpu.VMEM((layers, tokens, ch), F32),
            pltpu.VMEM((layers, tokens, ch), BF),
            pltpu.VMEM((layers, tokens, 2 * ff), F32),
            pltpu.VMEM((layers, tokens, ff), BF),
            pltpu.VMEM((1, tokens, 2 * ff), BF),
            pltpu.VMEM((1, tokens, 3 * ch), BF),
            pltpu.VMEM((width, tokens), BF),
            pltpu.VMEM((4, 4, 2, 32, layers * per), BF),
            pltpu.VMEM((4, 4, 2, 32, per), BF),
            pltpu.VMEM((4, 4, 32, per), BF),
            pltpu.VMEM((6, 2, 32, per), BF),
            pltpu.VMEM((6, 16, per), BF),
            pltpu.VMEM((3, 4, 16, ch), F32),
            dma((n, 6)),
            dma((n, 6)),
            dma((n, 6)),
            dma((n, 6)),
            dma((n, 3)),
            dma((n, 3)),
            dma((2 * layers,)),
            dma((2 * layers,)),
            dma((5 * layers, 12)),
            dma((5 * layers, 12)),
            dma((layers, 5, 13)),
            dma((layers, 5, 13)),
            dma((7,)),
            dma((7,)),
            pltpu.SemaphoreType.REGULAR((5, 3)),
        ],
        compiler_params=pltpu.CompilerParams(
            collective_id=0, has_side_effects=True, vmem_limit_bytes=67043328
        ),
        name="layers",
    )(x, cot, mine, kern, gain)


def adamw(weight, grad, first, second, rate, decay):
    first_new = 0.9 * first + 0.1 * grad
    second_new = 0.999 * second + 0.001 * grad * grad
    update = first_new / (1.0 - 0.9**STEP) / (jnp.sqrt(second_new / (1.0 - 0.999**STEP)) + 1e-08)
    return (weight - rate * (update + decay * weight), first_new, second_new)


def laid_out(entry, leave, gates, down):
    layers, ff = entry.shape[0], gates.shape[3]
    parts = []
    for l in range(layers):
        parts += [entry[l, 0], entry[l, 1], entry[l, 2], leave[l].T]
        for j in range(0, ff, SPAN):
            parts += [gates[l, 0, :, j : j + SPAN], gates[l, 1, :, j : j + SPAN]]
        parts.append(down[l].T)
    return jnp.concatenate(parts, axis=1)


def taken_apart(flat, layers, ch, ff):
    per = 4 * ch + 3 * ff
    entry, leave, gates, down = [], [], [], []
    for l in range(layers):
        b = l * per
        entry.append(jnp.stack([flat[:, b + c * ch : b + (c + 1) * ch] for c in range(3)]))
        leave.append(flat[:, b + 3 * ch : b + 4 * ch].T)
        g = b + 4 * ch
        halves = [
            jnp.concatenate([flat[:, g + 2 * j + k : g + 2 * j + k + SPAN] for j in range(0, ff, SPAN)], axis=1)
            for k in (0, SPAN)
        ]
        gates.append(jnp.stack(halves))
        down.append(flat[:, g + 2 * ff : g + 3 * ff].T)
    return tuple(jnp.stack(v) for v in (entry, leave, gates, down))


def per_device(
    inputs,
    cotangent,
    entry_weight,
    exit_weight,
    gate_up,
    down_weight,
    conv_kernel,
    norm_gain,
    entry_first,
    entry_second,
    exit_first,
    exit_second,
    gate_first,
    gate_second,
    down_first,
    down_second,
    kernel_first,
    kernel_second,
    gain_first,
    gain_second,
):
    layers, _, _, ch = entry_weight.shape
    ff = gate_up.shape[3]
    seqs = lax.axis_size("seq")
    mine = laid_out(
        entry_weight.astype(BF), exit_weight.astype(BF), gate_up.astype(BF), down_weight.astype(BF)
    )
    hidden, grad, summed, small = run_step(inputs, cotangent, mine, conv_kernel, norm_gain, seqs)
    entry_grad, exit_grad, gate_grad, down_grad = taken_apart(summed, layers, ch, ff)
    kernel_grad = small[: 3 * layers].reshape(layers, 3, ch)
    gain_grad = small[3 * layers : 5 * layers].reshape(layers, 2, ch)
    entry_u, entry_f, entry_s = adamw(entry_weight, entry_grad, entry_first, entry_second, 0.01, 0.1)
    exit_u, exit_f, exit_s = adamw(exit_weight, exit_grad, exit_first, exit_second, 0.01, 0.1)
    gate_u, gate_f, gate_s = adamw(gate_up, gate_grad, gate_first, gate_second, 0.01, 0.1)
    down_u, down_f, down_s = adamw(down_weight, down_grad, down_first, down_second, 0.01, 0.1)
    kernel_u, kernel_f, kernel_s = adamw(conv_kernel, kernel_grad, kernel_first, kernel_second, 0.2, 0.0)
    gain_u, gain_f, gain_s = adamw(norm_gain, gain_grad, gain_first, gain_second, 0.2, 0.0)
    return (
        hidden,
        grad,
        entry_grad,
        exit_grad,
        gate_grad,
        down_grad,
        kernel_grad,
        gain_grad,
        entry_u,
        exit_u,
        gate_u,
        down_u,
        kernel_u,
        gain_u,
        entry_f,
        entry_s,
        exit_f,
        exit_s,
        gate_f,
        gate_s,
        down_f,
        down_s,
        kernel_f,
        kernel_s,
        gain_f,
        gain_s,
    )


def solution(mesh):
    tokens, rows, columns, replicated = (
        P("seq", "tp"),
        P(None, None, "seq", "tp"),
        P(None, "tp", "seq"),
        P(None, None, "tp"),
    )
    matrices = (rows, columns, rows, columns)
    moments = (rows, rows, columns, columns, rows, rows, columns, columns)
    return jax.shard_map(
        per_device,
        mesh=mesh,
        in_specs=(tokens, tokens, *matrices, replicated, replicated, *moments, *([replicated] * 4)),
        out_specs=(
            tokens,
            tokens,
            *matrices,
            replicated,
            replicated,
            *matrices,
            replicated,
            replicated,
            *moments,
            *([replicated] * 4),
        ),
        check_vma=False,
    )
```

```python
import functools

import jax
import jax.numpy as jnp
from jax import lax
from jax.experimental import pallas as pl
from jax.experimental.pallas import tpu as pltpu
from jax.sharding import PartitionSpec as P

STEP = 4
EPS = 1e-06
MESH = pl.DeviceIdType.MESH
BF = jnp.bfloat16
F32 = jnp.float32
SPAN = 384


def nn(a, b):
    return lax.dot_general(a, b, (((1,), (0,)), ((), ())), preferred_element_type=F32)


def nt(a, b):
    return lax.dot_general(a, b, (((1,), (1,)), ((), ())), preferred_element_type=F32)


def as_column(row):
    return jnp.broadcast_to(row, (128, row.shape[1])).T[:, 0:1]


def step_kernel(
    cfg,
    x_ref,
    cot_ref,
    entry_ref,
    exit_ref,
    gate_ref,
    down_ref,
    kern_ref,
    gain_ref,
    out_ref,
    din_ref,
    final_ref,
    small_ref,
    rows,
    part,
    stage,
    landed,
    stats,
    normed,
    scales,
    ext,
    dext,
    bcx,
    conv,
    gated,
    gates,
    acted,
    dgates,
    dproj,
    turned,
    w_ref,
    gw_ref,
    from_pair,
    from_far,
    from_near,
    tally,
    ag_send,
    ag_recv,
    rs_send,
    rs_recv,
    st_send,
    st_recv,
    halo_send,
    halo_recv,
    w_send,
    w_recv,
    g_send,
    g_recv,
    t_send,
    t_recv,
    credit,
):
    layers, seqs, tokens, ch, ff = cfg
    half = tokens // 2
    width = 4 * ch
    per = 4 * ch + 3 * ff
    z = lax.axis_index("tp")
    s = lax.axis_index("seq")
    zr, zl, zo = lax.rem(z + 1, 4), lax.rem(z + 3, 4), lax.rem(z + 2, 4)
    after, before = lax.rem(s + 1, seqs), lax.rem(s + seqs - 1, seqs)

    c = lax.rem(s, 2)
    x, y = lax.div(s, 8), lax.rem(lax.div(s, 2), 4)
    u, v = x * (1 - c) + y * c, y * (1 - c) + x * c

    def place(uu, vv):
        return uu * (1 - c) + vv * c, vv * (1 - c) + uu * c

    def device(uu, vv):
        px, py = place(uu, vv)
        return (px * 8 + py * 2 + c, z)

    up, un, uo = lax.rem(u + 3, 4), lax.rem(u + 1, 4), lax.rem(u + 2, 4)
    vp, vn, vo = lax.rem(v + 3, 4), lax.rem(v + 1, 4), lax.rem(v + 2, 4)
    u_next, u_prev, v_next, v_prev = device(un, v), device(up, v), device(u, vn), device(u, vp)
    pair = (s + 1 - 2 * c, z)

    barrier = pltpu.get_barrier_semaphore()
    partners = [(s, zr), (s, zl), (s, zo), (after, z), (before, z), u_next, u_prev, v_next, v_prev, pair]
    partners += [device(uo, v), device(u, vo)]
    for where in partners:
        pl.semaphore_signal(barrier, inc=1, device_id=where, device_id_type=MESH)
    pl.semaphore_wait(barrier, len(partners))

    pending = []

    def send(src, dst, ssem, rsem, where):
        copy = pltpu.make_async_remote_copy(
            src_ref=src, dst_ref=dst, send_sem=ssem, recv_sem=rsem, device_id=where, device_id_type=MESH
        )
        copy.start()
        pending.append(copy)
        return copy

    def cols(who):
        return pl.ds(pl.multiple_of(who * ch, ch), ch)

    def own_rows(who):
        return pl.ds(pl.multiple_of(who * ch, ch), ch)

    top, low = pl.ds(0, half), pl.ds(half, half)

    def chunk_of(ref, lead, vv, lo, hi, where):
        if lead == 0:
            return ref.at[pl.ds(lo, hi - lo), vv, 0, :, where]
        return ref.at[vv, pl.ds(lo, hi - lo), 1, :, where]

    def send_either(make, ssem, rsem, where, held=pending):
        for core in (0, 1):

            @pl.when(c == core)
            def _(core=core):
                src, dst = make(core)
                pltpu.make_async_remote_copy(
                    src_ref=src, dst_ref=dst, send_sem=ssem, recv_sem=rsem, device_id=where, device_id_type=MESH
                ).start()

        src, dst = make(0)
        copy = pltpu.make_async_remote_copy(
            src_ref=src, dst_ref=dst, send_sem=ssem, recv_sem=rsem, device_id=where, device_id_type=MESH
        )
        held.append(copy)
        return copy

    spans = []
    for l in range(layers):
        at = l * per
        for size in (3 * ch, ch + 2 * SPAN, 2 * SPAN, 2 * SPAN, ff):
            spans.append(pl.ds(at, size))
            at += size

    def pack(k):
        l, part_index = k // 5, k % 5
        at = l * per

        def put(start, value):
            w_ref[x, y, c, :, start : start + value.shape[1]] = value.astype(BF)

        if part_index == 0:
            for j in range(3):
                put(at + j * ch, entry_ref[l, j])
        elif part_index == 4:
            put(at + 4 * ch + 2 * ff, down_ref[l])
        else:
            if part_index == 1:
                put(at + 3 * ch, exit_ref[l])
            j = part_index - 1
            for half_index in range(2):
                put(
                    at + 4 * ch + (2 * j + half_index) * SPAN,
                    gate_ref[l, half_index, :, j * SPAN : (j + 1) * SPAN],
                )

    class Weights:
        def __init__(self, k):
            self.k, self.where, self.stage = k, spans[k], 0

        def block(self, uu, vv, r=slice(None)):
            px, py = place(uu, vv)
            return w_ref.at[px, py, c, r, self.where]

        def move(self, ref, n, where):
            return send(ref, ref, w_send.at[self.k, n], w_recv.at[self.k, n], where)

        def move_row(self, vv, lo, hi, n, where):
            def make(core):
                ref = chunk_of(w_ref, core, vv, lo, hi, self.where)
                return ref, ref

            return send_either(make, w_send.at[self.k, n], w_recv.at[self.k, n], where)

        def step(self):
            stage, self.stage = self.stage, self.stage + 1
            if stage == 0:
                pack(self.k)
                self.a0 = self.move(self.block(u, v), 0, u_next)
                self.a1 = self.move(self.block(u, v), 1, u_prev)
            elif stage == 1:
                self.a0.wait_recv()
                self.a2 = self.move(self.block(up, v, pl.ds(0, 16)), 2, u_next)
                self.a1.wait_recv()
                self.a3 = self.move(self.block(un, v, pl.ds(16, 16)), 3, u_prev)
            elif stage == 2:
                self.a2.wait_recv()
                self.a3.wait_recv()
                self.b0 = self.move_row(v, 0, 4, 4, v_next)
                self.b1 = self.move_row(v, 0, 4, 5, v_prev)
                self.p0 = self.move_row(v, 0, 4, 8, pair)
            elif stage == 3:
                self.b0.wait_recv()
                self.b2 = self.move_row(vp, 0, 2, 6, v_next)
                self.b1.wait_recv()
                self.b3 = self.move_row(vn, 2, 4, 7, v_prev)
                self.p1 = self.move_row(vp, 0, 4, 9, pair)
                self.p2 = self.move_row(vn, 0, 4, 10, pair)
            elif stage == 4:
                self.b2.wait_recv()
                self.b3.wait_recv()
                self.p3 = self.move_row(vo, 0, 4, 11, pair)
            else:
                for copy in (self.p0, self.p1, self.p2, self.p3):
                    copy.wait_recv()

    class Sums:
        def __init__(self, l, k, where):
            self.l, self.k, self.where, self.stage = l, k, where, 0
            self.total = pl.ds(l * per + where.start, where.size)
            self.first = l == layers - 1
            self.sent = []

        def send(self, src, dst, n, where):
            copy = pltpu.make_async_remote_copy(
                src_ref=src,
                dst_ref=dst,
                send_sem=g_send.at[self.l, self.k, n],
                recv_sem=g_recv.at[self.l, self.k, n],
                device_id=where,
                device_id_type=MESH,
            )
            copy.start()
            self.sent.append(copy)
            return copy

        def far(self, vv, lo, n, where):
            def make(core):
                return chunk_of(gw_ref, core, vv, lo, lo + 2, self.where), from_far.at[n - 1, :, :, self.where]

            copy = send_either(make, g_send.at[self.l, self.k, n], g_recv.at[self.l, self.k, n], where, self.sent)
            return copy

        def near(self, uu, r, n, where):
            px, py = place(uu, v)
            return self.send(gw_ref.at[px, py, c, r, self.where], from_near.at[n - 7, :, self.where], n, where)

        def add_far(self, vv, lo, slots):
            for i in range(2):
                px, py = place(lo + i, vv)
                value = gw_ref[px, py, c, :, self.where].astype(F32)
                for slot in slots:
                    value += from_far[slot, i, :, self.where].astype(F32)
                gw_ref[px, py, c, :, self.where] = value.astype(BF)

        def add_near(self, uu, r, slots):
            px, py = place(uu, v)
            value = gw_ref[px, py, c, r, self.where].astype(F32)
            for slot in slots:
                value += from_near[slot, :, self.where].astype(F32)
            return value

        def allow(self, kind, devices):
            if self.first:
                for where in devices:
                    pl.semaphore_signal(credit.at[self.k, kind], inc=1, device_id=where, device_id_type=MESH)

        def ask(self, kind, count):
            if not self.first:
                pl.semaphore_wait(credit.at[self.k, kind], count)

        def step(self):
            stage, self.stage = self.stage, self.stage + 1
            upper, lower = pl.ds(0, 16), pl.ds(16, 16)
            if stage == 0:
                self.ask(0, 1)
                self.q = self.send(
                    gw_ref.at[:, :, 1 - c, :, self.where], from_pair.at[:, :, :, self.where], 0, pair
                )
            elif stage == 1:
                self.q.wait_recv()

                @pl.loop(0, 4)
                def _(i):
                    gw_ref[i, :, c, :, self.where] = (
                        gw_ref[i, :, c, :, self.where].astype(F32) + from_pair[i, :, :, self.where].astype(F32)
                    ).astype(BF)

                self.allow(0, [pair])
                self.ask(1, 2)
                self.f0 = self.far(vo, 0, 1, v_next)
                self.f1 = self.far(vo, 2, 2, v_prev)
                self.f2 = self.far(vn, 2, 3, v_next)
                self.f3 = self.far(vp, 0, 4, v_prev)
            elif stage == 2:
                self.f0.wait_recv()
                self.add_far(vn, 0, [0])
                self.f4 = self.far(vn, 0, 5, v_next)
                self.f1.wait_recv()
                self.add_far(vp, 2, [1])
                self.f5 = self.far(vp, 2, 6, v_prev)
            elif stage == 3:
                for copy in (self.f2, self.f3, self.f4, self.f5):
                    copy.wait_recv()
                self.add_far(v, 0, [3, 4])
                self.add_far(v, 2, [2, 5])
                self.allow(1, [v_next, v_prev])
                self.ask(2, 2)
                self.n0 = self.near(uo, upper, 7, u_next)
                self.n1 = self.near(uo, lower, 8, u_prev)
                self.n2 = self.near(un, lower, 9, u_next)
                self.n3 = self.near(up, upper, 10, u_prev)
            elif stage == 4:
                self.n0.wait_recv()
                px, py = place(un, v)
                gw_ref[px, py, c, upper, self.where] = self.add_near(un, upper, [0]).astype(BF)
                self.n4 = self.near(un, upper, 11, u_next)
                self.n1.wait_recv()
                px, py = place(up, v)
                gw_ref[px, py, c, lower, self.where] = self.add_near(up, lower, [1]).astype(BF)
                self.n5 = self.near(up, lower, 12, u_prev)
            else:
                for copy in (self.n2, self.n3, self.n4, self.n5):
                    copy.wait_recv()
                final_ref[0:16, self.total] = self.add_near(u, upper, [3, 4])
                final_ref[16:32, self.total] = self.add_near(u, lower, [2, 5])
                self.allow(2, [u_next, u_prev])
                for copy in self.sent:
                    copy.wait_send()

    fetches = [Weights(k) for k in range(len(spans))]
    fetched = [0]
    sums = []

    def tick():
        t = fetched[0]
        if t < len(fetches) + 5:
            fetched[0] += 1
            for k, fetch in enumerate(fetches):
                if 0 <= t - k < 6:
                    fetch.step()
        for total in sums:
            if total.stage < 6:
                total.step()

    def need(l, part_index):
        while fetches[5 * l + part_index].stage < 6:
            tick()

    def ready(l, k, at, size):
        total = Sums(l, k, pl.ds(at, size))
        total.step()
        sums.append(total)

    def clear(k):
        for total in sums:
            if total.k == k:
                while total.stage < 6:
                    tick()

    def weight(where):
        return w_ref[:, :, :, :, where].reshape(width, where.size)

    def weight_rows(who, where):
        return w_ref[who, :, :, :, where].reshape(ch, where.size)

    tick()

    class Gather:
        def __init__(self, i, block):
            self.i = i
            rows[i, :, cols(z)] = block
            mine = lambda r: rows.at[i, r, cols(z)]
            self.r1 = send(mine(top), mine(top), ag_send.at[i, 0], ag_recv.at[i, 0], (s, zr))
            self.l1 = send(mine(low), mine(low), ag_send.at[i, 1], ag_recv.at[i, 1], (s, zl))
            self.r2 = send(mine(low), mine(low), ag_send.at[i, 2], ag_recv.at[i, 2], (s, zr))
            self.l2 = send(mine(top), mine(top), ag_send.at[i, 3], ag_recv.at[i, 3], (s, zl))

        def pass_on(self):
            i = self.i
            self.r1.wait_recv()
            b = rows.at[i, top, cols(zl)]
            self.rf = send(b, b, ag_send.at[i, 4], ag_recv.at[i, 4], (s, zr))
            self.l1.wait_recv()
            b = rows.at[i, low, cols(zr)]
            self.lf = send(b, b, ag_send.at[i, 5], ag_recv.at[i, 5], (s, zl))

        def finish(self):
            for c in (self.r2, self.l2, self.rf, self.lf):
                c.wait_recv()

    class Scatter:
        def __init__(self, i, piece):
            self.i = i
            at = lambda k, r: stage.at[i, k, r]
            to = lambda k: landed.at[i, k]
            stage[i, 0] = piece(zo).astype(BF)
            self.r1 = send(at(0, top), to(0), rs_send.at[i, 0], rs_recv.at[i, 0], (s, zr))
            self.l1 = send(at(0, low), to(1), rs_send.at[i, 1], rs_recv.at[i, 1], (s, zl))
            right = piece(zr)
            stage[i, 1, half:] = right[half:].astype(BF)
            self.r2 = send(at(1, low), to(2), rs_send.at[i, 2], rs_recv.at[i, 2], (s, zr))
            part[0] = right[:half]
            left = piece(zl)
            stage[i, 2, :half] = left[:half].astype(BF)
            self.l2 = send(at(2, top), to(3), rs_send.at[i, 3], rs_recv.at[i, 3], (s, zl))
            part[1] = left[half:]
            own = piece(z)
            part[2] = own[:half]
            part[3] = own[half:]

        def pass_on(self):
            i = self.i
            self.r1.wait_recv()
            stage[i, 1, :half] = (part[0] + landed[i, 0].astype(F32)).astype(BF)
            self.rf = send(stage.at[i, 1, top], landed.at[i, 4], rs_send.at[i, 4], rs_recv.at[i, 4], (s, zr))
            self.l1.wait_recv()
            stage[i, 2, half:] = (part[1] + landed[i, 1].astype(F32)).astype(BF)
            self.lf = send(stage.at[i, 2, low], landed.at[i, 5], rs_send.at[i, 5], rs_recv.at[i, 5], (s, zl))

        def finish(self):
            i = self.i
            for c in (self.r2, self.l2, self.rf, self.lf):
                c.wait_recv()
            upper = part[2] + landed[i, 4].astype(F32) + landed[i, 3].astype(F32)
            lower = part[3] + landed[i, 2].astype(F32) + landed[i, 5].astype(F32)
            return jnp.concatenate([upper, lower], axis=0)

    class Total:
        def __init__(self, i, sums):
            self.i = i
            stats[i, z] = jnp.broadcast_to(sums, (tokens, 128)).T[0:8]
            there = stats.at[i, z]
            self.got = [
                send(there, there, st_send.at[i, k], st_recv.at[i, k], (s, who))
                for k, who in enumerate((zr, zl, zo))
            ]

        def finish(self):
            for copy in self.got:
                copy.wait_recv()
            i = self.i
            total = stats[i, 0] + stats[i, 1] + stats[i, 2] + stats[i, 3]
            return as_column(total[0:1])

    def row_sum(value):
        return jnp.sum(value, axis=1, keepdims=True)

    def columns(at, j, size=SPAN):
        return pl.ds(at + j * size, size)

    def turn(left_index, k=None):
        if k is None:
            turned[...] = rows[left_index].T
        else:
            turned[...] = (rows[left_index].astype(F32) * scales[k][:, 0:1]).astype(BF).T

    def weight_grad(l, k, right_ref, lead, start, size, at):
        clear(k)
        piece = nn(turned[...], right_ref[lead, :, start : start + size]).astype(BF)
        gw_ref[:, :, :, :, at : at + size] = piece.reshape(4, 4, 2, 32, size)

    def norm_scale(k, total, h):
        scale = lax.rsqrt(total.finish() / width + EPS)
        scales[k] = jnp.broadcast_to(scale, (tokens, 128))
        normed[k] = h * scale
        return scale

    def norm_backward(k, dn, inner, gain, small_row):
        a = normed[k]
        small_ref[pl.ds(small_row, 1), :] = jnp.sum(dn * a, axis=0, keepdims=True)
        return scales[k][:, 0:1] * (dn * gain - a * (inner / width))

    small_ref[...] = jnp.zeros_like(small_ref)
    hidden = x_ref[...]
    cot_gather = None
    for l in range(layers):
        base = l * per
        at_exit, at_gate, at_down = base + 3 * ch, base + 4 * ch, base + 4 * ch + 2 * ff
        gather = Gather(2 * l, (hidden * gain_ref[l, 0:1]).astype(BF))
        total = Total(2 * l, row_sum(hidden * hidden))
        if l == 0:
            cot_gather = Gather(2 * layers + 2 * (layers - 1), cot_ref[...].astype(BF))
        tick()
        gather.pass_on()
        tick()
        gather.finish()
        if l == 0:
            cot_gather.pass_on()
        scale = norm_scale(2 * l, total, hidden)
        need(l, 0)
        full = rows[2 * l]
        bm = nn(full, weight(columns(base, 0, ch))) * scale
        xm = nn(full, weight(columns(base, 2, ch))) * scale
        bx = bm * xm
        ext[l, 8:] = bx
        tail = send(
            ext.at[l, pl.ds(tokens, 8)], ext.at[l, pl.ds(0, 8)], halo_send.at[l], halo_recv.at[l], (after, z)
        )
        bcx[l, 0] = bm
        bcx[l, 2] = xm
        cm = nn(full, weight(columns(base, 1, ch))) * scale
        bcx[l, 1] = cm
        tick()
        tail.wait_recv()
        head = ext[l, 0:8]
        ext[l, 0:8] = jnp.where(s > 0, head, jnp.zeros_like(head))
        k = kern_ref[l]
        zc = k[0:1] * ext[l, 6 : 6 + tokens] + k[1:2] * ext[l, 7 : 7 + tokens] + k[2:3] * ext[l, 8 : 8 + tokens]
        conv[l] = zc
        gated[l] = (cm * zc).astype(BF)

        def exit_piece(who, l=l, at=at_exit):
            return nt(gated[l], weight_rows(who, columns(at, 0, ch)))

        need(l, 1)
        scatter = Scatter(2 * l, exit_piece)
        tick()
        scatter.pass_on()
        tick()
        mid = hidden + scatter.finish()
        gather = Gather(2 * l + 1, (mid * gain_ref[l, 1:2]).astype(BF))
        total = Total(2 * l + 1, row_sum(mid * mid))
        tick()
        gather.pass_on()
        tick()
        gather.finish()
        scale = norm_scale(2 * l + 1, total, mid)
        need(l, 1)

        for j in range(ff // SPAN):
            need(l, 1 + j)
            both = nn(rows[2 * l + 1], weight(columns(at_gate, j, 2 * SPAN))) * scale
            gates[l, :, j * 2 * SPAN : (j + 1) * 2 * SPAN] = both
            g, up_value = both[:, :SPAN], both[:, SPAN:]
            acted[l, :, j * SPAN : (j + 1) * SPAN] = (g * jax.nn.sigmoid(g) * up_value).astype(BF)

        def down_piece(who, l=l, at=at_down):
            return nt(acted[l], weight_rows(who, columns(at, 0, ff)))

        need(l, 4)
        scatter = Scatter(2 * l + 1, down_piece)
        tick()
        scatter.pass_on()
        tick()
        hidden = mid + scatter.finish()
    out_ref[...] = hidden

    grad = cot_ref[...]
    for l in reversed(range(layers)):
        base = l * per
        at_exit, at_gate, at_down = base + 3 * ch, base + 4 * ch, base + 4 * ch + 2 * ff
        ie = 2 * layers + 2 * l
        if l == layers - 1:
            gather = cot_gather
        else:
            gather = Gather(ie, grad.astype(BF))
            tick()
            gather.pass_on()
            tick()
        gather.finish()

        inner = jnp.zeros((tokens, 1), F32)
        for j in range(ff // SPAN):
            ds = nn(rows[ie], weight(columns(at_down, j)))
            g = gates[l, :, j * 2 * SPAN : j * 2 * SPAN + SPAN]
            up_value = gates[l, :, j * 2 * SPAN + SPAN : (j + 1) * 2 * SPAN]
            sig = jax.nn.sigmoid(g)
            dg = (ds * up_value * sig * (1.0 + g * (1.0 - sig))).astype(BF)
            du = (ds * (g * sig)).astype(BF)
            dgates[0, :, j * 2 * SPAN : j * 2 * SPAN + SPAN] = dg
            dgates[0, :, j * 2 * SPAN + SPAN : (j + 1) * 2 * SPAN] = du
            inner += row_sum(dg.astype(F32) * g + du.astype(F32) * up_value)
        total = Total(2 * layers + 2 * l + 1, inner)

        def norm2_piece(who, at_gate=at_gate):
            return nt(dgates[0], weight_rows(who, columns(at_gate, 0, 2 * ff)))

        scatter = Scatter(2 * layers + 2 * l, norm2_piece)
        turn(ie)
        weight_grad(l, 4, acted, l, 0, ff, 4 * ch + 2 * ff)
        scatter.pass_on()
        ready(l, 4, 4 * ch + 2 * ff, ff)
        turn(2 * l + 1, 2 * l + 1)
        for j in range(ff // SPAN):
            weight_grad(l, 1 + j, dgates, 0, j * 2 * SPAN, 2 * SPAN, 4 * ch + j * 2 * SPAN)
            ready(l, 1 + j, 4 * ch + j * 2 * SPAN, 2 * SPAN)
        dn2 = scatter.finish()
        dmid = grad + norm_backward(2 * l + 1, dn2, total.finish(), gain_ref[l, 1:2], 3 * layers + 2 * l + 1)
        gather = Gather(ie + 1, dmid.astype(BF))
        tick()
        gather.pass_on()
        tick()
        gather.finish()
        dy = nn(rows[ie + 1], weight(columns(at_exit, 0, ch)))
        dz = dy * bcx[l, 1]
        dext[l, :tokens] = dz
        tail = send(
            dext.at[l, pl.ds(0, 8)],
            dext.at[l, pl.ds(tokens, 8)],
            halo_send.at[layers + l],
            halo_recv.at[layers + l],
            (before, z),
        )
        dproj[0, :, ch : 2 * ch] = (dy * conv[l]).astype(BF)
        for j in range(3):
            small_ref[pl.ds(3 * l + j, 1), :] = jnp.sum(dz * ext[l, 6 + j : 6 + j + tokens], axis=0, keepdims=True)
        turn(ie + 1)
        weight_grad(l, 5, gated, l, 0, ch, 3 * ch)
        ready(l, 5, 3 * ch, ch)
        tick()
        tail.wait_recv()
        last = dext[l, tokens:]
        dext[l, tokens:] = jnp.where(s < seqs - 1, last, jnp.zeros_like(last))
        k = kern_ref[l]
        dbx = k[2:3] * dext[l, 0:tokens] + k[1:2] * dext[l, 1 : 1 + tokens] + k[0:1] * dext[l, 2 : 2 + tokens]
        db = (dbx * bcx[l, 2]).astype(BF)
        dx = (dbx * bcx[l, 0]).astype(BF)
        dproj[0, :, :ch] = db
        dproj[0, :, 2 * ch :] = dx
        dc = dproj[0, :, ch : 2 * ch].astype(F32)
        inner = row_sum(db.astype(F32) * bcx[l, 0] + dc * bcx[l, 1] + dx.astype(F32) * bcx[l, 2])
        total = Total(2 * layers + 2 * l, inner)

        def norm1_piece(who, base=base):
            return nt(dproj[0], weight_rows(who, columns(base, 0, 3 * ch)))

        scatter = Scatter(2 * layers + 2 * l + 1, norm1_piece)
        turn(2 * l, 2 * l)
        weight_grad(l, 0, dproj, 0, 0, 3 * ch, 0)
        scatter.pass_on()
        ready(l, 0, 0, 3 * ch)
        tick()
        dn1 = scatter.finish()
        grad = dmid + norm_backward(2 * l, dn1, total.finish(), gain_ref[l, 0:1], 3 * layers + 2 * l)
    din_ref[...] = grad
    own = tally.at[0, 0]
    tally[0, 0] = small_ref[...]
    copy = send(own, tally.at[0, 1], t_send.at[0], t_recv.at[0], pair)
    tick()
    copy.wait_recv()
    tally[1, x] = tally[0, 0] + tally[0, 1]
    stages = ((1, x, lambda k: (lax.rem(x + k, 4) * 8 + y * 2 + c, z)), (2, y, lambda k: (x * 8 + lax.rem(y + k, 4) * 2 + c, z)))
    for n, here, where in stages:
        slot = tally.at[n, here]
        copies = [send(slot, slot, t_send.at[3 * n - 3 + k], t_recv.at[3 * n - 3 + k], where(k)) for k in (1, 2, 3)]
        tick()
        for copy in copies:
            copy.wait_recv()
        total = tally[n, 0] + tally[n, 1] + tally[n, 2] + tally[n, 3]
        if n == 1:
            tally[2, y] = total
        else:
            small_ref[...] = total
    while any(total.stage < 6 for total in sums):
        tick()
    for copy in pending:
        copy.wait_send()


def run_step(x, cot, weights, kern, gain, seqs):
    layers, taps, ch = kern.shape
    tokens = x.shape[0]
    width = 4 * ch
    ff = weights[2].shape[3]
    per = 4 * ch + 3 * ff
    n = 4 * layers
    vmem = pl.BlockSpec(memory_space=pltpu.VMEM)
    dma = pltpu.SemaphoreType.DMA
    return pl.pallas_call(
        functools.partial(step_kernel, (layers, seqs, tokens, ch, ff)),
        out_shape=(
            jax.ShapeDtypeStruct((tokens, ch), F32),
            jax.ShapeDtypeStruct((tokens, ch), F32),
            jax.ShapeDtypeStruct((32, layers * per), F32),
            jax.ShapeDtypeStruct((16, ch), F32),
        ),
        in_specs=[vmem] * 8,
        out_specs=(vmem,) * 4,
        scratch_shapes=[
            pltpu.VMEM((n, tokens, width), BF),
            pltpu.VMEM((4, tokens // 2, ch), F32),
            pltpu.VMEM((n, 3, tokens, ch), BF),
            pltpu.VMEM((n, 6, tokens // 2, ch), BF),
            pltpu.VMEM((n, 4, 8, tokens), F32),
            pltpu.VMEM((2 * layers, tokens, ch), F32),
            pltpu.VMEM((2 * layers, tokens, 128), F32),
            pltpu.VMEM((layers, tokens + 8, ch), F32),
            pltpu.VMEM((layers, tokens + 8, ch), F32),
            pltpu.VMEM((layers, 3, tokens, ch), F32),
            pltpu.VMEM((layers, tokens, ch), F32),
            pltpu.VMEM((layers, tokens, ch), BF),
            pltpu.VMEM((layers, tokens, 2 * ff), F32),
            pltpu.VMEM((layers, tokens, ff), BF),
            pltpu.VMEM((1, tokens, 2 * ff), BF),
            pltpu.VMEM((1, tokens, 3 * ch), BF),
            pltpu.VMEM((width, tokens), BF),
            pltpu.VMEM((4, 4, 2, 32, layers * per), BF),
            pltpu.VMEM((4, 4, 2, 32, per), BF),
            pltpu.VMEM((4, 4, 32, per), BF),
            pltpu.VMEM((6, 2, 32, per), BF),
            pltpu.VMEM((6, 16, per), BF),
            pltpu.VMEM((3, 4, 16, ch), F32),
            dma((n, 6)),
            dma((n, 6)),
            dma((n, 6)),
            dma((n, 6)),
            dma((n, 3)),
            dma((n, 3)),
            dma((2 * layers,)),
            dma((2 * layers,)),
            dma((5 * layers, 12)),
            dma((5 * layers, 12)),
            dma((layers, 6, 13)),
            dma((layers, 6, 13)),
            dma((7,)),
            dma((7,)),
            pltpu.SemaphoreType.REGULAR((6, 3)),
        ],
        compiler_params=pltpu.CompilerParams(
            collective_id=0, has_side_effects=True, vmem_limit_bytes=67043328
        ),
        name="layers",
    )(x, cot, *weights, kern, gain)


def adamw(weight, grad, first, second, rate, decay):
    first_new = 0.9 * first + 0.1 * grad
    second_new = 0.999 * second + 0.001 * grad * grad
    update = first_new / (1.0 - 0.9**STEP) / (jnp.sqrt(second_new / (1.0 - 0.999**STEP)) + 1e-08)
    return (weight - rate * (update + decay * weight), first_new, second_new)


def taken_apart(flat, layers, ch, ff):
    per = 4 * ch + 3 * ff
    entry, leave, gates, down = [], [], [], []
    for l in range(layers):
        b = l * per
        entry.append(jnp.stack([flat[:, b + c * ch : b + (c + 1) * ch] for c in range(3)]))
        leave.append(flat[:, b + 3 * ch : b + 4 * ch].T)
        g = b + 4 * ch
        halves = [
            jnp.concatenate([flat[:, g + 2 * j + k : g + 2 * j + k + SPAN] for j in range(0, ff, SPAN)], axis=1)
            for k in (0, SPAN)
        ]
        gates.append(jnp.stack(halves))
        down.append(flat[:, g + 2 * ff : g + 3 * ff].T)
    return tuple(jnp.stack(v) for v in (entry, leave, gates, down))


def per_device(
    inputs,
    cotangent,
    entry_weight,
    exit_weight,
    gate_up,
    down_weight,
    conv_kernel,
    norm_gain,
    entry_first,
    entry_second,
    exit_first,
    exit_second,
    gate_first,
    gate_second,
    down_first,
    down_second,
    kernel_first,
    kernel_second,
    gain_first,
    gain_second,
):
    layers, _, _, ch = entry_weight.shape
    ff = gate_up.shape[3]
    seqs = lax.axis_size("seq")
    weights = (entry_weight, jnp.swapaxes(exit_weight, 1, 2), gate_up, jnp.swapaxes(down_weight, 1, 2))
    hidden, grad, summed, small = run_step(inputs, cotangent, weights, conv_kernel, norm_gain, seqs)
    entry_grad, exit_grad, gate_grad, down_grad = taken_apart(summed, layers, ch, ff)
    kernel_grad = small[: 3 * layers].reshape(layers, 3, ch)
    gain_grad = small[3 * layers : 5 * layers].reshape(layers, 2, ch)
    entry_u, entry_f, entry_s = adamw(entry_weight, entry_grad, entry_first, entry_second, 0.01, 0.1)
    exit_u, exit_f, exit_s = adamw(exit_weight, exit_grad, exit_first, exit_second, 0.01, 0.1)
    gate_u, gate_f, gate_s = adamw(gate_up, gate_grad, gate_first, gate_second, 0.01, 0.1)
    down_u, down_f, down_s = adamw(down_weight, down_grad, down_first, down_second, 0.01, 0.1)
    kernel_u, kernel_f, kernel_s = adamw(conv_kernel, kernel_grad, kernel_first, kernel_second, 0.2, 0.0)
    gain_u, gain_f, gain_s = adamw(norm_gain, gain_grad, gain_first, gain_second, 0.2, 0.0)
    return (
        hidden,
        grad,
        entry_grad,
        exit_grad,
        gate_grad,
        down_grad,
        kernel_grad,
        gain_grad,
        entry_u,
        exit_u,
        gate_u,
        down_u,
        kernel_u,
        gain_u,
        entry_f,
        entry_s,
        exit_f,
        exit_s,
        gate_f,
        gate_s,
        down_f,
        down_s,
        kernel_f,
        kernel_s,
        gain_f,
        gain_s,
    )


def solution(mesh):
    tokens, rows, columns, replicated = (
        P("seq", "tp"),
        P(None, None, "seq", "tp"),
        P(None, "tp", "seq"),
        P(None, None, "tp"),
    )
    matrices = (rows, columns, rows, columns)
    moments = (rows, rows, columns, columns, rows, rows, columns, columns)
    return jax.shard_map(
        per_device,
        mesh=mesh,
        in_specs=(tokens, tokens, *matrices, replicated, replicated, *moments, *([replicated] * 4)),
        out_specs=(
            tokens,
            tokens,
            *matrices,
            replicated,
            replicated,
            *matrices,
            replicated,
            replicated,
            *moments,
            *([replicated] * 4),
        ),
        check_vma=False,
    )
```

```python
import functools

import jax
import jax.numpy as jnp
from jax import lax
from jax.experimental import pallas as pl
from jax.experimental.pallas import tpu as pltpu
from jax.sharding import PartitionSpec as P

STEP = 4
EPS = 1e-06
MESH = pl.DeviceIdType.MESH
BF = jnp.bfloat16
F32 = jnp.float32
SPAN = 384
PACE = (-2, 0, 1, 3, 5, 6)


def nn(a, b):
    return lax.dot_general(a, b, (((1,), (0,)), ((), ())), preferred_element_type=F32)


def nt(a, b):
    return lax.dot_general(a, b, (((1,), (1,)), ((), ())), preferred_element_type=F32)


def as_column(row):
    return jnp.broadcast_to(row, (128, row.shape[1])).T[:, 0:1]


def step_kernel(
    cfg,
    x_ref,
    cot_ref,
    entry_ref,
    exit_ref,
    gate_ref,
    down_ref,
    kern_ref,
    gain_ref,
    out_ref,
    din_ref,
    final_ref,
    small_ref,
    rows,
    part,
    stage,
    landed,
    stats,
    normed,
    scales,
    ext,
    dext,
    bcx,
    conv,
    gated,
    gates,
    acted,
    dgates,
    dproj,
    turned,
    w_ref,
    gw_ref,
    from_pair,
    from_far,
    from_near,
    tally,
    ag_send,
    ag_recv,
    rs_send,
    rs_recv,
    st_send,
    st_recv,
    halo_send,
    halo_recv,
    w_send,
    w_recv,
    g_send,
    g_recv,
    t_send,
    t_recv,
    credit,
):
    layers, seqs, tokens, ch, ff = cfg
    half = tokens // 2
    width = 4 * ch
    per = 4 * ch + 3 * ff
    z = lax.axis_index("tp")
    s = lax.axis_index("seq")
    zr, zl, zo = lax.rem(z + 1, 4), lax.rem(z + 3, 4), lax.rem(z + 2, 4)
    after, before = lax.rem(s + 1, seqs), lax.rem(s + seqs - 1, seqs)

    c = lax.rem(s, 2)
    x, y = lax.div(s, 8), lax.rem(lax.div(s, 2), 4)
    u, v = x * (1 - c) + y * c, y * (1 - c) + x * c

    def place(uu, vv):
        return uu * (1 - c) + vv * c, vv * (1 - c) + uu * c

    def device(uu, vv):
        px, py = place(uu, vv)
        return (px * 8 + py * 2 + c, z)

    up, un, uo = lax.rem(u + 3, 4), lax.rem(u + 1, 4), lax.rem(u + 2, 4)
    vp, vn, vo = lax.rem(v + 3, 4), lax.rem(v + 1, 4), lax.rem(v + 2, 4)
    u_next, u_prev, v_next, v_prev = device(un, v), device(up, v), device(u, vn), device(u, vp)
    pair = (s + 1 - 2 * c, z)

    barrier = pltpu.get_barrier_semaphore()
    partners = [(s, zr), (s, zl), (s, zo), (after, z), (before, z), u_next, u_prev, v_next, v_prev, pair]
    partners += [device(uo, v), device(u, vo)]
    for where in partners:
        pl.semaphore_signal(barrier, inc=1, device_id=where, device_id_type=MESH)
    pl.semaphore_wait(barrier, len(partners))

    pending = []

    def send(src, dst, ssem, rsem, where):
        copy = pltpu.make_async_remote_copy(
            src_ref=src, dst_ref=dst, send_sem=ssem, recv_sem=rsem, device_id=where, device_id_type=MESH
        )
        copy.start()
        pending.append(copy)
        return copy

    def cols(who):
        return pl.ds(pl.multiple_of(who * ch, ch), ch)

    def own_rows(who):
        return pl.ds(pl.multiple_of(who * ch, ch), ch)

    top, low = pl.ds(0, half), pl.ds(half, half)

    def chunk_of(ref, lead, vv, lo, hi, where):
        if lead == 0:
            return ref.at[pl.ds(lo, hi - lo), vv, 0, :, where]
        return ref.at[vv, pl.ds(lo, hi - lo), 1, :, where]

    def send_either(make, ssem, rsem, where, held=pending):
        for core in (0, 1):

            @pl.when(c == core)
            def _(core=core):
                src, dst = make(core)
                pltpu.make_async_remote_copy(
                    src_ref=src, dst_ref=dst, send_sem=ssem, recv_sem=rsem, device_id=where, device_id_type=MESH
                ).start()

        src, dst = make(0)
        copy = pltpu.make_async_remote_copy(
            src_ref=src, dst_ref=dst, send_sem=ssem, recv_sem=rsem, device_id=where, device_id_type=MESH
        )
        held.append(copy)
        return copy

    spans = []
    for l in range(layers):
        at = l * per
        for size in (3 * ch, ch + 2 * SPAN, 2 * SPAN, 2 * SPAN, ff):
            spans.append(pl.ds(at, size))
            at += size

    def pack(k):
        l, part_index = k // 5, k % 5
        at = l * per

        def put(start, value):
            w_ref[x, y, c, :, start : start + value.shape[1]] = value.astype(BF)

        if part_index == 0:
            for j in range(3):
                put(at + (0, 2, 1)[j] * ch, entry_ref[l, j])
        elif part_index == 4:
            put(at + 4 * ch + 2 * ff, down_ref[l])
        else:
            if part_index == 1:
                put(at + 3 * ch, exit_ref[l])
            j = part_index - 1
            for half_index in range(2):
                put(
                    at + 4 * ch + (2 * j + half_index) * SPAN,
                    gate_ref[l, half_index, :, j * SPAN : (j + 1) * SPAN],
                )

    class Weights:
        def __init__(self, k):
            self.k, self.where, self.stage = k, spans[k], 0

        def block(self, uu, vv, r=slice(None)):
            px, py = place(uu, vv)
            return w_ref.at[px, py, c, r, self.where]

        def move(self, ref, n, where):
            return send(ref, ref, w_send.at[self.k, n], w_recv.at[self.k, n], where)

        def move_row(self, vv, lo, hi, n, where):
            def make(core):
                ref = chunk_of(w_ref, core, vv, lo, hi, self.where)
                return ref, ref

            return send_either(make, w_send.at[self.k, n], w_recv.at[self.k, n], where)

        def step(self):
            stage, self.stage = self.stage, self.stage + 1
            if stage == 0:
                pack(self.k)
                self.a0 = self.move(self.block(u, v), 0, u_next)
                self.a1 = self.move(self.block(u, v), 1, u_prev)
            elif stage == 1:
                self.a0.wait_recv()
                self.a2 = self.move(self.block(up, v, pl.ds(0, 16)), 2, u_next)
                self.a1.wait_recv()
                self.a3 = self.move(self.block(un, v, pl.ds(16, 16)), 3, u_prev)
            elif stage == 2:
                self.a2.wait_recv()
                self.a3.wait_recv()
                self.b0 = self.move_row(v, 0, 4, 4, v_next)
                self.b1 = self.move_row(v, 0, 4, 5, v_prev)
                self.p0 = self.move_row(v, 0, 4, 8, pair)
            elif stage == 3:
                self.b0.wait_recv()
                self.b2 = self.move_row(vp, 0, 2, 6, v_next)
                self.b1.wait_recv()
                self.b3 = self.move_row(vn, 2, 4, 7, v_prev)
                self.p1 = self.move_row(vp, 0, 4, 9, pair)
                self.p2 = self.move_row(vn, 0, 4, 10, pair)
            elif stage == 4:
                self.b2.wait_recv()
                self.b3.wait_recv()
                self.p3 = self.move_row(vo, 0, 4, 11, pair)
            else:
                for copy in (self.p0, self.p1, self.p2, self.p3):
                    copy.wait_recv()

    class Sums:
        def __init__(self, l, k, where):
            self.l, self.k, self.where, self.stage = l, k, where, 0
            self.total = pl.ds(l * per + where.start, where.size)
            self.first = l == layers - 1
            self.sent = []

        def send(self, src, dst, n, where):
            copy = pltpu.make_async_remote_copy(
                src_ref=src,
                dst_ref=dst,
                send_sem=g_send.at[self.l, self.k, n],
                recv_sem=g_recv.at[self.l, self.k, n],
                device_id=where,
                device_id_type=MESH,
            )
            copy.start()
            self.sent.append(copy)
            return copy

        def far(self, vv, lo, n, where):
            def make(core):
                return chunk_of(gw_ref, core, vv, lo, lo + 2, self.where), from_far.at[n - 1, :, :, self.where]

            copy = send_either(make, g_send.at[self.l, self.k, n], g_recv.at[self.l, self.k, n], where, self.sent)
            return copy

        def near(self, uu, r, n, where):
            px, py = place(uu, v)
            return self.send(gw_ref.at[px, py, c, r, self.where], from_near.at[n - 7, :, self.where], n, where)

        def add_far(self, vv, lo, slots):
            for i in range(2):
                px, py = place(lo + i, vv)
                value = gw_ref[px, py, c, :, self.where].astype(F32)
                for slot in slots:
                    value += from_far[slot, i, :, self.where].astype(F32)
                gw_ref[px, py, c, :, self.where] = value.astype(BF)

        def add_near(self, uu, r, slots):
            px, py = place(uu, v)
            value = gw_ref[px, py, c, r, self.where].astype(F32)
            for slot in slots:
                value += from_near[slot, :, self.where].astype(F32)
            return value

        def allow(self, kind, devices):
            if self.first:
                for where in devices:
                    pl.semaphore_signal(credit.at[self.k, kind], inc=1, device_id=where, device_id_type=MESH)

        def ask(self, kind, count):
            if not self.first:
                pl.semaphore_wait(credit.at[self.k, kind], count)

        def step(self):
            stage, self.stage = self.stage, self.stage + 1
            upper, lower = pl.ds(0, 16), pl.ds(16, 16)
            if stage == 0:
                self.ask(0, 1)
                self.q = self.send(
                    gw_ref.at[:, :, 1 - c, :, self.where], from_pair.at[:, :, :, self.where], 0, pair
                )
            elif stage == 1:
                self.q.wait_recv()

                @pl.loop(0, 4)
                def _(i):
                    gw_ref[i, :, c, :, self.where] = (
                        gw_ref[i, :, c, :, self.where].astype(F32) + from_pair[i, :, :, self.where].astype(F32)
                    ).astype(BF)

                self.allow(0, [pair])
                self.ask(1, 2)
                self.f0 = self.far(vo, 0, 1, v_next)
                self.f1 = self.far(vo, 2, 2, v_prev)
                self.f2 = self.far(vn, 2, 3, v_next)
                self.f3 = self.far(vp, 0, 4, v_prev)
            elif stage == 2:
                self.f0.wait_recv()
                self.add_far(vn, 0, [0])
                self.f4 = self.far(vn, 0, 5, v_next)
                self.f1.wait_recv()
                self.add_far(vp, 2, [1])
                self.f5 = self.far(vp, 2, 6, v_prev)
            elif stage == 3:
                for copy in (self.f2, self.f3, self.f4, self.f5):
                    copy.wait_recv()
                self.add_far(v, 0, [3, 4])
                self.add_far(v, 2, [2, 5])
                self.allow(1, [v_next, v_prev])
                self.ask(2, 2)
                self.n0 = self.near(uo, upper, 7, u_next)
                self.n1 = self.near(uo, lower, 8, u_prev)
                self.n2 = self.near(un, lower, 9, u_next)
                self.n3 = self.near(up, upper, 10, u_prev)
            elif stage == 4:
                self.n0.wait_recv()
                px, py = place(un, v)
                gw_ref[px, py, c, upper, self.where] = self.add_near(un, upper, [0]).astype(BF)
                self.n4 = self.near(un, upper, 11, u_next)
                self.n1.wait_recv()
                px, py = place(up, v)
                gw_ref[px, py, c, lower, self.where] = self.add_near(up, lower, [1]).astype(BF)
                self.n5 = self.near(up, lower, 12, u_prev)
            else:
                for copy in (self.n2, self.n3, self.n4, self.n5):
                    copy.wait_recv()
                final_ref[0:16, self.total] = self.add_near(u, upper, [3, 4])
                final_ref[16:32, self.total] = self.add_near(u, lower, [2, 5])
                self.allow(2, [u_next, u_prev])
                for copy in self.sent:
                    copy.wait_send()

    fetches = [Weights(k) for k in range(len(spans))]
    fetched = [0]
    sums = []

    def tick():
        t = fetched[0]
        fetched[0] += 1
        for k, fetch in enumerate(fetches):
            if fetch.stage == 0 and t >= k + PACE[0]:
                fetch.step()
        for k, fetch in enumerate(fetches):
            if 0 < fetch.stage < 6 and t >= k + PACE[fetch.stage]:
                fetch.step()
        for total in sums:
            if total.stage < 6:
                total.step()

    def need(l, part_index):
        fetch = fetches[5 * l + part_index]
        while fetch.stage < 6:
            fetch.step()

    def ready(l, k, at, size):
        total = Sums(l, k, pl.ds(at, size))
        total.step()
        sums.append(total)

    def clear(k):
        for total in sums:
            if total.k == k:
                while total.stage < 6:
                    tick()

    def weight(where):
        return w_ref[:, :, :, :, where].reshape(width, where.size)

    def weight_rows(who, where):
        return w_ref[who, :, :, :, where].reshape(ch, where.size)

    tick()

    class Gather:
        def __init__(self, i, block):
            self.i = i
            rows[i, :, cols(z)] = block
            mine = lambda r: rows.at[i, r, cols(z)]
            self.r1 = send(mine(top), mine(top), ag_send.at[i, 0], ag_recv.at[i, 0], (s, zr))
            self.l1 = send(mine(low), mine(low), ag_send.at[i, 1], ag_recv.at[i, 1], (s, zl))
            self.r2 = send(mine(low), mine(low), ag_send.at[i, 2], ag_recv.at[i, 2], (s, zr))
            self.l2 = send(mine(top), mine(top), ag_send.at[i, 3], ag_recv.at[i, 3], (s, zl))

        def pass_on(self):
            i = self.i
            self.r1.wait_recv()
            b = rows.at[i, top, cols(zl)]
            self.rf = send(b, b, ag_send.at[i, 4], ag_recv.at[i, 4], (s, zr))
            self.l1.wait_recv()
            b = rows.at[i, low, cols(zr)]
            self.lf = send(b, b, ag_send.at[i, 5], ag_recv.at[i, 5], (s, zl))

        def finish(self):
            for c in (self.r2, self.l2, self.rf, self.lf):
                c.wait_recv()

    class Scatter:
        def __init__(self, i, piece):
            self.i = i
            at = lambda k, r: stage.at[i, k, r]
            to = lambda k: landed.at[i, k]
            stage[i, 0] = piece(zo).astype(BF)
            self.r1 = send(at(0, top), to(0), rs_send.at[i, 0], rs_recv.at[i, 0], (s, zr))
            self.l1 = send(at(0, low), to(1), rs_send.at[i, 1], rs_recv.at[i, 1], (s, zl))
            right = piece(zr)
            stage[i, 1, half:] = right[half:].astype(BF)
            self.r2 = send(at(1, low), to(2), rs_send.at[i, 2], rs_recv.at[i, 2], (s, zr))
            part[0] = right[:half]
            left = piece(zl)
            stage[i, 2, :half] = left[:half].astype(BF)
            self.l2 = send(at(2, top), to(3), rs_send.at[i, 3], rs_recv.at[i, 3], (s, zl))
            part[1] = left[half:]
            own = piece(z)
            part[2] = own[:half]
            part[3] = own[half:]

        def pass_on(self):
            i = self.i
            self.r1.wait_recv()
            stage[i, 1, :half] = (part[0] + landed[i, 0].astype(F32)).astype(BF)
            self.rf = send(stage.at[i, 1, top], landed.at[i, 4], rs_send.at[i, 4], rs_recv.at[i, 4], (s, zr))
            self.l1.wait_recv()
            stage[i, 2, half:] = (part[1] + landed[i, 1].astype(F32)).astype(BF)
            self.lf = send(stage.at[i, 2, low], landed.at[i, 5], rs_send.at[i, 5], rs_recv.at[i, 5], (s, zl))

        def finish(self):
            i = self.i
            for c in (self.r2, self.l2, self.rf, self.lf):
                c.wait_recv()
            upper = part[2] + landed[i, 4].astype(F32) + landed[i, 3].astype(F32)
            lower = part[3] + landed[i, 2].astype(F32) + landed[i, 5].astype(F32)
            return jnp.concatenate([upper, lower], axis=0)

    class Total:
        def __init__(self, i, sums):
            self.i = i
            stats[i, z] = jnp.broadcast_to(sums, (tokens, 128)).T[0:8]
            there = stats.at[i, z]
            self.got = [
                send(there, there, st_send.at[i, k], st_recv.at[i, k], (s, who))
                for k, who in enumerate((zr, zl, zo))
            ]

        def finish(self):
            for copy in self.got:
                copy.wait_recv()
            i = self.i
            total = stats[i, 0] + stats[i, 1] + stats[i, 2] + stats[i, 3]
            return as_column(total[0:1])

    def row_sum(value):
        return jnp.sum(value, axis=1, keepdims=True)

    def columns(at, j, size=SPAN):
        return pl.ds(at + j * size, size)

    def turn(left_index, k=None):
        if k is None:
            turned[...] = rows[left_index].T
        else:
            turned[...] = (rows[left_index].astype(F32) * scales[k][:, 0:1]).astype(BF).T

    def weight_grad(l, k, right_ref, lead, start, size, at):
        clear(k)
        piece = nn(turned[...], right_ref[lead, :, start : start + size]).astype(BF)
        gw_ref[:, :, :, :, at : at + size] = piece.reshape(4, 4, 2, 32, size)

    def norm_scale(k, total, h):
        scale = lax.rsqrt(total.finish() / width + EPS)
        scales[k] = jnp.broadcast_to(scale, (tokens, 128))
        normed[k] = h * scale
        return scale

    def norm_backward(k, dn, inner, gain, small_row):
        a = normed[k]
        small_ref[pl.ds(small_row, 1), :] = jnp.sum(dn * a, axis=0, keepdims=True)
        return scales[k][:, 0:1] * (dn * gain - a * (inner / width))

    small_ref[...] = jnp.zeros_like(small_ref)
    hidden = x_ref[...]
    cot_gather = None
    for l in range(layers):
        base = l * per
        at_exit, at_gate, at_down = base + 3 * ch, base + 4 * ch, base + 4 * ch + 2 * ff
        gather = Gather(2 * l, (hidden * gain_ref[l, 0:1]).astype(BF))
        total = Total(2 * l, row_sum(hidden * hidden))
        if l == 0:
            cot_gather = Gather(2 * layers + 2 * (layers - 1), cot_ref[...].astype(BF))
        tick()
        gather.pass_on()
        tick()
        gather.finish()
        if l == 0:
            cot_gather.pass_on()
        scale = norm_scale(2 * l, total, hidden)
        need(l, 0)
        full = rows[2 * l]
        bm = nn(full, weight(columns(base, 0, ch))) * scale
        xm = nn(full, weight(columns(base, 1, ch))) * scale
        bx = bm * xm
        ext[l, 8:] = bx
        tail = send(
            ext.at[l, pl.ds(tokens, 8)], ext.at[l, pl.ds(0, 8)], halo_send.at[l], halo_recv.at[l], (after, z)
        )
        bcx[l, 0] = bm
        bcx[l, 2] = xm
        tick()
        cm = nn(full, weight(columns(base, 2, ch))) * scale
        bcx[l, 1] = cm
        tick()
        tail.wait_recv()
        head = ext[l, 0:8]
        ext[l, 0:8] = jnp.where(s > 0, head, jnp.zeros_like(head))
        k = kern_ref[l]
        zc = k[0:1] * ext[l, 6 : 6 + tokens] + k[1:2] * ext[l, 7 : 7 + tokens] + k[2:3] * ext[l, 8 : 8 + tokens]
        conv[l] = zc
        gated[l] = (cm * zc).astype(BF)

        def exit_piece(who, l=l, at=at_exit):
            return nt(gated[l], weight_rows(who, columns(at, 0, ch)))

        need(l, 1)
        scatter = Scatter(2 * l, exit_piece)
        tick()
        scatter.pass_on()
        tick()
        mid = hidden + scatter.finish()
        gather = Gather(2 * l + 1, (mid * gain_ref[l, 1:2]).astype(BF))
        total = Total(2 * l + 1, row_sum(mid * mid))
        tick()
        gather.pass_on()
        tick()
        gather.finish()
        scale = norm_scale(2 * l + 1, total, mid)
        need(l, 1)

        for j in range(ff // SPAN):
            need(l, 1 + j)
            tick()
            both = nn(rows[2 * l + 1], weight(columns(at_gate, j, 2 * SPAN))) * scale
            gates[l, :, j * 2 * SPAN : (j + 1) * 2 * SPAN] = both
            g, up_value = both[:, :SPAN], both[:, SPAN:]
            acted[l, :, j * SPAN : (j + 1) * SPAN] = (g * jax.nn.sigmoid(g) * up_value).astype(BF)

        def down_piece(who, l=l, at=at_down):
            return nt(acted[l], weight_rows(who, columns(at, 0, ff)))

        need(l, 4)
        scatter = Scatter(2 * l + 1, down_piece)
        tick()
        scatter.pass_on()
        tick()
        hidden = mid + scatter.finish()
    out_ref[...] = hidden

    grad = cot_ref[...]
    for l in reversed(range(layers)):
        base = l * per
        at_exit, at_gate, at_down = base + 3 * ch, base + 4 * ch, base + 4 * ch + 2 * ff
        ie = 2 * layers + 2 * l
        if l == layers - 1:
            gather = cot_gather
        else:
            gather = Gather(ie, grad.astype(BF))
            tick()
            gather.pass_on()
            tick()
        gather.finish()

        inner = jnp.zeros((tokens, 1), F32)
        for j in range(ff // SPAN):
            ds = nn(rows[ie], weight(columns(at_down, j)))
            g = gates[l, :, j * 2 * SPAN : j * 2 * SPAN + SPAN]
            up_value = gates[l, :, j * 2 * SPAN + SPAN : (j + 1) * 2 * SPAN]
            sig = jax.nn.sigmoid(g)
            dg = (ds * up_value * sig * (1.0 + g * (1.0 - sig))).astype(BF)
            du = (ds * (g * sig)).astype(BF)
            dgates[0, :, j * 2 * SPAN : j * 2 * SPAN + SPAN] = dg
            dgates[0, :, j * 2 * SPAN + SPAN : (j + 1) * 2 * SPAN] = du
            inner += row_sum(dg.astype(F32) * g + du.astype(F32) * up_value)
        total = Total(2 * layers + 2 * l + 1, inner)

        def norm2_piece(who, at_gate=at_gate):
            return nt(dgates[0], weight_rows(who, columns(at_gate, 0, 2 * ff)))

        scatter = Scatter(2 * layers + 2 * l, norm2_piece)
        turn(ie)
        weight_grad(l, 4, acted, l, 0, ff, 4 * ch + 2 * ff)
        scatter.pass_on()
        ready(l, 4, 4 * ch + 2 * ff, ff)
        turn(2 * l + 1, 2 * l + 1)
        for j in range(ff // SPAN):
            weight_grad(l, 1 + j, dgates, 0, j * 2 * SPAN, 2 * SPAN, 4 * ch + j * 2 * SPAN)
            ready(l, 1 + j, 4 * ch + j * 2 * SPAN, 2 * SPAN)
        dn2 = scatter.finish()
        dmid = grad + norm_backward(2 * l + 1, dn2, total.finish(), gain_ref[l, 1:2], 3 * layers + 2 * l + 1)
        gather = Gather(ie + 1, dmid.astype(BF))
        tick()
        gather.pass_on()
        tick()
        gather.finish()
        dy = nn(rows[ie + 1], weight(columns(at_exit, 0, ch)))
        dz = dy * bcx[l, 1]
        dext[l, :tokens] = dz
        tail = send(
            dext.at[l, pl.ds(0, 8)],
            dext.at[l, pl.ds(tokens, 8)],
            halo_send.at[layers + l],
            halo_recv.at[layers + l],
            (before, z),
        )
        dproj[0, :, 2 * ch :] = (dy * conv[l]).astype(BF)
        for j in range(3):
            small_ref[pl.ds(j * layers + l, 1), :] = jnp.sum(dz * ext[l, 6 + j : 6 + j + tokens], axis=0, keepdims=True)
        turn(ie + 1)
        weight_grad(l, 5, gated, l, 0, ch, 3 * ch)
        turn(2 * l, 2 * l)
        weight_grad(l, 5, dproj, 0, 2 * ch, ch, 2 * ch)
        ready(l, 5, 2 * ch, 2 * ch)
        tick()
        tail.wait_recv()
        last = dext[l, tokens:]
        dext[l, tokens:] = jnp.where(s < seqs - 1, last, jnp.zeros_like(last))
        k = kern_ref[l]
        dbx = k[2:3] * dext[l, 0:tokens] + k[1:2] * dext[l, 1 : 1 + tokens] + k[0:1] * dext[l, 2 : 2 + tokens]
        db = (dbx * bcx[l, 2]).astype(BF)
        dx = (dbx * bcx[l, 0]).astype(BF)
        dproj[0, :, :ch] = db
        dproj[0, :, ch : 2 * ch] = dx
        dc = dproj[0, :, 2 * ch :].astype(F32)
        inner = row_sum(db.astype(F32) * bcx[l, 0] + dc * bcx[l, 1] + dx.astype(F32) * bcx[l, 2])
        total = Total(2 * layers + 2 * l, inner)

        def norm1_piece(who, base=base):
            return nt(dproj[0], weight_rows(who, columns(base, 0, 3 * ch)))

        if l == 0:
            weight_grad(l, 0, dproj, 0, 0, 2 * ch, 0)
            ready(l, 0, 0, 2 * ch)
        scatter = Scatter(2 * layers + 2 * l + 1, norm1_piece)
        if l > 0:
            weight_grad(l, 0, dproj, 0, 0, 2 * ch, 0)
            ready(l, 0, 0, 2 * ch)
        tick()
        scatter.pass_on()
        tick()
        dn1 = scatter.finish()
        grad = dmid + norm_backward(2 * l, dn1, total.finish(), gain_ref[l, 0:1], 3 * layers + 2 * l)
    din_ref[...] = grad
    own = tally.at[0, 0]
    tally[0, 0] = small_ref[...]
    copy = send(own, tally.at[0, 1], t_send.at[0], t_recv.at[0], pair)
    tick()
    copy.wait_recv()
    tally[1, x] = tally[0, 0] + tally[0, 1]
    stages = ((1, x, lambda k: (lax.rem(x + k, 4) * 8 + y * 2 + c, z)), (2, y, lambda k: (x * 8 + lax.rem(y + k, 4) * 2 + c, z)))
    for n, here, where in stages:
        slot = tally.at[n, here]
        copies = [send(slot, slot, t_send.at[3 * n - 3 + k], t_recv.at[3 * n - 3 + k], where(k)) for k in (1, 2, 3)]
        tick()
        for copy in copies:
            copy.wait_recv()
        total = tally[n, 0] + tally[n, 1] + tally[n, 2] + tally[n, 3]
        if n == 1:
            tally[2, y] = total
        else:
            small_ref[...] = total
    while any(total.stage < 6 for total in sums):
        tick()
    for copy in pending:
        copy.wait_send()


def run_step(x, cot, weights, kern, gain, seqs):
    layers, taps, ch = kern.shape
    tokens = x.shape[0]
    width = 4 * ch
    ff = weights[2].shape[3]
    per = 4 * ch + 3 * ff
    n = 4 * layers
    vmem = pl.BlockSpec(memory_space=pltpu.VMEM)
    dma = pltpu.SemaphoreType.DMA
    return pl.pallas_call(
        functools.partial(step_kernel, (layers, seqs, tokens, ch, ff)),
        out_shape=(
            jax.ShapeDtypeStruct((tokens, ch), F32),
            jax.ShapeDtypeStruct((tokens, ch), F32),
            jax.ShapeDtypeStruct((32, layers * per), F32),
            jax.ShapeDtypeStruct((16, ch), F32),
        ),
        in_specs=[vmem] * 8,
        out_specs=(vmem,) * 4,
        scratch_shapes=[
            pltpu.VMEM((n, tokens, width), BF),
            pltpu.VMEM((4, tokens // 2, ch), F32),
            pltpu.VMEM((n, 3, tokens, ch), BF),
            pltpu.VMEM((n, 6, tokens // 2, ch), BF),
            pltpu.VMEM((n, 4, 8, tokens), F32),
            pltpu.VMEM((2 * layers, tokens, ch), F32),
            pltpu.VMEM((2 * layers, tokens, 128), F32),
            pltpu.VMEM((layers, tokens + 8, ch), F32),
            pltpu.VMEM((layers, tokens + 8, ch), F32),
            pltpu.VMEM((layers, 3, tokens, ch), F32),
            pltpu.VMEM((layers, tokens, ch), F32),
            pltpu.VMEM((layers, tokens, ch), BF),
            pltpu.VMEM((layers, tokens, 2 * ff), F32),
            pltpu.VMEM((layers, tokens, ff), BF),
            pltpu.VMEM((1, tokens, 2 * ff), BF),
            pltpu.VMEM((1, tokens, 3 * ch), BF),
            pltpu.VMEM((width, tokens), BF),
            pltpu.VMEM((4, 4, 2, 32, layers * per), BF),
            pltpu.VMEM((4, 4, 2, 32, per), BF),
            pltpu.VMEM((4, 4, 32, per), BF),
            pltpu.VMEM((6, 2, 32, per), BF),
            pltpu.VMEM((6, 16, per), BF),
            pltpu.VMEM((3, 4, 16, ch), F32),
            dma((n, 6)),
            dma((n, 6)),
            dma((n, 6)),
            dma((n, 6)),
            dma((n, 3)),
            dma((n, 3)),
            dma((2 * layers,)),
            dma((2 * layers,)),
            dma((5 * layers, 12)),
            dma((5 * layers, 12)),
            dma((layers, 6, 13)),
            dma((layers, 6, 13)),
            dma((7,)),
            dma((7,)),
            pltpu.SemaphoreType.REGULAR((6, 3)),
        ],
        compiler_params=pltpu.CompilerParams(
            collective_id=0, has_side_effects=True, vmem_limit_bytes=67043328
        ),
        name="layers",
    )(x, cot, *weights, kern, gain)


def adamw(weight, grad, first, second, rate, decay):
    first_new = 0.9 * first + 0.1 * grad
    second_new = 0.999 * second + 0.001 * grad * grad
    update = first_new / (1.0 - 0.9**STEP) / (jnp.sqrt(second_new / (1.0 - 0.999**STEP)) + 1e-08)
    return (weight - rate * (update + decay * weight), first_new, second_new)


def update_kernel(cfg, *refs):
    ch, ff = cfg
    ins, outs = refs[:22], refs[22:]
    flat, small, hidden, grad = ins[:4]
    entry, leave, gates, down, kern, gain = ins[4:10]
    moments = ins[10:]
    outs[0][...] = hidden[...]
    outs[1][...] = grad[...]
    at_gate = 4 * ch
    pieces = (
        [(0, (0, c), flat[:, k * ch : (k + 1) * ch]) for c, k in enumerate((0, 2, 1))]
        + [(1, (0,), flat[:, 3 * ch : 4 * ch])]
        + [
            (
                2,
                (0, k, slice(None), slice(j * SPAN, (j + 1) * SPAN)),
                flat[:, at_gate + (2 * j + k) * SPAN : at_gate + (2 * j + k + 1) * SPAN],
            )
            for k in range(2)
            for j in range(ff // SPAN)
        ]
        + [(3, (0,), flat[:, at_gate + 2 * ff : at_gate + 3 * ff])]
        + [(4, (j,), small[2 * j : 2 * j + 2]) for j in range(3)]
        + [(5, (l,), small[6 + 2 * l : 8 + 2 * l]) for l in range(2)]
    )
    for n, where, value in pieces:
        rate, decay = (0.01, 0.1) if n < 4 else (0.2, 0.0)
        new = adamw(ins[4 + n][where], value, moments[2 * n][where], moments[2 * n + 1][where], rate, decay)
        outs[2 + n][where] = value
        outs[8 + n][where] = new[0]
        outs[14 + 2 * n][where] = new[1]
        outs[15 + 2 * n][where] = new[2]


def run_update(flat, small, hidden, grad, params, moments):
    layers, _, rows, ch = params[0].shape
    ff = params[2].shape[3]
    per = flat.shape[1] // layers

    def whole(a):
        return pl.BlockSpec(a.shape, lambda l, n=a.ndim: (0,) * n)

    def layer(a):
        return pl.BlockSpec((1, *a.shape[1:]), lambda l, n=a.ndim: (l,) + (0,) * (n - 1))

    def spec(n, a):
        return layer(a) if n < 4 else whole(a)

    each = [spec(n, a) for n, a in enumerate(params)]
    token = pl.BlockSpec((hidden.shape[0] // layers, hidden.shape[1]), lambda l: (l, 0))
    twice = [e for e in each for _ in range(2)]
    shapes = [jax.ShapeDtypeStruct(a.shape, F32) for a in params]
    two = [e for e in shapes for _ in range(2)]
    token_shape = jax.ShapeDtypeStruct(hidden.shape, F32)
    return pl.pallas_call(
        functools.partial(update_kernel, (ch, ff)),
        grid=(layers,),
        out_shape=(token_shape, token_shape, *shapes, *shapes, *two),
        in_specs=[pl.BlockSpec((rows, per), lambda l: (0, l)), whole(small), token, token, *each, *twice],
        out_specs=(token, token, *each, *each, *twice),
        name="update",
    )(flat, small, hidden, grad, *params, *moments)


def per_device(
    inputs,
    cotangent,
    entry_weight,
    exit_weight,
    gate_up,
    down_weight,
    conv_kernel,
    norm_gain,
    entry_first,
    entry_second,
    exit_first,
    exit_second,
    gate_first,
    gate_second,
    down_first,
    down_second,
    kernel_first,
    kernel_second,
    gain_first,
    gain_second,
):
    layers, _, _, ch = entry_weight.shape
    ff = gate_up.shape[3]
    seqs = lax.axis_size("seq")
    weights = (entry_weight, jnp.swapaxes(exit_weight, 1, 2), gate_up, jnp.swapaxes(down_weight, 1, 2))
    hidden, grad, summed, small = run_step(inputs, cotangent, weights, conv_kernel, norm_gain, seqs)
    flip = lambda a: jnp.swapaxes(a, 1, 2)
    spin = lambda a: jnp.swapaxes(a, 0, 1)
    keep = lambda a: a
    turns = (keep, flip, keep, flip, spin, keep)
    params = (entry_weight, exit_weight, gate_up, down_weight, conv_kernel, norm_gain)
    moments = (
        entry_first,
        entry_second,
        exit_first,
        exit_second,
        gate_first,
        gate_second,
        down_first,
        down_second,
        kernel_first,
        kernel_second,
        gain_first,
        gain_second,
    )
    twice = [t for t in turns for _ in range(2)]
    done = run_update(
        summed,
        small,
        hidden,
        grad,
        [t(a) for t, a in zip(turns, params)],
        [t(a) for t, a in zip(twice, moments)],
    )
    return tuple(t(a) for t, a in zip((keep, keep, *turns, *turns, *twice), done))


def solution(mesh):
    tokens, rows, columns, replicated = (
        P("seq", "tp"),
        P(None, None, "seq", "tp"),
        P(None, "tp", "seq"),
        P(None, None, "tp"),
    )
    matrices = (rows, columns, rows, columns)
    moments = (rows, rows, columns, columns, rows, rows, columns, columns)
    return jax.shard_map(
        per_device,
        mesh=mesh,
        in_specs=(tokens, tokens, *matrices, replicated, replicated, *moments, *([replicated] * 4)),
        out_specs=(
            tokens,
            tokens,
            *matrices,
            replicated,
            replicated,
            *matrices,
            replicated,
            replicated,
            *moments,
            *([replicated] * 4),
        ),
        check_vma=False,
    )
```

```python
import functools

import jax
import jax.numpy as jnp
from jax import lax
from jax.experimental import pallas as pl
from jax.experimental.pallas import tpu as pltpu
from jax.sharding import PartitionSpec as P

STEP = 4
EPS = 1e-06
MESH = pl.DeviceIdType.MESH
BF = jnp.bfloat16
F32 = jnp.float32
SPAN = 384
PACE = (-2, 0, 1, 3, 5, 6)


def nn(a, b):
    return lax.dot_general(a, b, (((1,), (0,)), ((), ())), preferred_element_type=F32)


def nt(a, b):
    return lax.dot_general(a, b, (((1,), (1,)), ((), ())), preferred_element_type=F32)


def as_column(row):
    return jnp.broadcast_to(row, (128, row.shape[1])).T[:, 0:1]


def step_kernel(
    cfg,
    x_ref,
    cot_ref,
    entry_ref,
    exit_ref,
    gate_ref,
    down_ref,
    kern_ref,
    gain_ref,
    out_ref,
    din_ref,
    final_ref,
    small_ref,
    rows,
    part,
    stage,
    landed,
    stats,
    normed,
    scales,
    ext,
    dext,
    bcx,
    conv,
    gated,
    gates,
    acted,
    dgates,
    dproj,
    turned,
    w_ref,
    gw_ref,
    from_pair,
    from_far,
    from_near,
    tally,
    ag_send,
    ag_recv,
    rs_send,
    rs_recv,
    st_send,
    st_recv,
    halo_send,
    halo_recv,
    w_send,
    w_recv,
    g_send,
    g_recv,
    t_send,
    t_recv,
    credit,
):
    layers, seqs, tokens, ch, ff = cfg
    width = 4 * ch
    per = 4 * ch + 3 * ff
    z = lax.axis_index("tp")
    s = lax.axis_index("seq")
    zr, zl, zo = lax.rem(z + 1, 4), lax.rem(z + 3, 4), lax.rem(z + 2, 4)
    after, before = lax.rem(s + 1, seqs), lax.rem(s + seqs - 1, seqs)

    c = lax.rem(s, 2)
    x, y = lax.div(s, 8), lax.rem(lax.div(s, 2), 4)
    u, v = x * (1 - c) + y * c, y * (1 - c) + x * c

    def place(uu, vv):
        return uu * (1 - c) + vv * c, vv * (1 - c) + uu * c

    def device(uu, vv):
        px, py = place(uu, vv)
        return (px * 8 + py * 2 + c, z)

    up, un, uo = lax.rem(u + 3, 4), lax.rem(u + 1, 4), lax.rem(u + 2, 4)
    vp, vn, vo = lax.rem(v + 3, 4), lax.rem(v + 1, 4), lax.rem(v + 2, 4)
    u_next, u_prev, v_next, v_prev = device(un, v), device(up, v), device(u, vn), device(u, vp)
    u_over, v_over = device(uo, v), device(u, vo)
    pair = (s + 1 - 2 * c, z)

    barrier = pltpu.get_barrier_semaphore()
    partners = [(s, zr), (s, zl), (s, zo), (after, z), (before, z), u_next, u_prev, v_next, v_prev, pair]
    partners += [u_over, v_over]
    partners += [(lax.rem(x + k, 4) * 8 + y * 2 + 1 - c, z) for k in (1, 2, 3)]
    for where in partners:
        pl.semaphore_signal(barrier, inc=1, device_id=where, device_id_type=MESH)
    pl.semaphore_wait(barrier, len(partners))

    pending = []

    def send(src, dst, ssem, rsem, where):
        copy = pltpu.make_async_remote_copy(
            src_ref=src, dst_ref=dst, send_sem=ssem, recv_sem=rsem, device_id=where, device_id_type=MESH
        )
        copy.start()
        pending.append(copy)
        return copy

    def cols(who):
        return pl.ds(pl.multiple_of(who * ch, ch), ch)

    def own_rows(who):
        return pl.ds(pl.multiple_of(who * ch, ch), ch)

    def chunk_of(ref, lead, vv, lo, hi, where):
        if lead == 0:
            return ref.at[pl.ds(lo, hi - lo), vv, 0, :, where]
        return ref.at[vv, pl.ds(lo, hi - lo), 1, :, where]

    def send_either(make, ssem, rsem, where, held=pending):
        for core in (0, 1):

            @pl.when(c == core)
            def _(core=core):
                src, dst = make(core)
                pltpu.make_async_remote_copy(
                    src_ref=src, dst_ref=dst, send_sem=ssem, recv_sem=rsem, device_id=where, device_id_type=MESH
                ).start()

        src, dst = make(0)
        copy = pltpu.make_async_remote_copy(
            src_ref=src, dst_ref=dst, send_sem=ssem, recv_sem=rsem, device_id=where, device_id_type=MESH
        )
        held.append(copy)
        return copy

    spans = []
    for l in range(layers):
        at = l * per
        for size in (3 * ch, ch + 2 * SPAN, 2 * SPAN, 2 * SPAN, ff):
            spans.append(pl.ds(at, size))
            at += size

    def pack(k):
        l, part_index = k // 5, k % 5
        at = l * per

        def put(start, value):
            w_ref[x, y, c, :, start : start + value.shape[1]] = value.astype(BF)

        if part_index == 0:
            for j in range(3):
                put(at + (0, 2, 1)[j] * ch, entry_ref[l, j])
        elif part_index == 4:
            put(at + 4 * ch + 2 * ff, down_ref[l])
        else:
            if part_index == 1:
                put(at + 3 * ch, exit_ref[l])
            j = part_index - 1
            for half_index in range(2):
                put(
                    at + 4 * ch + (2 * j + half_index) * SPAN,
                    gate_ref[l, half_index, :, j * SPAN : (j + 1) * SPAN],
                )

    class Weights:
        def __init__(self, k):
            self.k, self.where, self.stage = k, spans[k], 0

        def block(self, uu, vv, r=slice(None)):
            px, py = place(uu, vv)
            return w_ref.at[px, py, c, r, self.where]

        def move(self, ref, n, where):
            return send(ref, ref, w_send.at[self.k, n], w_recv.at[self.k, n], where)

        def move_row(self, vv, lo, hi, n, where):
            def make(core):
                ref = chunk_of(w_ref, core, vv, lo, hi, self.where)
                return ref, ref

            return send_either(make, w_send.at[self.k, n], w_recv.at[self.k, n], where)

        def direct(self, stage):
            if stage == 0:
                pack(self.k)
                self.got = [
                    self.move(self.block(u, v), n, where) for n, where in enumerate((u_over, u_next, u_prev))
                ]
            elif stage == 1:
                for copy in self.got:
                    copy.wait_recv()
                self.got = [
                    self.move_row(v, 0, 4, 4 + n, where) for n, where in enumerate((v_over, v_next, v_prev))
                ]
                self.p0 = self.move_row(v, 0, 4, 8, pair)
            elif stage == 2:
                for n, (copy, vv) in enumerate(zip(self.got[::-1], (vn, vp, vo))):
                    copy.wait_recv()
                    self.got[2 - n] = self.move_row(vv, 0, 4, 9 + n, pair)
            else:
                for copy in (self.p0, *self.got):
                    copy.wait_recv()
                self.stage = 6

        def step(self):
            stage, self.stage = self.stage, self.stage + 1
            if self.k == 0:
                self.direct(stage)
            elif stage == 0:
                pack(self.k)
                self.a0 = self.move(self.block(u, v), 0, u_next)
                self.a1 = self.move(self.block(u, v), 1, u_prev)
            elif stage == 1:
                self.a0.wait_recv()
                self.a2 = self.move(self.block(up, v, pl.ds(0, 16)), 2, u_next)
                self.a1.wait_recv()
                self.a3 = self.move(self.block(un, v, pl.ds(16, 16)), 3, u_prev)
            elif stage == 2:
                self.a2.wait_recv()
                self.a3.wait_recv()
                self.b0 = self.move_row(v, 0, 4, 4, v_next)
                self.b1 = self.move_row(v, 0, 4, 5, v_prev)
                self.p0 = self.move_row(v, 0, 4, 8, pair)
            elif stage == 3:
                self.b0.wait_recv()
                self.b2 = self.move_row(vp, 0, 2, 6, v_next)
                self.b1.wait_recv()
                self.b3 = self.move_row(vn, 2, 4, 7, v_prev)
                self.p1 = self.move_row(vp, 0, 4, 9, pair)
                self.p2 = self.move_row(vn, 0, 4, 10, pair)
            elif stage == 4:
                self.b2.wait_recv()
                self.b3.wait_recv()
                self.p3 = self.move_row(vo, 0, 4, 11, pair)
            else:
                for copy in (self.p0, self.p1, self.p2, self.p3):
                    copy.wait_recv()

    class Sums:
        def __init__(self, l, k, where):
            self.l, self.k, self.where, self.stage = l, k, where, 0
            self.total = pl.ds(l * per + where.start, where.size)
            self.first = l == layers - 1
            self.sent = []

        def send(self, src, dst, n, where):
            copy = pltpu.make_async_remote_copy(
                src_ref=src,
                dst_ref=dst,
                send_sem=g_send.at[self.l, self.k, n],
                recv_sem=g_recv.at[self.l, self.k, n],
                device_id=where,
                device_id_type=MESH,
            )
            copy.start()
            self.sent.append(copy)
            return copy

        def far(self, vv, lo, n, where):
            def make(core):
                return chunk_of(gw_ref, core, vv, lo, lo + 2, self.where), from_far.at[n - 1, :, :, self.where]

            copy = send_either(make, g_send.at[self.l, self.k, n], g_recv.at[self.l, self.k, n], where, self.sent)
            return copy

        def near(self, uu, r, n, where):
            px, py = place(uu, v)
            return self.send(gw_ref.at[px, py, c, r, self.where], from_near.at[n - 7, :, self.where], n, where)

        def add_far(self, vv, lo, slots):
            for i in range(2):
                px, py = place(lo + i, vv)
                value = gw_ref[px, py, c, :, self.where].astype(F32)
                for slot in slots:
                    value += from_far[slot, i, :, self.where].astype(F32)
                gw_ref[px, py, c, :, self.where] = value.astype(BF)

        def add_near(self, uu, r, slots):
            px, py = place(uu, v)
            value = gw_ref[px, py, c, r, self.where].astype(F32)
            for slot in slots:
                value += from_near[slot, :, self.where].astype(F32)
            return value

        def allow(self, kind, devices):
            if self.first:
                for where in devices:
                    pl.semaphore_signal(credit.at[self.k, kind], inc=1, device_id=where, device_id_type=MESH)

        def ask(self, kind, count):
            if not self.first:
                pl.semaphore_wait(credit.at[self.k, kind], count)

        def add_pair(self):
            self.q.wait_recv()

            @pl.loop(0, 4)
            def _(i):
                gw_ref[i, :, c, :, self.where] = (
                    gw_ref[i, :, c, :, self.where].astype(F32) + from_pair[i, :, :, self.where].astype(F32)
                ).astype(BF)

        def direct(self, stage, upper, lower):
            if stage == 1:
                self.add_pair()
                self.ask(1, 3)
                pairs = ((vo, v_over), (vn, v_next), (vp, v_prev))
                self.got = [
                    self.far(vv, 2 * k, 1 + 2 * n + k, where) for n, (vv, where) in enumerate(pairs) for k in (0, 1)
                ]
            elif stage == 2:
                for copy in self.got:
                    copy.wait_recv()
                self.add_far(v, 0, [0, 2, 4])
                self.add_far(v, 2, [1, 3, 5])
                self.ask(2, 3)
                pairs = ((uo, u_over), (un, u_next), (up, u_prev))
                self.got = [
                    self.near(uu, r, 7 + 2 * n + k, where)
                    for n, (uu, where) in enumerate(pairs)
                    for k, r in enumerate((upper, lower))
                ]
            else:
                for copy in self.got:
                    copy.wait_recv()
                final_ref[0:16, self.total] = self.add_near(u, upper, [0, 2, 4])
                final_ref[16:32, self.total] = self.add_near(u, lower, [1, 3, 5])
                for copy in self.sent:
                    copy.wait_send()
                self.stage = 6

        def step(self):
            stage, self.stage = self.stage, self.stage + 1
            upper, lower = pl.ds(0, 16), pl.ds(16, 16)
            if self.l == 0 and self.k == 0 and stage > 0:
                self.direct(stage, upper, lower)
            elif stage == 0:
                self.ask(0, 1)
                self.q = self.send(
                    gw_ref.at[:, :, 1 - c, :, self.where], from_pair.at[:, :, :, self.where], 0, pair
                )
            elif stage == 1:
                self.add_pair()
                self.allow(0, [pair])
                self.ask(1, 2)
                self.f0 = self.far(vo, 0, 1, v_next)
                self.f1 = self.far(vo, 2, 2, v_prev)
                self.f2 = self.far(vn, 2, 3, v_next)
                self.f3 = self.far(vp, 0, 4, v_prev)
            elif stage == 2:
                self.f0.wait_recv()
                self.add_far(vn, 0, [0])
                self.f4 = self.far(vn, 0, 5, v_next)
                self.f1.wait_recv()
                self.add_far(vp, 2, [1])
                self.f5 = self.far(vp, 2, 6, v_prev)
            elif stage == 3:
                for copy in (self.f2, self.f3, self.f4, self.f5):
                    copy.wait_recv()
                self.add_far(v, 0, [3, 4])
                self.add_far(v, 2, [2, 5])
                self.allow(1, [v_next, v_prev, v_over] if self.k == 0 else [v_next, v_prev])
                self.ask(2, 2)
                self.n0 = self.near(uo, upper, 7, u_next)
                self.n1 = self.near(uo, lower, 8, u_prev)
                self.n2 = self.near(un, lower, 9, u_next)
                self.n3 = self.near(up, upper, 10, u_prev)
            elif stage == 4:
                self.n0.wait_recv()
                px, py = place(un, v)
                gw_ref[px, py, c, upper, self.where] = self.add_near(un, upper, [0]).astype(BF)
                self.n4 = self.near(un, upper, 11, u_next)
                self.n1.wait_recv()
                px, py = place(up, v)
                gw_ref[px, py, c, lower, self.where] = self.add_near(up, lower, [1]).astype(BF)
                self.n5 = self.near(up, lower, 12, u_prev)
            else:
                for copy in (self.n2, self.n3, self.n4, self.n5):
                    copy.wait_recv()
                final_ref[0:16, self.total] = self.add_near(u, upper, [3, 4])
                final_ref[16:32, self.total] = self.add_near(u, lower, [2, 5])
                self.allow(2, [u_next, u_prev, u_over] if self.k == 0 else [u_next, u_prev])
                for copy in self.sent:
                    copy.wait_send()

    fetches = [Weights(k) for k in range(len(spans))]
    fetched = [0]
    sums = []

    def tick():
        t = fetched[0]
        fetched[0] += 1
        for k, fetch in enumerate(fetches):
            if fetch.stage == 0 and t >= k + PACE[0]:
                fetch.step()
        for k, fetch in enumerate(fetches):
            if 0 < fetch.stage < 6 and t >= k + PACE[fetch.stage]:
                fetch.step()
        for total in sums:
            if total.stage < 6:
                total.step()

    def need(l, part_index):
        fetch = fetches[5 * l + part_index]
        while fetch.stage < 6:
            fetch.step()

    def ready(l, k, at, size):
        total = Sums(l, k, pl.ds(at, size))
        total.step()
        sums.append(total)

    def clear(k):
        for total in sums:
            if total.k == k:
                while total.stage < 6:
                    tick()

    def weight(where):
        return w_ref[:, :, :, :, where].reshape(width, where.size)

    def weight_rows(who, where):
        return w_ref[who, :, :, :, where].reshape(ch, where.size)

    tick()

    class Gather:
        def __init__(self, i, block):
            rows[i, :, cols(z)] = block
            mine = rows.at[i, :, cols(z)]
            self.got = [
                send(mine, mine, ag_send.at[i, k], ag_recv.at[i, k], (s, who)) for k, who in enumerate((zo, zr, zl))
            ]

        def finish(self):
            for copy in self.got:
                copy.wait_recv()

    class Scatter:
        def __init__(self, i, piece):
            self.i, self.got = i, []
            for k, who in enumerate((zo, zr, zl)):
                stage[i, k] = piece(who).astype(BF)
                copy = send(stage.at[i, k], landed.at[i, k], rs_send.at[i, k], rs_recv.at[i, k], (s, who))
                self.got.append(copy)
            part[...] = piece(z)

        def finish(self):
            for copy in self.got:
                copy.wait_recv()
            i = self.i
            return part[...] + landed[i, 0].astype(F32) + landed[i, 1].astype(F32) + landed[i, 2].astype(F32)

    class Total:
        def __init__(self, i, sums):
            self.i = i
            stats[i, z] = jnp.broadcast_to(sums, (tokens, 128)).T[0:8]
            there = stats.at[i, z]
            self.got = [
                send(there, there, st_send.at[i, k], st_recv.at[i, k], (s, who))
                for k, who in enumerate((zr, zl, zo))
            ]

        def finish(self):
            for copy in self.got:
                copy.wait_recv()
            i = self.i
            total = stats[i, 0] + stats[i, 1] + stats[i, 2] + stats[i, 3]
            return as_column(total[0:1])

    def row_sum(value):
        return jnp.sum(value, axis=1, keepdims=True)

    def columns(at, j, size=SPAN):
        return pl.ds(at + j * size, size)

    def turn(left_index, k=None):
        if k is None:
            turned[...] = rows[left_index].T
        else:
            turned[...] = (rows[left_index].astype(F32) * scales[k][:, 0:1]).astype(BF).T

    def weight_grad(l, k, right_ref, lead, start, size, at):
        clear(k)
        piece = nn(turned[...], right_ref[lead, :, start : start + size]).astype(BF)
        gw_ref[:, :, :, :, at : at + size] = piece.reshape(4, 4, 2, 32, size)

    def norm_scale(k, total, h):
        scale = lax.rsqrt(total.finish() / width + EPS)
        scales[k] = jnp.broadcast_to(scale, (tokens, 128))
        normed[k] = h * scale
        return scale

    def norm_backward(k, dn, inner, gain, small_row):
        a = normed[k]
        small_ref[pl.ds(small_row, 1), :] = jnp.sum(dn * a, axis=0, keepdims=True)
        return scales[k][:, 0:1] * (dn * gain - a * (inner / width))

    small_ref[...] = jnp.zeros_like(small_ref)
    hidden = x_ref[...]
    cot_gather = None
    for l in range(layers):
        base = l * per
        at_exit, at_gate, at_down = base + 3 * ch, base + 4 * ch, base + 4 * ch + 2 * ff
        gather = Gather(2 * l, (hidden * gain_ref[l, 0:1]).astype(BF))
        total = Total(2 * l, row_sum(hidden * hidden))
        if l == 0:
            cot_gather = Gather(2 * layers + 2 * (layers - 1), cot_ref[...].astype(BF))
        tick()
        tick()
        gather.finish()
        scale = norm_scale(2 * l, total, hidden)
        need(l, 0)
        full = rows[2 * l]
        bm = nn(full, weight(columns(base, 0, ch))) * scale
        xm = nn(full, weight(columns(base, 1, ch))) * scale
        bx = bm * xm
        ext[l, 8:] = bx
        tail = send(
            ext.at[l, pl.ds(tokens, 8)], ext.at[l, pl.ds(0, 8)], halo_send.at[l], halo_recv.at[l], (after, z)
        )
        bcx[l, 0] = bm
        bcx[l, 2] = xm
        tick()
        cm = nn(full, weight(columns(base, 2, ch))) * scale
        bcx[l, 1] = cm
        tick()
        tail.wait_recv()
        head = ext[l, 0:8]
        ext[l, 0:8] = jnp.where(s > 0, head, jnp.zeros_like(head))
        k = [kern_ref[j, l : l + 1] for j in range(3)]
        zc = k[0] * ext[l, 6 : 6 + tokens] + k[1] * ext[l, 7 : 7 + tokens] + k[2] * ext[l, 8 : 8 + tokens]
        conv[l] = zc
        gated[l] = (cm * zc).astype(BF)

        def exit_piece(who, l=l, at=at_exit):
            return nt(gated[l], weight_rows(who, columns(at, 0, ch)))

        need(l, 1)
        scatter = Scatter(2 * l, exit_piece)
        tick()
        tick()
        mid = hidden + scatter.finish()
        gather = Gather(2 * l + 1, (mid * gain_ref[l, 1:2]).astype(BF))
        total = Total(2 * l + 1, row_sum(mid * mid))
        tick()
        tick()
        gather.finish()
        scale = norm_scale(2 * l + 1, total, mid)
        need(l, 1)

        for j in range(ff // SPAN):
            need(l, 1 + j)
            tick()
            both = nn(rows[2 * l + 1], weight(columns(at_gate, j, 2 * SPAN))) * scale
            gates[l, :, j * 2 * SPAN : (j + 1) * 2 * SPAN] = both
            g, up_value = both[:, :SPAN], both[:, SPAN:]
            acted[l, :, j * SPAN : (j + 1) * SPAN] = (g * jax.nn.sigmoid(g) * up_value).astype(BF)

        def down_piece(who, l=l, at=at_down):
            return nt(acted[l], weight_rows(who, columns(at, 0, ff)))

        need(l, 4)
        scatter = Scatter(2 * l + 1, down_piece)
        tick()
        tick()
        hidden = mid + scatter.finish()
    out_ref[...] = hidden

    grad = cot_ref[...]
    for l in reversed(range(layers)):
        base = l * per
        at_exit, at_gate, at_down = base + 3 * ch, base + 4 * ch, base + 4 * ch + 2 * ff
        ie = 2 * layers + 2 * l
        if l == layers - 1:
            gather = cot_gather
        else:
            gather = Gather(ie, grad.astype(BF))
            tick()
            tick()
        gather.finish()

        inner = jnp.zeros((tokens, 1), F32)
        for j in range(ff // SPAN):
            ds = nn(rows[ie], weight(columns(at_down, j)))
            g = gates[l, :, j * 2 * SPAN : j * 2 * SPAN + SPAN]
            up_value = gates[l, :, j * 2 * SPAN + SPAN : (j + 1) * 2 * SPAN]
            sig = jax.nn.sigmoid(g)
            dg = (ds * up_value * sig * (1.0 + g * (1.0 - sig))).astype(BF)
            du = (ds * (g * sig)).astype(BF)
            dgates[0, :, j * 2 * SPAN : j * 2 * SPAN + SPAN] = dg
            dgates[0, :, j * 2 * SPAN + SPAN : (j + 1) * 2 * SPAN] = du
            inner += row_sum(dg.astype(F32) * g + du.astype(F32) * up_value)
        total = Total(2 * layers + 2 * l + 1, inner)

        def norm2_piece(who, at_gate=at_gate):
            return nt(dgates[0], weight_rows(who, columns(at_gate, 0, 2 * ff)))

        scatter = Scatter(2 * layers + 2 * l, norm2_piece)
        turn(ie)
        weight_grad(l, 4, acted, l, 0, ff, 4 * ch + 2 * ff)
        ready(l, 4, 4 * ch + 2 * ff, ff)
        turn(2 * l + 1, 2 * l + 1)
        for j in range(ff // SPAN):
            weight_grad(l, 1 + j, dgates, 0, j * 2 * SPAN, 2 * SPAN, 4 * ch + j * 2 * SPAN)
            ready(l, 1 + j, 4 * ch + j * 2 * SPAN, 2 * SPAN)
        dn2 = scatter.finish()
        dmid = grad + norm_backward(2 * l + 1, dn2, total.finish(), gain_ref[l, 1:2], 3 * layers + 2 * l + 1)
        gather = Gather(ie + 1, dmid.astype(BF))
        tick()
        tick()
        gather.finish()
        dy = nn(rows[ie + 1], weight(columns(at_exit, 0, ch)))
        dz = dy * bcx[l, 1]
        dext[l, :tokens] = dz
        tail = send(
            dext.at[l, pl.ds(0, 8)],
            dext.at[l, pl.ds(tokens, 8)],
            halo_send.at[layers + l],
            halo_recv.at[layers + l],
            (before, z),
        )
        dproj[0, :, 2 * ch :] = (dy * conv[l]).astype(BF)
        for j in range(3):
            small_ref[pl.ds(j * layers + l, 1), :] = jnp.sum(dz * ext[l, 6 + j : 6 + j + tokens], axis=0, keepdims=True)
        turn(ie + 1)
        weight_grad(l, 5, gated, l, 0, ch, 3 * ch)
        turn(2 * l, 2 * l)
        weight_grad(l, 5, dproj, 0, 2 * ch, ch, 2 * ch)
        ready(l, 5, 2 * ch, 2 * ch)
        tick()
        tail.wait_recv()
        last = dext[l, tokens:]
        dext[l, tokens:] = jnp.where(s < seqs - 1, last, jnp.zeros_like(last))
        k = [kern_ref[j, l : l + 1] for j in range(3)]
        dbx = k[2] * dext[l, 0:tokens] + k[1] * dext[l, 1 : 1 + tokens] + k[0] * dext[l, 2 : 2 + tokens]
        db = (dbx * bcx[l, 2]).astype(BF)
        dx = (dbx * bcx[l, 0]).astype(BF)
        dproj[0, :, :ch] = db
        dproj[0, :, ch : 2 * ch] = dx
        dc = dproj[0, :, 2 * ch :].astype(F32)
        inner = row_sum(db.astype(F32) * bcx[l, 0] + dc * bcx[l, 1] + dx.astype(F32) * bcx[l, 2])
        total = Total(2 * layers + 2 * l, inner)

        def norm1_piece(who, base=base):
            return nt(dproj[0], weight_rows(who, columns(base, 0, 3 * ch)))

        if l == 0:
            weight_grad(l, 0, dproj, 0, 0, 2 * ch, 0)
            ready(l, 0, 0, 2 * ch)
        scatter = Scatter(2 * layers + 2 * l + 1, norm1_piece)
        if l > 0:
            weight_grad(l, 0, dproj, 0, 0, 2 * ch, 0)
            ready(l, 0, 0, 2 * ch)
        tick()
        tick()
        dn1 = scatter.finish()
        grad = dmid + norm_backward(2 * l, dn1, total.finish(), gain_ref[l, 0:1], 3 * layers + 2 * l)
    din_ref[...] = grad
    tally[0, 2 * x + c] = small_ref[...]
    slot = tally.at[0, 2 * x + c]
    near_by = [(lax.rem(x + k // 2, 4) * 8 + y * 2 + lax.rem(c + k, 2), z) for k in range(1, 8)]
    copies = [send(slot, slot, t_send.at[k], t_recv.at[k], where) for k, where in enumerate(near_by)]
    tick()
    for copy in copies:
        copy.wait_recv()
    tally[1, y] = sum((tally[0, k] for k in range(1, 8)), tally[0, 0])
    slot = tally.at[1, y]
    copies = [
        send(slot, slot, t_send.at[6 + k], t_recv.at[6 + k], (x * 8 + lax.rem(y + k, 4) * 2 + c, z)) for k in (1, 2, 3)
    ]
    tick()
    for copy in copies:
        copy.wait_recv()
    small_ref[...] = tally[1, 0] + tally[1, 1] + tally[1, 2] + tally[1, 3]
    while any(total.stage < 6 for total in sums):
        tick()
    for copy in pending:
        copy.wait_send()


def run_step(x, cot, weights, kern, gain, seqs):
    taps, layers, ch = kern.shape
    tokens = x.shape[0]
    width = 4 * ch
    ff = weights[2].shape[3]
    per = 4 * ch + 3 * ff
    n = 4 * layers
    vmem = pl.BlockSpec(memory_space=pltpu.VMEM)
    dma = pltpu.SemaphoreType.DMA
    return pl.pallas_call(
        functools.partial(step_kernel, (layers, seqs, tokens, ch, ff)),
        out_shape=(
            jax.ShapeDtypeStruct((tokens, ch), F32),
            jax.ShapeDtypeStruct((tokens, ch), F32),
            jax.ShapeDtypeStruct((32, layers * per), F32),
            jax.ShapeDtypeStruct((16, ch), F32),
        ),
        in_specs=[vmem] * 8,
        out_specs=(vmem,) * 4,
        scratch_shapes=[
            pltpu.VMEM((n, tokens, width), BF),
            pltpu.VMEM((tokens, ch), F32),
            pltpu.VMEM((n, 3, tokens, ch), BF),
            pltpu.VMEM((n, 3, tokens, ch), BF),
            pltpu.VMEM((n, 4, 8, tokens), F32),
            pltpu.VMEM((2 * layers, tokens, ch), F32),
            pltpu.VMEM((2 * layers, tokens, 128), F32),
            pltpu.VMEM((layers, tokens + 8, ch), F32),
            pltpu.VMEM((layers, tokens + 8, ch), F32),
            pltpu.VMEM((layers, 3, tokens, ch), F32),
            pltpu.VMEM((layers, tokens, ch), F32),
            pltpu.VMEM((layers, tokens, ch), BF),
            pltpu.VMEM((layers, tokens, 2 * ff), F32),
            pltpu.VMEM((layers, tokens, ff), BF),
            pltpu.VMEM((1, tokens, 2 * ff), BF),
            pltpu.VMEM((1, tokens, 3 * ch), BF),
            pltpu.VMEM((width, tokens), BF),
            pltpu.VMEM((4, 4, 2, 32, layers * per), BF),
            pltpu.VMEM((4, 4, 2, 32, per), BF),
            pltpu.VMEM((4, 4, 32, per), BF),
            pltpu.VMEM((6, 2, 32, per), BF),
            pltpu.VMEM((6, 16, per), BF),
            pltpu.VMEM((2, 8, 16, ch), F32),
            dma((n, 3)),
            dma((n, 3)),
            dma((n, 3)),
            dma((n, 3)),
            dma((n, 3)),
            dma((n, 3)),
            dma((2 * layers,)),
            dma((2 * layers,)),
            dma((5 * layers, 12)),
            dma((5 * layers, 12)),
            dma((layers, 6, 13)),
            dma((layers, 6, 13)),
            dma((10,)),
            dma((10,)),
            pltpu.SemaphoreType.REGULAR((6, 3)),
        ],
        compiler_params=pltpu.CompilerParams(
            collective_id=0, has_side_effects=True, vmem_limit_bytes=67043328
        ),
        name="layers",
    )(x, cot, *weights, kern, gain)


def adamw(weight, grad, first, second, rate, decay):
    first_new = 0.9 * first + 0.1 * grad
    second_new = 0.999 * second + 0.001 * grad * grad
    update = first_new / (1.0 - 0.9**STEP) / (jnp.sqrt(second_new / (1.0 - 0.999**STEP)) + 1e-08)
    return (weight - rate * (update + decay * weight), first_new, second_new)


def update_kernel(cfg, *refs):
    ch, ff = cfg
    ins, outs = refs[:22], refs[22:]
    flat, small, hidden, grad = ins[:4]
    entry, leave, gates, down, kern, gain = ins[4:10]
    moments = ins[10:]
    outs[0][...] = hidden[...]
    outs[1][...] = grad[...]
    at_gate = 4 * ch
    pieces = (
        [(0, (0, c), flat[:, k * ch : (k + 1) * ch]) for c, k in enumerate((0, 2, 1))]
        + [(1, (0,), flat[:, 3 * ch : 4 * ch])]
        + [
            (
                2,
                (0, k, slice(None), slice(j * SPAN, (j + 1) * SPAN)),
                flat[:, at_gate + (2 * j + k) * SPAN : at_gate + (2 * j + k + 1) * SPAN],
            )
            for k in range(2)
            for j in range(ff // SPAN)
        ]
        + [(3, (0,), flat[:, at_gate + 2 * ff : at_gate + 3 * ff])]
        + [(4, (j,), small[2 * j : 2 * j + 2]) for j in range(3)]
        + [(5, (l,), small[6 + 2 * l : 8 + 2 * l]) for l in range(2)]
    )
    for n, where, value in pieces:
        rate, decay = (0.01, 0.1) if n < 4 else (0.2, 0.0)
        new = adamw(ins[4 + n][where], value, moments[2 * n][where], moments[2 * n + 1][where], rate, decay)
        outs[2 + n][where] = value
        outs[8 + n][where] = new[0]
        outs[14 + 2 * n][where] = new[1]
        outs[15 + 2 * n][where] = new[2]


def run_update(flat, small, hidden, grad, params, moments):
    layers, _, rows, ch = params[0].shape
    ff = params[2].shape[3]
    per = flat.shape[1] // layers

    def whole(a):
        return pl.BlockSpec(a.shape, lambda l, n=a.ndim: (0,) * n)

    def layer(a):
        return pl.BlockSpec((1, *a.shape[1:]), lambda l, n=a.ndim: (l,) + (0,) * (n - 1))

    def spec(n, a):
        return layer(a) if n < 4 else whole(a)

    each = [spec(n, a) for n, a in enumerate(params)]
    token = pl.BlockSpec((hidden.shape[0] // layers, hidden.shape[1]), lambda l: (l, 0))
    twice = [e for e in each for _ in range(2)]
    shapes = [jax.ShapeDtypeStruct(a.shape, F32) for a in params]
    two = [e for e in shapes for _ in range(2)]
    token_shape = jax.ShapeDtypeStruct(hidden.shape, F32)
    return pl.pallas_call(
        functools.partial(update_kernel, (ch, ff)),
        grid=(layers,),
        out_shape=(token_shape, token_shape, *shapes, *shapes, *two),
        in_specs=[pl.BlockSpec((rows, per), lambda l: (0, l)), whole(small), token, token, *each, *twice],
        out_specs=(token, token, *each, *each, *twice),
        name="update",
    )(flat, small, hidden, grad, *params, *moments)


def per_device(
    inputs,
    cotangent,
    entry_weight,
    exit_weight,
    gate_up,
    down_weight,
    conv_kernel,
    norm_gain,
    entry_first,
    entry_second,
    exit_first,
    exit_second,
    gate_first,
    gate_second,
    down_first,
    down_second,
    kernel_first,
    kernel_second,
    gain_first,
    gain_second,
):
    layers, _, _, ch = entry_weight.shape
    ff = gate_up.shape[3]
    seqs = lax.axis_size("seq")
    weights = (entry_weight, jnp.swapaxes(exit_weight, 1, 2), gate_up, jnp.swapaxes(down_weight, 1, 2))
    hidden, grad, summed, small = run_step(inputs, cotangent, weights, jnp.swapaxes(conv_kernel, 0, 1), norm_gain, seqs)
    flip = lambda a: jnp.swapaxes(a, 1, 2)
    spin = lambda a: jnp.swapaxes(a, 0, 1)
    keep = lambda a: a
    turns = (keep, flip, keep, flip, spin, keep)
    params = (entry_weight, exit_weight, gate_up, down_weight, conv_kernel, norm_gain)
    moments = (
        entry_first,
        entry_second,
        exit_first,
        exit_second,
        gate_first,
        gate_second,
        down_first,
        down_second,
        kernel_first,
        kernel_second,
        gain_first,
        gain_second,
    )
    twice = [t for t in turns for _ in range(2)]
    done = run_update(
        summed,
        small,
        hidden,
        grad,
        [t(a) for t, a in zip(turns, params)],
        [t(a) for t, a in zip(twice, moments)],
    )
    return tuple(t(a) for t, a in zip((keep, keep, *turns, *turns, *twice), done))


def solution(mesh):
    tokens, rows, columns, replicated = (
        P("seq", "tp"),
        P(None, None, "seq", "tp"),
        P(None, "tp", "seq"),
        P(None, None, "tp"),
    )
    matrices = (rows, columns, rows, columns)
    moments = (rows, rows, columns, columns, rows, rows, columns, columns)
    return jax.shard_map(
        per_device,
        mesh=mesh,
        in_specs=(tokens, tokens, *matrices, replicated, replicated, *moments, *([replicated] * 4)),
        out_specs=(
            tokens,
            tokens,
            *matrices,
            replicated,
            replicated,
            *matrices,
            replicated,
            replicated,
            *moments,
            *([replicated] * 4),
        ),
        check_vma=False,
    )
```

```python
import functools

import jax
import jax.numpy as jnp
from jax import lax
from jax.experimental import pallas as pl
from jax.experimental.pallas import tpu as pltpu
from jax.sharding import PartitionSpec as P

STEP = 4
EPS = 1e-06
MESH = pl.DeviceIdType.MESH
BF = jnp.bfloat16
F32 = jnp.float32
SPAN = 384
PACE = (-2, 0, 1, 3, 5, 6)


def nn(a, b):
    return lax.dot_general(a, b, (((1,), (0,)), ((), ())), preferred_element_type=F32)


def nt(a, b):
    return lax.dot_general(a, b, (((1,), (1,)), ((), ())), preferred_element_type=F32)


def as_column(row):
    return jnp.broadcast_to(row, (128, row.shape[1])).T[:, 0:1]


def step_kernel(
    cfg,
    x_ref,
    cot_ref,
    entry_ref,
    exit_ref,
    gate_ref,
    down_ref,
    kern_ref,
    gain_ref,
    out_ref,
    din_ref,
    final_ref,
    small_ref,
    rows,
    part,
    stage,
    landed,
    stats,
    normed,
    scales,
    ext,
    dext,
    bcx,
    conv,
    gated,
    gates,
    acted,
    dgates,
    dproj,
    turned,
    w_ref,
    gw_ref,
    from_pair,
    from_far,
    from_near,
    tally,
    ag_send,
    ag_recv,
    rs_send,
    rs_recv,
    st_send,
    st_recv,
    halo_send,
    halo_recv,
    w_send,
    w_recv,
    g_send,
    g_recv,
    t_send,
    t_recv,
    credit,
):
    layers, seqs, tokens, ch, ff = cfg
    width = 4 * ch
    per = 4 * ch + 3 * ff
    z = lax.axis_index("tp")
    s = lax.axis_index("seq")
    zr, zl, zo = lax.rem(z + 1, 4), lax.rem(z + 3, 4), lax.rem(z + 2, 4)
    after, before = lax.rem(s + 1, seqs), lax.rem(s + seqs - 1, seqs)

    c = lax.rem(s, 2)
    x, y = lax.div(s, 8), lax.rem(lax.div(s, 2), 4)
    u, v = x * (1 - c) + y * c, y * (1 - c) + x * c

    def place(uu, vv):
        return uu * (1 - c) + vv * c, vv * (1 - c) + uu * c

    def device(uu, vv):
        px, py = place(uu, vv)
        return (px * 8 + py * 2 + c, z)

    up, un, uo = lax.rem(u + 3, 4), lax.rem(u + 1, 4), lax.rem(u + 2, 4)
    vp, vn, vo = lax.rem(v + 3, 4), lax.rem(v + 1, 4), lax.rem(v + 2, 4)
    u_next, u_prev, v_next, v_prev = device(un, v), device(up, v), device(u, vn), device(u, vp)
    u_over, v_over = device(uo, v), device(u, vo)
    pair = (s + 1 - 2 * c, z)

    barrier = pltpu.get_barrier_semaphore()
    partners = [(s, zr), (s, zl), (s, zo), (after, z), (before, z), u_next, u_prev, v_next, v_prev, pair]
    partners += [u_over, v_over]
    partners += [(lax.rem(x + k, 4) * 8 + y * 2 + 1 - c, z) for k in (1, 2, 3)]
    for where in partners:
        pl.semaphore_signal(barrier, inc=1, device_id=where, device_id_type=MESH)
    pl.semaphore_wait(barrier, len(partners))

    pending = []

    def send(src, dst, ssem, rsem, where):
        copy = pltpu.make_async_remote_copy(
            src_ref=src, dst_ref=dst, send_sem=ssem, recv_sem=rsem, device_id=where, device_id_type=MESH
        )
        copy.start()
        pending.append(copy)
        return copy

    def cols(who):
        return pl.ds(pl.multiple_of(who * ch, ch), ch)

    def own_rows(who):
        return pl.ds(pl.multiple_of(who * ch, ch), ch)

    def chunk_of(ref, lead, vv, lo, hi, where):
        if lead == 0:
            return ref.at[pl.ds(lo, hi - lo), vv, 0, :, where]
        return ref.at[vv, pl.ds(lo, hi - lo), 1, :, where]

    def send_either(make, ssem, rsem, where, held=pending):
        for core in (0, 1):

            @pl.when(c == core)
            def _(core=core):
                src, dst = make(core)
                pltpu.make_async_remote_copy(
                    src_ref=src, dst_ref=dst, send_sem=ssem, recv_sem=rsem, device_id=where, device_id_type=MESH
                ).start()

        src, dst = make(0)
        copy = pltpu.make_async_remote_copy(
            src_ref=src, dst_ref=dst, send_sem=ssem, recv_sem=rsem, device_id=where, device_id_type=MESH
        )
        held.append(copy)
        return copy

    spans = []
    for l in range(layers):
        at = l * per
        for size in (3 * ch, ch + 2 * SPAN, 2 * SPAN, 2 * SPAN, ff):
            spans.append(pl.ds(at, size))
            at += size

    def pack(k):
        l, part_index = k // 5, k % 5
        at = l * per

        def put(start, value):
            w_ref[x, y, c, :, start : start + value.shape[1]] = value.astype(BF)

        if part_index == 0:
            for j in range(3):
                put(at + (0, 2, 1)[j] * ch, entry_ref[l, j])
        elif part_index == 4:
            put(at + 4 * ch + 2 * ff, down_ref[l])
        else:
            if part_index == 1:
                put(at + 3 * ch, exit_ref[l])
            j = part_index - 1
            for half_index in range(2):
                put(
                    at + 4 * ch + (2 * j + half_index) * SPAN,
                    gate_ref[l, half_index, :, j * SPAN : (j + 1) * SPAN],
                )

    class Weights:
        def __init__(self, k):
            self.k, self.where, self.stage = k, spans[k], 0

        def block(self, uu, vv, r=slice(None)):
            px, py = place(uu, vv)
            return w_ref.at[px, py, c, r, self.where]

        def move(self, ref, n, where):
            return send(ref, ref, w_send.at[self.k, n], w_recv.at[self.k, n], where)

        def move_row(self, vv, lo, hi, n, where):
            def make(core):
                ref = chunk_of(w_ref, core, vv, lo, hi, self.where)
                return ref, ref

            return send_either(make, w_send.at[self.k, n], w_recv.at[self.k, n], where)

        def direct(self, stage):
            if stage == 0:
                pack(self.k)
                self.got = [
                    self.move(self.block(u, v), n, where) for n, where in enumerate((u_over, u_next, u_prev))
                ]
            elif stage == 1:
                for copy in self.got:
                    copy.wait_recv()
                self.got = [
                    self.move_row(v, 0, 4, 4 + n, where) for n, where in enumerate((v_over, v_next, v_prev))
                ]
                self.p0 = self.move_row(v, 0, 4, 8, pair)
            elif stage == 2:
                for n, (copy, vv) in enumerate(zip(self.got[::-1], (vn, vp, vo))):
                    copy.wait_recv()
                    self.got[2 - n] = self.move_row(vv, 0, 4, 9 + n, pair)
            else:
                for copy in (self.p0, *self.got):
                    copy.wait_recv()
                self.stage = 6

        def step(self):
            stage, self.stage = self.stage, self.stage + 1
            if self.k < 2:
                self.direct(stage)
            elif stage == 0:
                pack(self.k)
                self.a0 = self.move(self.block(u, v), 0, u_next)
                self.a1 = self.move(self.block(u, v), 1, u_prev)
            elif stage == 1:
                self.a0.wait_recv()
                self.a2 = self.move(self.block(up, v, pl.ds(0, 16)), 2, u_next)
                self.a1.wait_recv()
                self.a3 = self.move(self.block(un, v, pl.ds(16, 16)), 3, u_prev)
            elif stage == 2:
                self.a2.wait_recv()
                self.a3.wait_recv()
                self.b0 = self.move_row(v, 0, 4, 4, v_next)
                self.b1 = self.move_row(v, 0, 4, 5, v_prev)
                self.p0 = self.move_row(v, 0, 4, 8, pair)
            elif stage == 3:
                self.b0.wait_recv()
                self.b2 = self.move_row(vp, 0, 2, 6, v_next)
                self.b1.wait_recv()
                self.b3 = self.move_row(vn, 2, 4, 7, v_prev)
                self.p1 = self.move_row(vp, 0, 4, 9, pair)
                self.p2 = self.move_row(vn, 0, 4, 10, pair)
            elif stage == 4:
                self.b2.wait_recv()
                self.b3.wait_recv()
                self.p3 = self.move_row(vo, 0, 4, 11, pair)
            else:
                for copy in (self.p0, self.p1, self.p2, self.p3):
                    copy.wait_recv()

    class Sums:
        def __init__(self, l, k, where):
            self.l, self.k, self.where, self.stage = l, k, where, 0
            self.total = pl.ds(l * per + where.start, where.size)
            self.first = l == layers - 1
            self.due = 0
            self.sent = []

        def send(self, src, dst, n, where):
            copy = pltpu.make_async_remote_copy(
                src_ref=src,
                dst_ref=dst,
                send_sem=g_send.at[self.l, self.k, n],
                recv_sem=g_recv.at[self.l, self.k, n],
                device_id=where,
                device_id_type=MESH,
            )
            copy.start()
            self.sent.append(copy)
            return copy

        def far(self, vv, lo, n, where):
            def make(core):
                return chunk_of(gw_ref, core, vv, lo, lo + 2, self.where), from_far.at[n - 1, :, :, self.where]

            copy = send_either(make, g_send.at[self.l, self.k, n], g_recv.at[self.l, self.k, n], where, self.sent)
            return copy

        def near(self, uu, r, n, where):
            px, py = place(uu, v)
            return self.send(gw_ref.at[px, py, c, r, self.where], from_near.at[n - 7, :, self.where], n, where)

        def add_far(self, vv, lo, slots):
            for i in range(2):
                px, py = place(lo + i, vv)
                value = gw_ref[px, py, c, :, self.where].astype(F32)
                for slot in slots:
                    value += from_far[slot, i, :, self.where].astype(F32)
                gw_ref[px, py, c, :, self.where] = value.astype(BF)

        def add_near(self, uu, r, slots):
            px, py = place(uu, v)
            value = gw_ref[px, py, c, r, self.where].astype(F32)
            for slot in slots:
                value += from_near[slot, :, self.where].astype(F32)
            return value

        def allow(self, kind, devices):
            if self.first:
                for where in devices:
                    pl.semaphore_signal(credit.at[self.k, kind], inc=1, device_id=where, device_id_type=MESH)

        def ask(self, kind, count):
            if not self.first:
                pl.semaphore_wait(credit.at[self.k, kind], count)

        def add_pair(self):
            self.q.wait_recv()

            @pl.loop(0, 4)
            def _(i):
                gw_ref[i, :, c, :, self.where] = (
                    gw_ref[i, :, c, :, self.where].astype(F32) + from_pair[i, :, :, self.where].astype(F32)
                ).astype(BF)

        def direct(self, stage, upper, lower):
            if stage == 1:
                self.add_pair()
                self.ask(1, 3)
                pairs = ((vo, v_over), (vn, v_next), (vp, v_prev))
                self.got = [
                    self.far(vv, 2 * k, 1 + 2 * n + k, where) for n, (vv, where) in enumerate(pairs) for k in (0, 1)
                ]
            elif stage == 2:
                for copy in self.got:
                    copy.wait_recv()
                self.add_far(v, 0, [0, 2, 4])
                self.add_far(v, 2, [1, 3, 5])
                self.ask(2, 3)
                pairs = ((uo, u_over), (un, u_next), (up, u_prev))
                self.got = [
                    self.near(uu, r, 7 + 2 * n + k, where)
                    for n, (uu, where) in enumerate(pairs)
                    for k, r in enumerate((upper, lower))
                ]
            else:
                for copy in self.got:
                    copy.wait_recv()
                final_ref[0:16, self.total] = self.add_near(u, upper, [0, 2, 4])
                final_ref[16:32, self.total] = self.add_near(u, lower, [1, 3, 5])
                for copy in self.sent:
                    copy.wait_send()
                self.stage = 6

        def step(self):
            stage, self.stage = self.stage, self.stage + 1
            upper, lower = pl.ds(0, 16), pl.ds(16, 16)
            if self.l == 0 and self.k == 0 and stage > 0:
                self.direct(stage, upper, lower)
            elif stage == 0:
                self.ask(0, 1)
                self.q = self.send(
                    gw_ref.at[:, :, 1 - c, :, self.where], from_pair.at[:, :, :, self.where], 0, pair
                )
            elif stage == 1:
                self.add_pair()
                self.allow(0, [pair])
                self.ask(1, 2)
                self.f0 = self.far(vo, 0, 1, v_next)
                self.f1 = self.far(vo, 2, 2, v_prev)
                self.f2 = self.far(vn, 2, 3, v_next)
                self.f3 = self.far(vp, 0, 4, v_prev)
            elif stage == 2:
                self.f0.wait_recv()
                self.add_far(vn, 0, [0])
                self.f4 = self.far(vn, 0, 5, v_next)
                self.f1.wait_recv()
                self.add_far(vp, 2, [1])
                self.f5 = self.far(vp, 2, 6, v_prev)
            elif stage == 3:
                for copy in (self.f2, self.f3, self.f4, self.f5):
                    copy.wait_recv()
                self.add_far(v, 0, [3, 4])
                self.add_far(v, 2, [2, 5])
                self.allow(1, [v_next, v_prev, v_over] if self.k == 0 else [v_next, v_prev])
                self.ask(2, 2)
                self.n0 = self.near(uo, upper, 7, u_next)
                self.n1 = self.near(uo, lower, 8, u_prev)
                self.n2 = self.near(un, lower, 9, u_next)
                self.n3 = self.near(up, upper, 10, u_prev)
            elif stage == 4:
                self.n0.wait_recv()
                px, py = place(un, v)
                gw_ref[px, py, c, upper, self.where] = self.add_near(un, upper, [0]).astype(BF)
                self.n4 = self.near(un, upper, 11, u_next)
                self.n1.wait_recv()
                px, py = place(up, v)
                gw_ref[px, py, c, lower, self.where] = self.add_near(up, lower, [1]).astype(BF)
                self.n5 = self.near(up, lower, 12, u_prev)
            else:
                for copy in (self.n2, self.n3, self.n4, self.n5):
                    copy.wait_recv()
                final_ref[0:16, self.total] = self.add_near(u, upper, [3, 4])
                final_ref[16:32, self.total] = self.add_near(u, lower, [2, 5])
                self.allow(2, [u_next, u_prev, u_over] if self.k == 0 else [u_next, u_prev])
                for copy in self.sent:
                    copy.wait_send()

    fetches = [Weights(k) for k in range(len(spans))]
    fetched = [0]
    sums = []

    def tick():
        t = fetched[0]
        fetched[0] += 1
        for k, fetch in enumerate(fetches):
            if fetch.stage == 0 and t >= k + PACE[0]:
                fetch.step()
        for k, fetch in enumerate(fetches):
            if 0 < fetch.stage < 6 and t >= k + PACE[fetch.stage]:
                fetch.step()
        for total in sums:
            if total.stage < 6 and (t >= total.due or total.l + total.k == 0):
                total.due = t + 2
                total.step()

    def need(l, part_index):
        fetch = fetches[5 * l + part_index]
        while fetch.stage < 6:
            fetch.step()

    def ready(l, k, at, size):
        total = Sums(l, k, pl.ds(at, size))
        total.step()
        sums.append(total)

    def clear(k):
        for total in sums:
            if total.k == k:
                while total.stage < 6:
                    tick()

    def weight(where):
        return w_ref[:, :, :, :, where].reshape(width, where.size)

    def weight_rows(who, where):
        return w_ref[who, :, :, :, where].reshape(ch, where.size)

    tick()

    class Gather:
        def __init__(self, i, block):
            rows[i, :, cols(z)] = block
            mine = rows.at[i, :, cols(z)]
            self.got = [
                send(mine, mine, ag_send.at[i, k], ag_recv.at[i, k], (s, who)) for k, who in enumerate((zo, zr, zl))
            ]

        def finish(self):
            for copy in self.got:
                copy.wait_recv()

    class Scatter:
        def __init__(self, i, piece, lo=0, hi=tokens):
            self.i, self.piece, self.got = i, piece, []
            self.give(lo, hi, 0)

        def give(self, lo, hi, at):
            i = self.i
            for k, who in enumerate((zo, zr, zl)):
                stage[i, k, lo:hi] = self.piece(who, lo, hi).astype(BF)
                here, there = stage.at[i, k, pl.ds(lo, hi - lo)], landed.at[i, k, pl.ds(lo, hi - lo)]
                self.got.append(send(here, there, rs_send.at[i, at + k], rs_recv.at[i, at + k], (s, who)))
            part[lo:hi] = self.piece(z, lo, hi)

        def finish(self):
            for copy in self.got:
                copy.wait_recv()
            i = self.i
            return part[...] + landed[i, 0].astype(F32) + landed[i, 1].astype(F32) + landed[i, 2].astype(F32)

    class Total:
        def __init__(self, i, sums):
            self.i = i
            stats[i, z] = jnp.broadcast_to(sums, (tokens, 128)).T[0:8]
            there = stats.at[i, z]
            self.got = [
                send(there, there, st_send.at[i, k], st_recv.at[i, k], (s, who))
                for k, who in enumerate((zr, zl, zo))
            ]

        def finish(self):
            for copy in self.got:
                copy.wait_recv()
            i = self.i
            total = stats[i, 0] + stats[i, 1] + stats[i, 2] + stats[i, 3]
            return as_column(total[0:1])

    def row_sum(value):
        return jnp.sum(value, axis=1, keepdims=True)

    def columns(at, j, size=SPAN):
        return pl.ds(at + j * size, size)

    def turn(left_index, k=None):
        if k is None:
            turned[...] = rows[left_index].T
        else:
            turned[...] = (rows[left_index].astype(F32) * scales[k][:, 0:1]).astype(BF).T

    def weight_grad(l, k, right_ref, lead, start, size, at):
        clear(k)
        piece = nn(turned[...], right_ref[lead, :, start : start + size]).astype(BF)
        gw_ref[:, :, :, :, at : at + size] = piece.reshape(4, 4, 2, 32, size)

    def norm_scale(k, total, h):
        scale = lax.rsqrt(total.finish() / width + EPS)
        scales[k] = jnp.broadcast_to(scale, (tokens, 128))
        normed[k] = h * scale
        return scale

    def norm_backward(k, dn, inner, gain, small_row):
        a = normed[k]
        small_ref[pl.ds(small_row, 1), :] = jnp.sum(dn * a, axis=0, keepdims=True)
        return scales[k][:, 0:1] * (dn * gain - a * (inner / width))

    small_ref[...] = jnp.zeros_like(small_ref)
    hidden = x_ref[...]
    cot_gather = None
    for l in range(layers):
        base = l * per
        at_exit, at_gate, at_down = base + 3 * ch, base + 4 * ch, base + 4 * ch + 2 * ff
        gather = Gather(2 * l, (hidden * gain_ref[l, 0:1]).astype(BF))
        total = Total(2 * l, row_sum(hidden * hidden))
        if l == 0:
            cot_gather = Gather(2 * layers + 2 * (layers - 1), cot_ref[...].astype(BF))
        tick()
        tick()
        gather.finish()
        scale = norm_scale(2 * l, total, hidden)
        need(l, 0)
        full = rows[2 * l]
        bm = nn(full, weight(columns(base, 0, ch))) * scale
        xm = nn(full, weight(columns(base, 1, ch))) * scale
        bx = bm * xm
        ext[l, 8:] = bx
        tail = send(
            ext.at[l, pl.ds(tokens, 8)], ext.at[l, pl.ds(0, 8)], halo_send.at[l], halo_recv.at[l], (after, z)
        )
        bcx[l, 0] = bm
        bcx[l, 2] = xm
        tick()
        cm = nn(full, weight(columns(base, 2, ch))) * scale
        bcx[l, 1] = cm
        k = [kern_ref[j, l : l + 1] for j in range(3)]

        def mix(lo, hi, l=l, k=k):
            zc = sum(k[j] * ext[l, 6 + j + lo : 6 + j + hi] for j in range(3))
            conv[l, lo:hi] = zc
            gated[l, lo:hi] = (bcx[l, 1, lo:hi] * zc).astype(BF)

        def exit_piece(who, lo, hi, l=l, at=at_exit):
            return nt(gated[l, lo:hi], weight_rows(who, columns(at, 0, ch)))

        mix(16, tokens)
        need(l, 1)
        scatter = Scatter(2 * l, exit_piece, 16)
        tail.wait_recv()
        head = ext[l, 0:8]
        ext[l, 0:8] = jnp.where(s > 0, head, jnp.zeros_like(head))
        mix(0, 16)
        scatter.give(0, 16, 3)
        tick()
        tick()
        mid = hidden + scatter.finish()
        gather = Gather(2 * l + 1, (mid * gain_ref[l, 1:2]).astype(BF))
        total = Total(2 * l + 1, row_sum(mid * mid))
        tick()
        tick()
        gather.finish()
        scale = norm_scale(2 * l + 1, total, mid)
        need(l, 1)

        for j in range(ff // SPAN):
            need(l, 1 + j)
            tick()
            both = nn(rows[2 * l + 1], weight(columns(at_gate, j, 2 * SPAN))) * scale
            gates[l, :, j * 2 * SPAN : (j + 1) * 2 * SPAN] = both
            g, up_value = both[:, :SPAN], both[:, SPAN:]
            acted[l, :, j * SPAN : (j + 1) * SPAN] = (g * jax.nn.sigmoid(g) * up_value).astype(BF)

        def down_piece(who, lo, hi, l=l, at=at_down):
            return nt(acted[l], weight_rows(who, columns(at, 0, ff)))

        need(l, 4)
        scatter = Scatter(2 * l + 1, down_piece)
        tick()
        tick()
        hidden = mid + scatter.finish()
    out_ref[...] = hidden

    grad = cot_ref[...]
    for l in reversed(range(layers)):
        base = l * per
        at_exit, at_gate, at_down = base + 3 * ch, base + 4 * ch, base + 4 * ch + 2 * ff
        ie = 2 * layers + 2 * l
        if l == layers - 1:
            gather = cot_gather
        else:
            gather = Gather(ie, grad.astype(BF))
            tick()
            tick()
        gather.finish()

        inner = jnp.zeros((tokens, 1), F32)
        for j in range(ff // SPAN):
            ds = nn(rows[ie], weight(columns(at_down, j)))
            g = gates[l, :, j * 2 * SPAN : j * 2 * SPAN + SPAN]
            up_value = gates[l, :, j * 2 * SPAN + SPAN : (j + 1) * 2 * SPAN]
            sig = jax.nn.sigmoid(g)
            dg = (ds * up_value * sig * (1.0 + g * (1.0 - sig))).astype(BF)
            du = (ds * (g * sig)).astype(BF)
            dgates[0, :, j * 2 * SPAN : j * 2 * SPAN + SPAN] = dg
            dgates[0, :, j * 2 * SPAN + SPAN : (j + 1) * 2 * SPAN] = du
            inner += row_sum(dg.astype(F32) * g + du.astype(F32) * up_value)
        total = Total(2 * layers + 2 * l + 1, inner)

        def norm2_piece(who, lo, hi, at_gate=at_gate):
            return nt(dgates[0], weight_rows(who, columns(at_gate, 0, 2 * ff)))

        scatter = Scatter(2 * layers + 2 * l, norm2_piece)
        turn(ie)
        weight_grad(l, 4, acted, l, 0, ff, 4 * ch + 2 * ff)
        ready(l, 4, 4 * ch + 2 * ff, ff)
        turn(2 * l + 1, 2 * l + 1)
        for j in range(ff // SPAN):
            weight_grad(l, 1 + j, dgates, 0, j * 2 * SPAN, 2 * SPAN, 4 * ch + j * 2 * SPAN)
            ready(l, 1 + j, 4 * ch + j * 2 * SPAN, 2 * SPAN)
        dn2 = scatter.finish()
        dmid = grad + norm_backward(2 * l + 1, dn2, total.finish(), gain_ref[l, 1:2], 3 * layers + 2 * l + 1)
        gather = Gather(ie + 1, dmid.astype(BF))
        tick()
        tick()
        gather.finish()
        dy = nn(rows[ie + 1], weight(columns(at_exit, 0, ch)))
        dz = dy * bcx[l, 1]
        dext[l, :tokens] = dz
        tail = send(
            dext.at[l, pl.ds(0, 8)],
            dext.at[l, pl.ds(tokens, 8)],
            halo_send.at[layers + l],
            halo_recv.at[layers + l],
            (before, z),
        )
        dproj[0, :, 2 * ch :] = (dy * conv[l]).astype(BF)
        k = [kern_ref[j, l : l + 1] for j in range(3)]

        def unmix(lo, hi, l=l, k=k):
            dbx = sum(k[2 - j] * dext[l, lo + j : hi + j] for j in range(3))
            db = (dbx * bcx[l, 2, lo:hi]).astype(BF)
            dx = (dbx * bcx[l, 0, lo:hi]).astype(BF)
            dproj[0, lo:hi, :ch] = db
            dproj[0, lo:hi, ch : 2 * ch] = dx
            dc = dproj[0, lo:hi, 2 * ch :].astype(F32)
            return row_sum(
                db.astype(F32) * bcx[l, 0, lo:hi] + dc * bcx[l, 1, lo:hi] + dx.astype(F32) * bcx[l, 2, lo:hi]
            )

        def norm1_piece(who, lo, hi, base=base):
            return nt(dproj[0, lo:hi], weight_rows(who, columns(base, 0, 3 * ch)))

        late = tokens - 16
        inner = unmix(0, late)
        scatter = Scatter(2 * layers + 2 * l + 1, norm1_piece, 0, late)
        turn(ie + 1)
        weight_grad(l, 5, gated, l, 0, ch, 3 * ch)
        tail.wait_recv()
        last = dext[l, tokens:]
        dext[l, tokens:] = jnp.where(s < seqs - 1, last, jnp.zeros_like(last))
        inner = jnp.concatenate([inner, unmix(late, tokens)], axis=0)
        total = Total(2 * layers + 2 * l, inner)
        scatter.give(late, tokens, 3)
        for j in range(3):
            small_ref[pl.ds(j * layers + l, 1), :] = jnp.sum(
                dz * ext[l, 6 + j : 6 + j + tokens], axis=0, keepdims=True
            )
        turn(2 * l, 2 * l)
        if l == 0:
            weight_grad(l, 0, dproj, 0, 0, 2 * ch, 0)
            ready(l, 0, 0, 2 * ch)
        weight_grad(l, 5, dproj, 0, 2 * ch, ch, 2 * ch)
        ready(l, 5, 2 * ch, 2 * ch)
        if l > 0:
            weight_grad(l, 0, dproj, 0, 0, 2 * ch, 0)
            ready(l, 0, 0, 2 * ch)
        tick()
        tick()
        dn1 = scatter.finish()
        grad = dmid + norm_backward(2 * l, dn1, total.finish(), gain_ref[l, 0:1], 3 * layers + 2 * l)
    din_ref[...] = grad
    tally[0, 2 * x + c] = small_ref[...]
    slot = tally.at[0, 2 * x + c]
    near_by = [(lax.rem(x + k // 2, 4) * 8 + y * 2 + lax.rem(c + k, 2), z) for k in range(1, 8)]
    copies = [send(slot, slot, t_send.at[k], t_recv.at[k], where) for k, where in enumerate(near_by)]
    tick()
    for copy in copies:
        copy.wait_recv()
    tally[1, y] = sum((tally[0, k] for k in range(1, 8)), tally[0, 0])
    slot = tally.at[1, y]
    copies = [
        send(slot, slot, t_send.at[6 + k], t_recv.at[6 + k], (x * 8 + lax.rem(y + k, 4) * 2 + c, z)) for k in (1, 2, 3)
    ]
    tick()
    for copy in copies:
        copy.wait_recv()
    small_ref[...] = tally[1, 0] + tally[1, 1] + tally[1, 2] + tally[1, 3]
    while any(total.stage < 6 for total in sums):
        tick()
    for copy in pending:
        copy.wait_send()


def run_step(x, cot, weights, kern, gain, seqs):
    taps, layers, ch = kern.shape
    tokens = x.shape[0]
    width = 4 * ch
    ff = weights[2].shape[3]
    per = 4 * ch + 3 * ff
    n = 4 * layers
    vmem = pl.BlockSpec(memory_space=pltpu.VMEM)
    dma = pltpu.SemaphoreType.DMA
    return pl.pallas_call(
        functools.partial(step_kernel, (layers, seqs, tokens, ch, ff)),
        out_shape=(
            jax.ShapeDtypeStruct((tokens, ch), F32),
            jax.ShapeDtypeStruct((tokens, ch), F32),
            jax.ShapeDtypeStruct((32, layers * per), F32),
            jax.ShapeDtypeStruct((16, ch), F32),
        ),
        in_specs=[vmem] * 8,
        out_specs=(vmem,) * 4,
        scratch_shapes=[
            pltpu.VMEM((n, tokens, width), BF),
            pltpu.VMEM((tokens, ch), F32),
            pltpu.VMEM((n, 3, tokens, ch), BF),
            pltpu.VMEM((n, 3, tokens, ch), BF),
            pltpu.VMEM((n, 4, 8, tokens), F32),
            pltpu.VMEM((2 * layers, tokens, ch), F32),
            pltpu.VMEM((2 * layers, tokens, 128), F32),
            pltpu.VMEM((layers, tokens + 8, ch), F32),
            pltpu.VMEM((layers, tokens + 8, ch), F32),
            pltpu.VMEM((layers, 3, tokens, ch), F32),
            pltpu.VMEM((layers, tokens, ch), F32),
            pltpu.VMEM((layers, tokens, ch), BF),
            pltpu.VMEM((layers, tokens, 2 * ff), F32),
            pltpu.VMEM((layers, tokens, ff), BF),
            pltpu.VMEM((1, tokens, 2 * ff), BF),
            pltpu.VMEM((1, tokens, 3 * ch), BF),
            pltpu.VMEM((width, tokens), BF),
            pltpu.VMEM((4, 4, 2, 32, layers * per), BF),
            pltpu.VMEM((4, 4, 2, 32, per), BF),
            pltpu.VMEM((4, 4, 32, per), BF),
            pltpu.VMEM((6, 2, 32, per), BF),
            pltpu.VMEM((6, 16, per), BF),
            pltpu.VMEM((2, 8, 16, ch), F32),
            dma((n, 3)),
            dma((n, 3)),
            dma((n, 6)),
            dma((n, 6)),
            dma((n, 3)),
            dma((n, 3)),
            dma((2 * layers,)),
            dma((2 * layers,)),
            dma((5 * layers, 12)),
            dma((5 * layers, 12)),
            dma((layers, 6, 13)),
            dma((layers, 6, 13)),
            dma((10,)),
            dma((10,)),
            pltpu.SemaphoreType.REGULAR((6, 3)),
        ],
        compiler_params=pltpu.CompilerParams(
            collective_id=0, has_side_effects=True, vmem_limit_bytes=67043328
        ),
        name="layers",
    )(x, cot, *weights, kern, gain)


def adamw(weight, grad, first, second, rate, decay):
    first_new = 0.9 * first + 0.1 * grad
    second_new = 0.999 * second + 0.001 * grad * grad
    update = first_new / (1.0 - 0.9**STEP) / (jnp.sqrt(second_new / (1.0 - 0.999**STEP)) + 1e-08)
    return (weight - rate * (update + decay * weight), first_new, second_new)


def update_kernel(cfg, *refs):
    ch, ff = cfg
    ins, outs = refs[:22], refs[22:]
    flat, small, hidden, grad = ins[:4]
    entry, leave, gates, down, kern, gain = ins[4:10]
    moments = ins[10:]
    outs[0][...] = hidden[...]
    outs[1][...] = grad[...]
    at_gate = 4 * ch
    pieces = (
        [(0, (0, c), flat[:, k * ch : (k + 1) * ch]) for c, k in enumerate((0, 2, 1))]
        + [(1, (0,), flat[:, 3 * ch : 4 * ch])]
        + [
            (
                2,
                (0, k, slice(None), slice(j * SPAN, (j + 1) * SPAN)),
                flat[:, at_gate + (2 * j + k) * SPAN : at_gate + (2 * j + k + 1) * SPAN],
            )
            for k in range(2)
            for j in range(ff // SPAN)
        ]
        + [(3, (0,), flat[:, at_gate + 2 * ff : at_gate + 3 * ff])]
        + [(4, (j,), small[2 * j : 2 * j + 2]) for j in range(3)]
        + [(5, (l,), small[6 + 2 * l : 8 + 2 * l]) for l in range(2)]
    )
    for n, where, value in pieces:
        rate, decay = (0.01, 0.1) if n < 4 else (0.2, 0.0)
        new = adamw(ins[4 + n][where], value, moments[2 * n][where], moments[2 * n + 1][where], rate, decay)
        outs[2 + n][where] = value
        outs[8 + n][where] = new[0]
        outs[14 + 2 * n][where] = new[1]
        outs[15 + 2 * n][where] = new[2]


def run_update(flat, small, hidden, grad, params, moments):
    layers, _, rows, ch = params[0].shape
    ff = params[2].shape[3]
    per = flat.shape[1] // layers

    def whole(a):
        return pl.BlockSpec(a.shape, lambda l, n=a.ndim: (0,) * n)

    def layer(a):
        return pl.BlockSpec((1, *a.shape[1:]), lambda l, n=a.ndim: (l,) + (0,) * (n - 1))

    def spec(n, a):
        return layer(a) if n < 4 else whole(a)

    each = [spec(n, a) for n, a in enumerate(params)]
    token = pl.BlockSpec((hidden.shape[0] // layers, hidden.shape[1]), lambda l: (l, 0))
    twice = [e for e in each for _ in range(2)]
    shapes = [jax.ShapeDtypeStruct(a.shape, F32) for a in params]
    two = [e for e in shapes for _ in range(2)]
    token_shape = jax.ShapeDtypeStruct(hidden.shape, F32)
    return pl.pallas_call(
        functools.partial(update_kernel, (ch, ff)),
        grid=(layers,),
        out_shape=(token_shape, token_shape, *shapes, *shapes, *two),
        in_specs=[pl.BlockSpec((rows, per), lambda l: (0, l)), whole(small), token, token, *each, *twice],
        out_specs=(token, token, *each, *each, *twice),
        name="update",
    )(flat, small, hidden, grad, *params, *moments)


def per_device(
    inputs,
    cotangent,
    entry_weight,
    exit_weight,
    gate_up,
    down_weight,
    conv_kernel,
    norm_gain,
    entry_first,
    entry_second,
    exit_first,
    exit_second,
    gate_first,
    gate_second,
    down_first,
    down_second,
    kernel_first,
    kernel_second,
    gain_first,
    gain_second,
):
    layers, _, _, ch = entry_weight.shape
    ff = gate_up.shape[3]
    seqs = lax.axis_size("seq")
    weights = (entry_weight, jnp.swapaxes(exit_weight, 1, 2), gate_up, jnp.swapaxes(down_weight, 1, 2))
    hidden, grad, summed, small = run_step(inputs, cotangent, weights, jnp.swapaxes(conv_kernel, 0, 1), norm_gain, seqs)
    flip = lambda a: jnp.swapaxes(a, 1, 2)
    spin = lambda a: jnp.swapaxes(a, 0, 1)
    keep = lambda a: a
    turns = (keep, flip, keep, flip, spin, keep)
    params = (entry_weight, exit_weight, gate_up, down_weight, conv_kernel, norm_gain)
    moments = (
        entry_first,
        entry_second,
        exit_first,
        exit_second,
        gate_first,
        gate_second,
        down_first,
        down_second,
        kernel_first,
        kernel_second,
        gain_first,
        gain_second,
    )
    twice = [t for t in turns for _ in range(2)]
    done = run_update(
        summed,
        small,
        hidden,
        grad,
        [t(a) for t, a in zip(turns, params)],
        [t(a) for t, a in zip(twice, moments)],
    )
    return tuple(t(a) for t, a in zip((keep, keep, *turns, *turns, *twice), done))


def solution(mesh):
    tokens, rows, columns, replicated = (
        P("seq", "tp"),
        P(None, None, "seq", "tp"),
        P(None, "tp", "seq"),
        P(None, None, "tp"),
    )
    matrices = (rows, columns, rows, columns)
    moments = (rows, rows, columns, columns, rows, rows, columns, columns)
    return jax.shard_map(
        per_device,
        mesh=mesh,
        in_specs=(tokens, tokens, *matrices, replicated, replicated, *moments, *([replicated] * 4)),
        out_specs=(
            tokens,
            tokens,
            *matrices,
            replicated,
            replicated,
            *matrices,
            replicated,
            replicated,
            *moments,
            *([replicated] * 4),
        ),
        check_vma=False,
    )
```

```python
import functools

import jax
import jax.numpy as jnp
from jax import lax
from jax.experimental import pallas as pl
from jax.experimental.pallas import tpu as pltpu
from jax.sharding import PartitionSpec as P

STEP = 4
EPS = 1e-06
MESH = pl.DeviceIdType.MESH
BF = jnp.bfloat16
F32 = jnp.float32
SPAN = 384
PACE = (-2, 0, 1, 3, 5, 6)


def nn(a, b):
    return lax.dot_general(a, b, (((1,), (0,)), ((), ())), preferred_element_type=F32)


def nt(a, b):
    return lax.dot_general(a, b, (((1,), (1,)), ((), ())), preferred_element_type=F32)


def as_column(row):
    return jnp.broadcast_to(row, (128, row.shape[1])).T[:, 0:1]


def step_kernel(
    cfg,
    x_ref,
    cot_ref,
    entry_ref,
    exit_ref,
    gate_ref,
    down_ref,
    kern_ref,
    gain_ref,
    out_ref,
    din_ref,
    final_ref,
    small_ref,
    rows,
    part,
    stage,
    landed,
    stats,
    normed,
    scales,
    ext,
    dext,
    bcx,
    conv,
    gated,
    gates,
    acted,
    dgates,
    dproj,
    turned,
    w_ref,
    gw_ref,
    from_pair,
    from_far,
    from_near,
    tally,
    ag_send,
    ag_recv,
    rs_send,
    rs_recv,
    st_send,
    st_recv,
    halo_send,
    halo_recv,
    w_send,
    w_recv,
    g_send,
    g_recv,
    t_send,
    t_recv,
    credit,
):
    layers, seqs, tokens, ch, ff = cfg
    width = 4 * ch
    per = 4 * ch + 3 * ff
    z = lax.axis_index("tp")
    s = lax.axis_index("seq")
    zr, zl, zo = lax.rem(z + 1, 4), lax.rem(z + 3, 4), lax.rem(z + 2, 4)
    after, before = lax.rem(s + 1, seqs), lax.rem(s + seqs - 1, seqs)

    c = lax.rem(s, 2)
    x, y = lax.div(s, 8), lax.rem(lax.div(s, 2), 4)
    u, v = x * (1 - c) + y * c, y * (1 - c) + x * c

    def place(uu, vv):
        return uu * (1 - c) + vv * c, vv * (1 - c) + uu * c

    def device(uu, vv):
        px, py = place(uu, vv)
        return (px * 8 + py * 2 + c, z)

    up, un, uo = lax.rem(u + 3, 4), lax.rem(u + 1, 4), lax.rem(u + 2, 4)
    vp, vn, vo = lax.rem(v + 3, 4), lax.rem(v + 1, 4), lax.rem(v + 2, 4)
    u_next, u_prev, v_next, v_prev = device(un, v), device(up, v), device(u, vn), device(u, vp)
    u_over, v_over = device(uo, v), device(u, vo)
    pair = (s + 1 - 2 * c, z)

    barrier = pltpu.get_barrier_semaphore()
    partners = [(s, zr), (s, zl), (s, zo), (after, z), (before, z), u_next, u_prev, v_next, v_prev, pair]
    partners += [u_over, v_over]
    partners += [(lax.rem(x + k, 4) * 8 + y * 2 + 1 - c, z) for k in (1, 2, 3)]
    for where in partners:
        pl.semaphore_signal(barrier, inc=1, device_id=where, device_id_type=MESH)
    pl.semaphore_wait(barrier, len(partners))

    pending = []

    def send(src, dst, ssem, rsem, where):
        copy = pltpu.make_async_remote_copy(
            src_ref=src, dst_ref=dst, send_sem=ssem, recv_sem=rsem, device_id=where, device_id_type=MESH
        )
        copy.start()
        pending.append(copy)
        return copy

    def cols(who):
        return pl.ds(pl.multiple_of(who * ch, ch), ch)

    def own_rows(who):
        return pl.ds(pl.multiple_of(who * ch, ch), ch)

    def chunk_of(ref, lead, vv, lo, hi, where):
        if lead == 0:
            return ref.at[pl.ds(lo, hi - lo), vv, 0, :, where]
        return ref.at[vv, pl.ds(lo, hi - lo), 1, :, where]

    def send_either(make, ssem, rsem, where, held=pending):
        for core in (0, 1):

            @pl.when(c == core)
            def _(core=core):
                src, dst = make(core)
                pltpu.make_async_remote_copy(
                    src_ref=src, dst_ref=dst, send_sem=ssem, recv_sem=rsem, device_id=where, device_id_type=MESH
                ).start()

        src, dst = make(0)
        copy = pltpu.make_async_remote_copy(
            src_ref=src, dst_ref=dst, send_sem=ssem, recv_sem=rsem, device_id=where, device_id_type=MESH
        )
        held.append(copy)
        return copy

    spans = []
    for l in range(layers):
        at = l * per
        for size in (3 * ch, ch + 2 * SPAN, 2 * SPAN, 2 * SPAN, ff):
            spans.append(pl.ds(at, size))
            at += size

    def pack(k):
        l, part_index = k // 5, k % 5
        at = l * per

        def put(start, value):
            w_ref[x, y, c, :, start : start + value.shape[1]] = value.astype(BF)

        if part_index == 0:
            for j in range(3):
                put(at + (0, 2, 1)[j] * ch, entry_ref[l, j])
        elif part_index == 4:
            put(at + 4 * ch + 2 * ff, down_ref[l])
        else:
            if part_index == 1:
                put(at + 3 * ch, exit_ref[l])
            j = part_index - 1
            for half_index in range(2):
                put(
                    at + 4 * ch + (2 * j + half_index) * SPAN,
                    gate_ref[l, half_index, :, j * SPAN : (j + 1) * SPAN],
                )

    class Weights:
        def __init__(self, k):
            self.k, self.where, self.stage = k, spans[k], 0

        def block(self, uu, vv, r=slice(None)):
            px, py = place(uu, vv)
            return w_ref.at[px, py, c, r, self.where]

        def move(self, ref, n, where):
            return send(ref, ref, w_send.at[self.k, n], w_recv.at[self.k, n], where)

        def move_row(self, vv, lo, hi, n, where):
            def make(core):
                ref = chunk_of(w_ref, core, vv, lo, hi, self.where)
                return ref, ref

            return send_either(make, w_send.at[self.k, n], w_recv.at[self.k, n], where)

        def direct(self, stage):
            if stage == 0:
                pack(self.k)
                self.got = [
                    self.move(self.block(u, v), n, where) for n, where in enumerate((u_over, u_next, u_prev))
                ]
            elif stage == 1:
                for copy in self.got:
                    copy.wait_recv()
                self.got = [
                    self.move_row(v, 0, 4, 4 + n, where) for n, where in enumerate((v_over, v_next, v_prev))
                ]
                self.p0 = self.move_row(v, 0, 4, 8, pair)
            elif stage == 2:
                for n, (copy, vv) in enumerate(zip(self.got[::-1], (vn, vp, vo))):
                    copy.wait_recv()
                    self.got[2 - n] = self.move_row(vv, 0, 4, 9 + n, pair)
            else:
                for copy in (self.p0, *self.got):
                    copy.wait_recv()
                self.stage = 6

        def step(self):
            stage, self.stage = self.stage, self.stage + 1
            if self.k < 2:
                self.direct(stage)
            elif stage == 0:
                pack(self.k)
                self.a0 = self.move(self.block(u, v), 0, u_next)
                self.a1 = self.move(self.block(u, v), 1, u_prev)
            elif stage == 1:
                self.a0.wait_recv()
                self.a2 = self.move(self.block(up, v, pl.ds(0, 16)), 2, u_next)
                self.a1.wait_recv()
                self.a3 = self.move(self.block(un, v, pl.ds(16, 16)), 3, u_prev)
            elif stage == 2:
                self.a2.wait_recv()
                self.a3.wait_recv()
                self.b0 = self.move_row(v, 0, 4, 4, v_next)
                self.b1 = self.move_row(v, 0, 4, 5, v_prev)
                self.p0 = self.move_row(v, 0, 4, 8, pair)
            elif stage == 3:
                self.b0.wait_recv()
                self.b2 = self.move_row(vp, 0, 2, 6, v_next)
                self.b1.wait_recv()
                self.b3 = self.move_row(vn, 2, 4, 7, v_prev)
                self.p1 = self.move_row(vp, 0, 4, 9, pair)
                self.p2 = self.move_row(vn, 0, 4, 10, pair)
            elif stage == 4:
                self.b2.wait_recv()
                self.b3.wait_recv()
                self.p3 = self.move_row(vo, 0, 4, 11, pair)
            else:
                for copy in (self.p0, self.p1, self.p2, self.p3):
                    copy.wait_recv()

    class Sums:
        def __init__(self, l, k, where):
            self.l, self.k, self.where, self.stage = l, k, where, 0
            self.total = pl.ds(l * per + where.start, where.size)
            self.first = l == layers - 1
            self.due = 0
            self.sent = []

        def send(self, src, dst, n, where):
            copy = pltpu.make_async_remote_copy(
                src_ref=src,
                dst_ref=dst,
                send_sem=g_send.at[self.l, self.k, n],
                recv_sem=g_recv.at[self.l, self.k, n],
                device_id=where,
                device_id_type=MESH,
            )
            copy.start()
            self.sent.append(copy)
            return copy

        def far(self, vv, lo, n, where):
            def make(core):
                return chunk_of(gw_ref, core, vv, lo, lo + 2, self.where), from_far.at[n - 1, :, :, self.where]

            copy = send_either(make, g_send.at[self.l, self.k, n], g_recv.at[self.l, self.k, n], where, self.sent)
            return copy

        def near(self, uu, r, n, where):
            px, py = place(uu, v)
            return self.send(gw_ref.at[px, py, c, r, self.where], from_near.at[n - 7, :, self.where], n, where)

        def add_far(self, vv, lo, slots):
            for i in range(2):
                px, py = place(lo + i, vv)
                value = gw_ref[px, py, c, :, self.where].astype(F32)
                for slot in slots:
                    value += from_far[slot, i, :, self.where].astype(F32)
                gw_ref[px, py, c, :, self.where] = value.astype(BF)

        def add_near(self, uu, r, slots):
            px, py = place(uu, v)
            value = gw_ref[px, py, c, r, self.where].astype(F32)
            for slot in slots:
                value += from_near[slot, :, self.where].astype(F32)
            return value

        def allow(self, kind, devices):
            if self.first:
                for where in devices:
                    pl.semaphore_signal(credit.at[self.k, kind], inc=1, device_id=where, device_id_type=MESH)

        def ask(self, kind, count):
            if not self.first:
                pl.semaphore_wait(credit.at[self.k, kind], count)

        def add_pair(self):
            self.q.wait_recv()

            @pl.loop(0, 4)
            def _(i):
                gw_ref[i, :, c, :, self.where] = (
                    gw_ref[i, :, c, :, self.where].astype(F32) + from_pair[i, :, :, self.where].astype(F32)
                ).astype(BF)

        def direct(self, stage, upper, lower):
            if stage == 1:
                self.add_pair()
                self.ask(1, 3)
                pairs = ((vo, v_over), (vn, v_next), (vp, v_prev))
                self.got = [
                    self.far(vv, 2 * k, 1 + 2 * n + k, where) for n, (vv, where) in enumerate(pairs) for k in (0, 1)
                ]
            elif stage == 2:
                for copy in self.got:
                    copy.wait_recv()
                self.add_far(v, 0, [0, 2, 4])
                self.add_far(v, 2, [1, 3, 5])
                self.ask(2, 3)
                pairs = ((uo, u_over), (un, u_next), (up, u_prev))
                self.got = [
                    self.near(uu, r, 7 + 2 * n + k, where)
                    for n, (uu, where) in enumerate(pairs)
                    for k, r in enumerate((upper, lower))
                ]
            else:
                for copy in self.got:
                    copy.wait_recv()
                final_ref[0:16, self.total] = self.add_near(u, upper, [0, 2, 4])
                final_ref[16:32, self.total] = self.add_near(u, lower, [1, 3, 5])
                for copy in self.sent:
                    copy.wait_send()
                self.stage = 6

        def step(self):
            stage, self.stage = self.stage, self.stage + 1
            upper, lower = pl.ds(0, 16), pl.ds(16, 16)
            if self.l == 0 and self.k in (0, 5) and stage > 0:
                self.direct(stage, upper, lower)
            elif stage == 0:
                self.ask(0, 1)
                self.q = self.send(
                    gw_ref.at[:, :, 1 - c, :, self.where], from_pair.at[:, :, :, self.where], 0, pair
                )
            elif stage == 1:
                self.add_pair()
                self.allow(0, [pair])
                self.ask(1, 2)
                self.f0 = self.far(vo, 0, 1, v_next)
                self.f1 = self.far(vo, 2, 2, v_prev)
                self.f2 = self.far(vn, 2, 3, v_next)
                self.f3 = self.far(vp, 0, 4, v_prev)
            elif stage == 2:
                self.f0.wait_recv()
                self.add_far(vn, 0, [0])
                self.f4 = self.far(vn, 0, 5, v_next)
                self.f1.wait_recv()
                self.add_far(vp, 2, [1])
                self.f5 = self.far(vp, 2, 6, v_prev)
            elif stage == 3:
                for copy in (self.f2, self.f3, self.f4, self.f5):
                    copy.wait_recv()
                self.add_far(v, 0, [3, 4])
                self.add_far(v, 2, [2, 5])
                self.allow(1, [v_next, v_prev, v_over] if self.k in (0, 5) else [v_next, v_prev])
                self.ask(2, 2)
                self.n0 = self.near(uo, upper, 7, u_next)
                self.n1 = self.near(uo, lower, 8, u_prev)
                self.n2 = self.near(un, lower, 9, u_next)
                self.n3 = self.near(up, upper, 10, u_prev)
            elif stage == 4:
                self.n0.wait_recv()
                px, py = place(un, v)
                gw_ref[px, py, c, upper, self.where] = self.add_near(un, upper, [0]).astype(BF)
                self.n4 = self.near(un, upper, 11, u_next)
                self.n1.wait_recv()
                px, py = place(up, v)
                gw_ref[px, py, c, lower, self.where] = self.add_near(up, lower, [1]).astype(BF)
                self.n5 = self.near(up, lower, 12, u_prev)
            else:
                for copy in (self.n2, self.n3, self.n4, self.n5):
                    copy.wait_recv()
                final_ref[0:16, self.total] = self.add_near(u, upper, [3, 4])
                final_ref[16:32, self.total] = self.add_near(u, lower, [2, 5])
                self.allow(2, [u_next, u_prev, u_over] if self.k in (0, 5) else [u_next, u_prev])
                for copy in self.sent:
                    copy.wait_send()

    fetches = [Weights(k) for k in range(len(spans))]
    fetched = [0]
    sums = []

    def tick():
        t = fetched[0]
        fetched[0] += 1
        for k, fetch in enumerate(fetches):
            if fetch.stage == 0 and t >= k + PACE[0]:
                fetch.step()
        for k, fetch in enumerate(fetches):
            if 0 < fetch.stage < 6 and t >= k + PACE[fetch.stage]:
                fetch.step()
        for total in sums:
            if total.stage < 6 and (t >= total.due or (total.l == 0 and total.k in (0, 5))):
                total.due = t + 2
                total.step()

    def need(l, part_index):
        fetch = fetches[5 * l + part_index]
        while fetch.stage < 6:
            fetch.step()

    def ready(l, k, at, size):
        total = Sums(l, k, pl.ds(at, size))
        total.step()
        sums.append(total)

    def clear(k):
        for total in sums:
            if total.k == k:
                while total.stage < 6:
                    tick()

    def weight(where):
        return w_ref[:, :, :, :, where].reshape(width, where.size)

    def weight_rows(who, where):
        return w_ref[who, :, :, :, where].reshape(ch, where.size)

    tick()

    class Gather:
        def __init__(self, i, block):
            rows[i, :, cols(z)] = block
            mine = rows.at[i, :, cols(z)]
            self.got = [
                send(mine, mine, ag_send.at[i, k], ag_recv.at[i, k], (s, who)) for k, who in enumerate((zo, zr, zl))
            ]

        def finish(self):
            for copy in self.got:
                copy.wait_recv()

    class Scatter:
        def __init__(self, i, piece, lo=0, hi=tokens):
            self.i, self.piece, self.got = i, piece, []
            self.give(lo, hi, 0)

        def give(self, lo, hi, at):
            i = self.i
            for k, who in enumerate((zo, zr, zl)):
                stage[i, k, lo:hi] = self.piece(who, lo, hi).astype(BF)
                here, there = stage.at[i, k, pl.ds(lo, hi - lo)], landed.at[i, k, pl.ds(lo, hi - lo)]
                self.got.append(send(here, there, rs_send.at[i, at + k], rs_recv.at[i, at + k], (s, who)))
            part[lo:hi] = self.piece(z, lo, hi)

        def finish(self):
            for copy in self.got:
                copy.wait_recv()
            i = self.i
            return part[...] + landed[i, 0].astype(F32) + landed[i, 1].astype(F32) + landed[i, 2].astype(F32)

    class Total:
        def __init__(self, i, sums):
            self.i = i
            stats[i, z] = jnp.broadcast_to(sums, (tokens, 128)).T[0:8]
            there = stats.at[i, z]
            self.got = [
                send(there, there, st_send.at[i, k], st_recv.at[i, k], (s, who))
                for k, who in enumerate((zr, zl, zo))
            ]

        def finish(self):
            for copy in self.got:
                copy.wait_recv()
            i = self.i
            total = stats[i, 0] + stats[i, 1] + stats[i, 2] + stats[i, 3]
            return as_column(total[0:1])

    def row_sum(value):
        return jnp.sum(value, axis=1, keepdims=True)

    def columns(at, j, size=SPAN):
        return pl.ds(at + j * size, size)

    def turn(left_index, k=None):
        if k is None:
            turned[...] = rows[left_index].T
        else:
            turned[...] = (rows[left_index].astype(F32) * scales[k][:, 0:1]).astype(BF).T

    def weight_grad(l, k, right_ref, lead, start, size, at):
        clear(k)
        piece = nn(turned[...], right_ref[lead, :, start : start + size]).astype(BF)
        gw_ref[:, :, :, :, at : at + size] = piece.reshape(4, 4, 2, 32, size)

    def norm_scale(k, total, h):
        scale = lax.rsqrt(total.finish() / width + EPS)
        scales[k] = jnp.broadcast_to(scale, (tokens, 128))
        normed[k] = h * scale
        return scale

    def norm_backward(k, dn, inner, gain, small_row):
        a = normed[k]
        small_ref[pl.ds(small_row, 1), :] = jnp.sum(dn * a, axis=0, keepdims=True)
        return scales[k][:, 0:1] * (dn * gain - a * (inner / width))

    small_ref[...] = jnp.zeros_like(small_ref)
    hidden = x_ref[...]
    cot_gather = None
    for l in range(layers):
        base = l * per
        at_exit, at_gate, at_down = base + 3 * ch, base + 4 * ch, base + 4 * ch + 2 * ff
        gather = Gather(2 * l, (hidden * gain_ref[l, 0:1]).astype(BF))
        total = Total(2 * l, row_sum(hidden * hidden))
        if l == 0:
            cot_gather = Gather(2 * layers + 2 * (layers - 1), cot_ref[...].astype(BF))
        tick()
        tick()
        gather.finish()
        scale = norm_scale(2 * l, total, hidden)
        need(l, 0)
        full = rows[2 * l]
        bm = nn(full, weight(columns(base, 0, ch))) * scale
        xm = nn(full, weight(columns(base, 1, ch))) * scale
        bx = bm * xm
        ext[l, 8:] = bx
        tail = send(
            ext.at[l, pl.ds(tokens, 8)], ext.at[l, pl.ds(0, 8)], halo_send.at[l], halo_recv.at[l], (after, z)
        )
        bcx[l, 0] = bm
        bcx[l, 2] = xm
        tick()
        cm = nn(full, weight(columns(base, 2, ch))) * scale
        bcx[l, 1] = cm
        k = [kern_ref[j, l : l + 1] for j in range(3)]

        def mix(lo, hi, l=l, k=k):
            zc = sum(k[j] * ext[l, 6 + j + lo : 6 + j + hi] for j in range(3))
            conv[l, lo:hi] = zc
            gated[l, lo:hi] = (bcx[l, 1, lo:hi] * zc).astype(BF)

        def exit_piece(who, lo, hi, l=l, at=at_exit):
            return nt(gated[l, lo:hi], weight_rows(who, columns(at, 0, ch)))

        mix(16, tokens)
        need(l, 1)
        scatter = Scatter(2 * l, exit_piece, 16)
        tail.wait_recv()
        head = ext[l, 0:8]
        ext[l, 0:8] = jnp.where(s > 0, head, jnp.zeros_like(head))
        mix(0, 16)
        scatter.give(0, 16, 3)
        tick()
        tick()
        mid = hidden + scatter.finish()
        gather = Gather(2 * l + 1, (mid * gain_ref[l, 1:2]).astype(BF))
        total = Total(2 * l + 1, row_sum(mid * mid))
        tick()
        tick()
        gather.finish()
        scale = norm_scale(2 * l + 1, total, mid)
        need(l, 1)

        for j in range(ff // SPAN):
            need(l, 1 + j)
            tick()
            both = nn(rows[2 * l + 1], weight(columns(at_gate, j, 2 * SPAN))) * scale
            gates[l, :, j * 2 * SPAN : (j + 1) * 2 * SPAN] = both
            g, up_value = both[:, :SPAN], both[:, SPAN:]
            acted[l, :, j * SPAN : (j + 1) * SPAN] = (g * jax.nn.sigmoid(g) * up_value).astype(BF)

        def down_piece(who, lo, hi, l=l, at=at_down):
            return nt(acted[l], weight_rows(who, columns(at, 0, ff)))

        need(l, 4)
        scatter = Scatter(2 * l + 1, down_piece)
        tick()
        tick()
        hidden = mid + scatter.finish()
    out_ref[...] = hidden

    grad = cot_ref[...]
    for l in reversed(range(layers)):
        base = l * per
        at_exit, at_gate, at_down = base + 3 * ch, base + 4 * ch, base + 4 * ch + 2 * ff
        ie = 2 * layers + 2 * l
        if l == layers - 1:
            gather = cot_gather
        else:
            gather = Gather(ie, grad.astype(BF))
            tick()
            tick()
        gather.finish()

        inner = jnp.zeros((tokens, 1), F32)
        for j in range(ff // SPAN):
            ds = nn(rows[ie], weight(columns(at_down, j)))
            g = gates[l, :, j * 2 * SPAN : j * 2 * SPAN + SPAN]
            up_value = gates[l, :, j * 2 * SPAN + SPAN : (j + 1) * 2 * SPAN]
            sig = jax.nn.sigmoid(g)
            dg = (ds * up_value * sig * (1.0 + g * (1.0 - sig))).astype(BF)
            du = (ds * (g * sig)).astype(BF)
            dgates[0, :, j * 2 * SPAN : j * 2 * SPAN + SPAN] = dg
            dgates[0, :, j * 2 * SPAN + SPAN : (j + 1) * 2 * SPAN] = du
            inner += row_sum(dg.astype(F32) * g + du.astype(F32) * up_value)
        total = Total(2 * layers + 2 * l + 1, inner)

        def norm2_piece(who, lo, hi, at_gate=at_gate):
            return nt(dgates[0], weight_rows(who, columns(at_gate, 0, 2 * ff)))

        scatter = Scatter(2 * layers + 2 * l, norm2_piece)
        turn(ie)
        weight_grad(l, 4, acted, l, 0, ff, 4 * ch + 2 * ff)
        ready(l, 4, 4 * ch + 2 * ff, ff)
        turn(2 * l + 1, 2 * l + 1)
        for j in range(ff // SPAN):
            weight_grad(l, 1 + j, dgates, 0, j * 2 * SPAN, 2 * SPAN, 4 * ch + j * 2 * SPAN)
            ready(l, 1 + j, 4 * ch + j * 2 * SPAN, 2 * SPAN)
        dn2 = scatter.finish()
        dmid = grad + norm_backward(2 * l + 1, dn2, total.finish(), gain_ref[l, 1:2], 3 * layers + 2 * l + 1)
        gather = Gather(ie + 1, dmid.astype(BF))
        tick()
        tick()
        gather.finish()
        dy = nn(rows[ie + 1], weight(columns(at_exit, 0, ch)))
        dz = dy * bcx[l, 1]
        dext[l, :tokens] = dz
        tail = send(
            dext.at[l, pl.ds(0, 8)],
            dext.at[l, pl.ds(tokens, 8)],
            halo_send.at[layers + l],
            halo_recv.at[layers + l],
            (before, z),
        )
        dproj[0, :, 2 * ch :] = (dy * conv[l]).astype(BF)
        k = [kern_ref[j, l : l + 1] for j in range(3)]

        def unmix(lo, hi, l=l, k=k):
            dbx = sum(k[2 - j] * dext[l, lo + j : hi + j] for j in range(3))
            db = (dbx * bcx[l, 2, lo:hi]).astype(BF)
            dx = (dbx * bcx[l, 0, lo:hi]).astype(BF)
            dproj[0, lo:hi, :ch] = db
            dproj[0, lo:hi, ch : 2 * ch] = dx
            dc = dproj[0, lo:hi, 2 * ch :].astype(F32)
            return row_sum(
                db.astype(F32) * bcx[l, 0, lo:hi] + dc * bcx[l, 1, lo:hi] + dx.astype(F32) * bcx[l, 2, lo:hi]
            )

        def norm1_piece(who, lo, hi, base=base):
            return nt(dproj[0, lo:hi], weight_rows(who, columns(base, 0, 3 * ch)))

        late = tokens - 16
        inner = unmix(0, late)
        scatter = Scatter(2 * layers + 2 * l + 1, norm1_piece, 0, late)
        turn(ie + 1)
        weight_grad(l, 5, gated, l, 0, ch, 3 * ch)
        tail.wait_recv()
        last = dext[l, tokens:]
        dext[l, tokens:] = jnp.where(s < seqs - 1, last, jnp.zeros_like(last))
        inner = jnp.concatenate([inner, unmix(late, tokens)], axis=0)
        total = Total(2 * layers + 2 * l, inner)
        scatter.give(late, tokens, 3)
        for j in range(3):
            small_ref[pl.ds(j * layers + l, 1), :] = jnp.sum(
                dz * ext[l, 6 + j : 6 + j + tokens], axis=0, keepdims=True
            )
        turn(2 * l, 2 * l)
        if l == 0:
            weight_grad(l, 0, dproj, 0, 0, 2 * ch, 0)
            ready(l, 0, 0, 2 * ch)
        weight_grad(l, 5, dproj, 0, 2 * ch, ch, 2 * ch)
        ready(l, 5, 2 * ch, 2 * ch)
        if l > 0:
            weight_grad(l, 0, dproj, 0, 0, 2 * ch, 0)
            ready(l, 0, 0, 2 * ch)
        tick()
        tick()
        dn1 = scatter.finish()
        grad = dmid + norm_backward(2 * l, dn1, total.finish(), gain_ref[l, 0:1], 3 * layers + 2 * l)
    din_ref[...] = grad
    tally[0, 2 * x + c] = small_ref[...]
    slot = tally.at[0, 2 * x + c]
    near_by = [(lax.rem(x + k // 2, 4) * 8 + y * 2 + lax.rem(c + k, 2), z) for k in range(1, 8)]
    copies = [send(slot, slot, t_send.at[k], t_recv.at[k], where) for k, where in enumerate(near_by)]
    tick()
    for copy in copies:
        copy.wait_recv()
    tally[1, y] = sum((tally[0, k] for k in range(1, 8)), tally[0, 0])
    slot = tally.at[1, y]
    copies = [
        send(slot, slot, t_send.at[6 + k], t_recv.at[6 + k], (x * 8 + lax.rem(y + k, 4) * 2 + c, z)) for k in (1, 2, 3)
    ]
    tick()
    for copy in copies:
        copy.wait_recv()
    small_ref[...] = tally[1, 0] + tally[1, 1] + tally[1, 2] + tally[1, 3]
    while any(total.stage < 6 for total in sums):
        tick()
    for copy in pending:
        copy.wait_send()


def run_step(x, cot, weights, kern, gain, seqs):
    taps, layers, ch = kern.shape
    tokens = x.shape[0]
    width = 4 * ch
    ff = weights[2].shape[3]
    per = 4 * ch + 3 * ff
    n = 4 * layers
    vmem = pl.BlockSpec(memory_space=pltpu.VMEM)
    dma = pltpu.SemaphoreType.DMA
    return pl.pallas_call(
        functools.partial(step_kernel, (layers, seqs, tokens, ch, ff)),
        out_shape=(
            jax.ShapeDtypeStruct((tokens, ch), F32),
            jax.ShapeDtypeStruct((tokens, ch), F32),
            jax.ShapeDtypeStruct((32, layers * per), F32),
            jax.ShapeDtypeStruct((16, ch), F32),
        ),
        in_specs=[vmem] * 8,
        out_specs=(vmem,) * 4,
        scratch_shapes=[
            pltpu.VMEM((n, tokens, width), BF),
            pltpu.VMEM((tokens, ch), F32),
            pltpu.VMEM((n, 3, tokens, ch), BF),
            pltpu.VMEM((n, 3, tokens, ch), BF),
            pltpu.VMEM((n, 4, 8, tokens), F32),
            pltpu.VMEM((2 * layers, tokens, ch), F32),
            pltpu.VMEM((2 * layers, tokens, 128), F32),
            pltpu.VMEM((layers, tokens + 8, ch), F32),
            pltpu.VMEM((layers, tokens + 8, ch), F32),
            pltpu.VMEM((layers, 3, tokens, ch), F32),
            pltpu.VMEM((layers, tokens, ch), F32),
            pltpu.VMEM((layers, tokens, ch), BF),
            pltpu.VMEM((layers, tokens, 2 * ff), F32),
            pltpu.VMEM((layers, tokens, ff), BF),
            pltpu.VMEM((1, tokens, 2 * ff), BF),
            pltpu.VMEM((1, tokens, 3 * ch), BF),
            pltpu.VMEM((width, tokens), BF),
            pltpu.VMEM((4, 4, 2, 32, layers * per), BF),
            pltpu.VMEM((4, 4, 2, 32, per), BF),
            pltpu.VMEM((4, 4, 32, per), BF),
            pltpu.VMEM((6, 2, 32, per), BF),
            pltpu.VMEM((6, 16, per), BF),
            pltpu.VMEM((2, 8, 16, ch), F32),
            dma((n, 3)),
            dma((n, 3)),
            dma((n, 6)),
            dma((n, 6)),
            dma((n, 3)),
            dma((n, 3)),
            dma((2 * layers,)),
            dma((2 * layers,)),
            dma((5 * layers, 12)),
            dma((5 * layers, 12)),
            dma((layers, 6, 13)),
            dma((layers, 6, 13)),
            dma((10,)),
            dma((10,)),
            pltpu.SemaphoreType.REGULAR((6, 3)),
        ],
        compiler_params=pltpu.CompilerParams(
            collective_id=0, has_side_effects=True, vmem_limit_bytes=67043328
        ),
        name="layers",
    )(x, cot, *weights, kern, gain)


def adamw(weight, grad, first, second, rate, decay):
    first_new = 0.9 * first + 0.1 * grad
    second_new = 0.999 * second + 0.001 * grad * grad
    update = first_new / (1.0 - 0.9**STEP) / (jnp.sqrt(second_new / (1.0 - 0.999**STEP)) + 1e-08)
    return (weight - rate * (update + decay * weight), first_new, second_new)


def update_kernel(cfg, *refs):
    ch, ff = cfg
    ins, outs = refs[:22], refs[22:]
    flat, small, hidden, grad = ins[:4]
    entry, leave, gates, down, kern, gain = ins[4:10]
    moments = ins[10:]
    outs[0][...] = hidden[...]
    outs[1][...] = grad[...]
    at_gate = 4 * ch
    pieces = (
        [(0, (0, c), flat[:, k * ch : (k + 1) * ch]) for c, k in enumerate((0, 2, 1))]
        + [(1, (0,), flat[:, 3 * ch : 4 * ch])]
        + [
            (
                2,
                (0, k, slice(None), slice(j * SPAN, (j + 1) * SPAN)),
                flat[:, at_gate + (2 * j + k) * SPAN : at_gate + (2 * j + k + 1) * SPAN],
            )
            for k in range(2)
            for j in range(ff // SPAN)
        ]
        + [(3, (0,), flat[:, at_gate + 2 * ff : at_gate + 3 * ff])]
        + [(4, (j,), small[2 * j : 2 * j + 2]) for j in range(3)]
        + [(5, (l,), small[6 + 2 * l : 8 + 2 * l]) for l in range(2)]
    )
    for n, where, value in pieces:
        rate, decay = (0.01, 0.1) if n < 4 else (0.2, 0.0)
        new = adamw(ins[4 + n][where], value, moments[2 * n][where], moments[2 * n + 1][where], rate, decay)
        outs[2 + n][where] = value
        outs[8 + n][where] = new[0]
        outs[14 + 2 * n][where] = new[1]
        outs[15 + 2 * n][where] = new[2]


def run_update(flat, small, hidden, grad, params, moments):
    layers, _, rows, ch = params[0].shape
    ff = params[2].shape[3]
    per = flat.shape[1] // layers

    def whole(a):
        return pl.BlockSpec(a.shape, lambda l, n=a.ndim: (0,) * n)

    def layer(a):
        return pl.BlockSpec((1, *a.shape[1:]), lambda l, n=a.ndim: (l,) + (0,) * (n - 1))

    def spec(n, a):
        return layer(a) if n < 4 else whole(a)

    each = [spec(n, a) for n, a in enumerate(params)]
    token = pl.BlockSpec((hidden.shape[0] // layers, hidden.shape[1]), lambda l: (l, 0))
    twice = [e for e in each for _ in range(2)]
    shapes = [jax.ShapeDtypeStruct(a.shape, F32) for a in params]
    two = [e for e in shapes for _ in range(2)]
    token_shape = jax.ShapeDtypeStruct(hidden.shape, F32)
    return pl.pallas_call(
        functools.partial(update_kernel, (ch, ff)),
        grid=(layers,),
        out_shape=(token_shape, token_shape, *shapes, *shapes, *two),
        in_specs=[pl.BlockSpec((rows, per), lambda l: (0, l)), whole(small), token, token, *each, *twice],
        out_specs=(token, token, *each, *each, *twice),
        name="update",
    )(flat, small, hidden, grad, *params, *moments)


def per_device(
    inputs,
    cotangent,
    entry_weight,
    exit_weight,
    gate_up,
    down_weight,
    conv_kernel,
    norm_gain,
    entry_first,
    entry_second,
    exit_first,
    exit_second,
    gate_first,
    gate_second,
    down_first,
    down_second,
    kernel_first,
    kernel_second,
    gain_first,
    gain_second,
):
    layers, _, _, ch = entry_weight.shape
    ff = gate_up.shape[3]
    seqs = lax.axis_size("seq")
    weights = (entry_weight, jnp.swapaxes(exit_weight, 1, 2), gate_up, jnp.swapaxes(down_weight, 1, 2))
    hidden, grad, summed, small = run_step(inputs, cotangent, weights, jnp.swapaxes(conv_kernel, 0, 1), norm_gain, seqs)
    flip = lambda a: jnp.swapaxes(a, 1, 2)
    spin = lambda a: jnp.swapaxes(a, 0, 1)
    keep = lambda a: a
    turns = (keep, flip, keep, flip, spin, keep)
    params = (entry_weight, exit_weight, gate_up, down_weight, conv_kernel, norm_gain)
    moments = (
        entry_first,
        entry_second,
        exit_first,
        exit_second,
        gate_first,
        gate_second,
        down_first,
        down_second,
        kernel_first,
        kernel_second,
        gain_first,
        gain_second,
    )
    twice = [t for t in turns for _ in range(2)]
    done = run_update(
        summed,
        small,
        hidden,
        grad,
        [t(a) for t, a in zip(turns, params)],
        [t(a) for t, a in zip(twice, moments)],
    )
    return tuple(t(a) for t, a in zip((keep, keep, *turns, *turns, *twice), done))


def solution(mesh):
    tokens, rows, columns, replicated = (
        P("seq", "tp"),
        P(None, None, "seq", "tp"),
        P(None, "tp", "seq"),
        P(None, None, "tp"),
    )
    matrices = (rows, columns, rows, columns)
    moments = (rows, rows, columns, columns, rows, rows, columns, columns)
    return jax.shard_map(
        per_device,
        mesh=mesh,
        in_specs=(tokens, tokens, *matrices, replicated, replicated, *moments, *([replicated] * 4)),
        out_specs=(
            tokens,
            tokens,
            *matrices,
            replicated,
            replicated,
            *matrices,
            replicated,
            replicated,
            *moments,
            *([replicated] * 4),
        ),
        check_vma=False,
    )
```
